32 devices in a mesh: row: 4 (over y, x), col: 8 (over z, core).
Axes of the slice: x: 2, y: 2, z: 4, core: 2. Of those that a mesh axis runs over, the one named last changes fastest.
Arguments:
- noise_points: float32 [16384, 512], P('row'), may hold values from -30 to 30
- data_points: float32 [2048, 512], P('col'), may hold values from -30 to 30
- times: float32 [16384, 8], P(('row', 'col')), may hold values from 0 to 1
- time_shift: float32 [1024], replicated, may hold values from -6 to 6
- weight_in: bfloat16 [512, 1024], replicated, may hold values from -0.25 to 0.25
- weight_out: bfloat16 [1024, 512], replicated, may hold values from -0.1875 to 0.1875
Outputs:
- predicted: bfloat16 [131072, 512], P(('row', 'col'))
- grad_in: float32 [512, 1024], replicated
- grad_out: float32 [1024, 512], replicated
The draws below stay inside these ranges and needn't reach their ends.
All inputs are finite; a program needn't handle non-finite values.
Results may differ from the reference program's by a relative error of at most 0.0057.
Values sent between devices are 32-bit elements; how exact they have to be, the bound alone decides.
No kernel may reach another device: no remote copies, remote signals or barrier semaphores. Data moves between devices by JAX's collectives and lax.ppermute only.
A program may use at most 128 MiB of HBM per device.

```python
import math
import jax
import jax.numpy as jnp
from jax import lax

P_SIZE = 512
HID = 1024
NOISE_DEV = 4096
ITERS = 1
TSTEPS = 8
NN = 16384
ND = 2048
N_ROW = 4


def shared_points(key):
    keys = jax.random.split(jax.random.fold_in(key, 7), 2)
    data_base = jnp.clip(jax.random.normal(keys[0], (ND, P_SIZE), jnp.float32), -6.0, 6.0)
    noise_base = jnp.clip(jax.random.normal(keys[1], (NN, P_SIZE), jnp.float32), -6.0, 6.0)
    return (noise_base, data_base)


def draw_noise_points(key, part):
    return shared_points(key)[0]


def draw_data_points(key, part):
    return shared_points(key)[1]


def block_scale(rng, extent, pieces, low, top_value):
    factor_of = 1.0
    for axis_at, shards_of in pieces:
        steps = jax.random.uniform(jax.random.fold_in(jax.random.fold_in(rng, 6), axis_at), (shards_of,), jnp.float32, low / len(pieces), top_value / len(pieces))
        factor_of = factor_of * jnp.repeat(jnp.exp(steps), extent[axis_at] // shards_of).reshape((-1,) + (1,) * (len(extent) - 1 - axis_at))
    return factor_of


def centred(stream_key, shape, deviation, reach, dtype=jnp.bfloat16):
    array = deviation * jax.random.normal(stream_key, shape, jnp.float32)
    return jnp.clip(array, min=-reach, max=reach).astype(dtype)


def setup_inputs(seed: int = 0) -> dict:
    streams_of = jax.random.split(jax.random.key(seed), 7)
    noise_points = draw_noise_points(jax.random.fold_in(streams_of[6], 71), 0)
    data_points = draw_data_points(jax.random.fold_in(streams_of[6], 71), 0)
    times = jnp.clip(1.0 * jax.random.uniform(streams_of[2], (NN, TSTEPS), jnp.float32) ** block_scale(streams_of[2], (NN, TSTEPS), ((0, 32),), -0.2, 0.2), 0.0, 1.0)
    time_shift = centred(streams_of[3], (HID,), 1.0, 6.0, jnp.float32)
    weight_in = centred(streams_of[4], (P_SIZE, HID), P_SIZE ** -0.5, 0.25)
    weight_out = centred(streams_of[5], (HID, P_SIZE), HID ** -0.5, 0.1875)
    return dict(noise_points=noise_points, data_points=data_points, times=times, time_shift=time_shift, weight_in=weight_in, weight_out=weight_out)


ENTROPY = 0.05
HIGHEST_PREC = lax.Precision.HIGHEST

def cost_block(noise_block, data_all):
    noise_sq = lax.optimization_barrier(jnp.sum(noise_block * noise_block, axis=1))
    data_sq = lax.optimization_barrier(jnp.sum(data_all * data_all, axis=1))
    inner = jnp.dot(noise_block, data_all.T, precision=HIGHEST_PREC, preferred_element_type=jnp.float32)
    return (noise_sq[:, None] + data_sq[None, :] - 2.0 * inner) / P_SIZE

def reference(noise_points, data_points, times, time_shift, weight_in, weight_out):
    blocks = noise_points.reshape(N_ROW, NOISE_DEV, P_SIZE)
    potential_g = jnp.zeros((ND,), jnp.float32)
    for sweep in range(ITERS):

        def row_pass(block):
            scores = (potential_g[None, :] - cost_block(block, data_points)) / ENTROPY
            peak = lax.optimization_barrier(jnp.max(scores, axis=1))
            total = lax.optimization_barrier(jnp.sum(jnp.exp(scores - peak[:, None]), axis=1))
            return -ENTROPY * (peak + jnp.log(total) - math.log(float(ND)))
        potential_f = lax.map(row_pass, blocks)

        def col_step(carry, pair):
            block, f_part = pair
            scores = (f_part[:, None] - cost_block(block, data_points)) / ENTROPY
            new_peak = jnp.maximum(carry[0], lax.optimization_barrier(jnp.max(scores, axis=0)))
            total = carry[1] * jnp.exp(carry[0] - new_peak) + lax.optimization_barrier(jnp.sum(jnp.exp(scores - new_peak[None, :]), axis=0))
            return ((new_peak, total), None)
        start = (jnp.full((ND,), -jnp.inf, jnp.float32), jnp.zeros((ND,), jnp.float32))
        (peak_all, total_all), unused = lax.scan(col_step, start, (blocks, potential_f))
        potential_g = -ENTROPY * (peak_all + jnp.log(total_all) - math.log(float(NN)))

    def target_pass(block):
        scores = (potential_g[None, :] - cost_block(block, data_points)) / ENTROPY
        peak = lax.optimization_barrier(jnp.max(scores, axis=1))
        weights = jnp.exp(scores - peak[:, None])
        numer = jnp.dot(weights, data_points, precision=HIGHEST_PREC, preferred_element_type=jnp.float32)
        return numer / lax.optimization_barrier(jnp.sum(weights, axis=1))[:, None]
    target = lax.map(target_pass, blocks).reshape(NN, P_SIZE)
    tvals = times[:, :, None]
    mixed = ((1.0 - tvals) * noise_points[:, None, :] + tvals * target[:, None, :]).reshape(NN * TSTEPS, P_SIZE).astype(jnp.bfloat16)
    velocity = jnp.broadcast_to((target - noise_points)[:, None, :], (NN, TSTEPS, P_SIZE)).reshape(NN * TSTEPS, P_SIZE)
    pre = jnp.dot(mixed, weight_in, preferred_element_type=jnp.float32) + times.reshape(NN * TSTEPS, 1) * time_shift[None, :]
    hidden = jax.nn.silu(pre).astype(jnp.bfloat16)
    output = jnp.dot(hidden, weight_out, preferred_element_type=jnp.float32)
    predicted = output.astype(jnp.bfloat16)
    scale = 1.0 / math.sqrt(float(NN * TSTEPS))
    delta = ((output - velocity) * scale).astype(jnp.bfloat16)
    grad_out = lax.dot_general(hidden, delta, (((0,), (0,)), ((), ())), preferred_element_type=jnp.float32)
    back = lax.dot_general(delta, weight_out, (((1,), (1,)), ((), ())), preferred_element_type=jnp.float32)
    sig = jax.nn.sigmoid(pre)
    delta_pre = (back * sig * (1.0 + pre * (1.0 - sig))).astype(jnp.bfloat16)
    grad_in = lax.dot_general(mixed, delta_pre, (((0,), (0,)), ((), ())), preferred_element_type=jnp.float32)
    return (predicted, grad_in, grad_out)
```

```python
import math

import jax
import jax.numpy as jnp
from jax import lax
from jax.sharding import PartitionSpec as P

ENTROPY = 0.05


def swap(value, axis, mask):
    size = lax.axis_size(axis)
    return lax.ppermute(value, axis, [(i, i ^ mask) for i in range(size)])


def xor_rows(value, axis, mask):
    if mask == 0:
        return value
    pieces = [
        lax.index_in_dim(value, i ^ mask, axis, True) for i in range(value.shape[axis])
    ]
    return jnp.concatenate(pieces, axis=axis)


def log_sum(values):
    peak = values[0]
    for value in values[1:]:
        peak = jnp.maximum(peak, value)
    total = sum(jnp.exp(value - peak) for value in values)
    return peak + jnp.log(total)


def gather_points(data_points):
    count_row = lax.axis_size("row")
    count_z = lax.axis_size("col") // 2
    part = data_points.shape[0] // count_row
    width = data_points.shape[1]
    quarter = lax.dynamic_slice_in_dim(data_points, lax.axis_index("row") * part, part, 0)
    far = jnp.stack([swap(quarter, "col", 2 * m) for m in range(1, count_z)])
    quarters = [far] + [swap(far, "row", k) for k in range(1, count_row)]
    far_all = jnp.stack(quarters, axis=1)
    index = lax.axis_index("row")
    own = data_points.reshape(count_row, part, width)
    own = jnp.stack([lax.dynamic_index_in_dim(own, index ^ k, 0, False) for k in range(count_row)])
    mine = jnp.concatenate([own[None], far_all], axis=0)
    return jnp.stack([mine, swap(mine, "col", 1)])


def column_log_sum(local):
    count_core, count_z, count_row, part = local.shape
    parts = [local]
    for k in range(1, count_row):
        parts.append(xor_rows(swap(local, "row", k), 2, k))
    local = log_sum(parts)
    local = log_sum([local, xor_rows(swap(local, "col", 1), 0, 1)])
    parts = [local]
    for m in range(1, count_z):
        parts.append(xor_rows(swap(local, "col", 2 * m), 1, m))
    return log_sum(parts)


def halve(value, axis, bit):
    half = value.shape[0] // 2
    side = (lax.axis_index(axis) >> bit) & 1
    send = lax.dynamic_slice_in_dim(value, (1 - side) * half, half, 0)
    keep = lax.dynamic_slice_in_dim(value, side * half, half, 0)
    return keep + swap(send, axis, 1 << bit)


def double(value, axis, bit):
    half = value.shape[0]
    side = (lax.axis_index(axis) >> bit) & 1
    other = swap(value, axis, 1 << bit)
    out = jnp.zeros((2 * half,) + value.shape[1:], value.dtype)
    out = lax.dynamic_update_slice_in_dim(out, value, side * half, 0)
    return lax.dynamic_update_slice_in_dim(out, other, (1 - side) * half, 0)


def sum_everywhere(value):
    row_bits = list(range(lax.axis_size("row").bit_length() - 1))
    count_z = lax.axis_size("col") // 2
    z_at = lax.axis_index("col") >> 1
    value = halve(value, "col", 0)
    half = value.shape[0] // 2
    colours = [value[:half], value[half:]]
    orders = [row_bits, row_bits[::-1]]
    for step in range(len(row_bits)):
        colours = [halve(c, "row", o[step]) for c, o in zip(colours, orders)]
    cut = colours[0].shape[0]
    value = jnp.concatenate(colours, axis=0)
    piece = value.shape[0] // count_z
    take = lambda m: lax.dynamic_slice_in_dim(value, (z_at ^ m) * piece, piece, 0)
    total = take(0)
    got = [swap(take(m), "col", 2 * m) for m in range(1, count_z)]
    for g in got:
        total = total + g
    out = jnp.zeros_like(value)
    out = lax.dynamic_update_slice_in_dim(out, total, z_at * piece, 0)
    for m in range(1, count_z):
        other = swap(total, "col", 2 * m)
        out = lax.dynamic_update_slice_in_dim(out, other, (z_at ^ m) * piece, 0)
    colours = [out[:cut], out[cut:]]
    for step in reversed(range(len(row_bits))):
        colours = [double(c, "row", o[step]) for c, o in zip(colours, orders)]
    return double(jnp.concatenate(colours, axis=0), "col", 0)


def split_halves(value):
    high = value.astype(jnp.bfloat16)
    low = (value - high.astype(jnp.float32)).astype(jnp.bfloat16)
    return high, low


def on_device(noise_points, data_points, times, time_shift, weight_in, weight_out):
    count_row = lax.axis_size("row")
    count_col = lax.axis_size("col")
    rows_here = noise_points.shape[0]
    total_noise = rows_here * count_row
    total_data = data_points.shape[0] * count_col
    width = noise_points.shape[1]
    share = rows_here // count_col
    anchor = lax.dynamic_slice_in_dim(noise_points, lax.axis_index("col") * share, share, 0)
    relative = gather_points(data_points)
    grid = relative.shape[:-1]
    points = relative.reshape(total_data, width)
    anchor_sq = jnp.sum(anchor * anchor, axis=1)
    points_sq = jnp.sum(points * points, axis=1)
    a_high, a_low = split_halves(anchor)
    p_high, p_low = split_halves(points)
    contract_last = (((1,), (1,)), ((), ()))
    times_of = lambda a, b: lax.dot_general(
        a, b, contract_last, preferred_element_type=jnp.float32
    )
    inner = times_of(a_high, p_high) + (times_of(a_high, p_low) + times_of(a_low, p_high))
    scores = -(anchor_sq[:, None] + points_sq[None, :] - 2.0 * inner) / (width * ENTROPY)
    peak = jnp.max(scores, axis=1)
    total = jnp.sum(jnp.exp(scores - peak[:, None]), axis=1)
    f_scaled = math.log(float(total_data)) - peak - jnp.log(total)
    by_column = scores + f_scaled[:, None]
    peak = jnp.max(by_column, axis=0)
    total = jnp.sum(jnp.exp(by_column - peak[None, :]), axis=0)
    local = (peak + jnp.log(total)).reshape(grid)
    g_scaled = math.log(float(total_noise)) - column_log_sum(local).reshape(total_data)
    final = scores + g_scaled[None, :]
    weights = jnp.exp(final - jnp.max(final, axis=1)[:, None]).astype(jnp.bfloat16)
    numer = jnp.dot(weights, p_high, preferred_element_type=jnp.float32) + jnp.dot(
        weights, p_low, preferred_element_type=jnp.float32
    )
    target = numer / jnp.sum(weights.astype(jnp.float32), axis=1)[:, None]
    steps_each = times.shape[1]
    tvals = times[:, :, None]
    mixed = (
        ((1.0 - tvals) * anchor[:, None, :] + tvals * target[:, None, :])
        .reshape(share * steps_each, width)
        .astype(jnp.bfloat16)
    )
    velocity = jnp.broadcast_to((target - anchor)[:, None, :], (share, steps_each, width)).reshape(
        share * steps_each, width
    )
    hid_width = weight_in.shape[1]
    pre = (
        jnp.dot(mixed, weight_in, preferred_element_type=jnp.float32)
        + times.reshape(share * steps_each, 1) * time_shift[None, :]
    )
    hidden = jax.nn.silu(pre).astype(jnp.bfloat16)
    output = jnp.dot(hidden, weight_out, preferred_element_type=jnp.float32)
    predicted = output.astype(jnp.bfloat16)
    scale = 1.0 / math.sqrt(float(total_noise * steps_each))
    delta = ((output - velocity) * scale).astype(jnp.bfloat16)
    back = lax.dot_general(
        delta, weight_out, (((1,), (1,)), ((), ())), preferred_element_type=jnp.float32
    )
    sig = jax.nn.sigmoid(pre)
    delta_pre = (back * sig * (1.0 + pre * (1.0 - sig))).astype(jnp.bfloat16)
    contract = (((0,), (0,)), ((), ()))
    first = lax.dot_general(mixed, delta_pre, contract, preferred_element_type=jnp.float32)
    second = lax.dot_general(hidden, delta, contract, preferred_element_type=jnp.float32)
    half = hid_width // 2
    stacked = jnp.concatenate([first[:, :half], first[:, half:], second], axis=0)
    summed = sum_everywhere(stacked)
    grad_in = jnp.concatenate([summed[:width], summed[width : 2 * width]], axis=1)
    return (predicted, grad_in, summed[2 * width :])


def solution(mesh):
    in_specs = (P("row", None), P("col", None), P(("row", "col"), None), P(), P(), P())
    out_specs = (P(("row", "col"), None), P(), P())
    return jax.shard_map(
        on_device, mesh=mesh, in_specs=in_specs, out_specs=out_specs, check_vma=False
    )
```

```python
import functools
import math

import jax
import jax.numpy as jnp
from jax import lax
from jax.experimental import pallas as pl
from jax.experimental.pallas import tpu as pltpu
from jax.sharding import PartitionSpec as P

ENTROPY = 0.05


def swap(value, axis, mask):
    size = lax.axis_size(axis)
    return lax.ppermute(value, axis, [(i, i ^ mask) for i in range(size)])


def xor_rows(value, axis, mask):
    if mask == 0:
        return value
    pieces = [
        lax.index_in_dim(value, i ^ mask, axis, True) for i in range(value.shape[axis])
    ]
    return jnp.concatenate(pieces, axis=axis)


def log_sum(values):
    peak = values[0]
    for value in values[1:]:
        peak = jnp.maximum(peak, value)
    total = sum(jnp.exp(value - peak) for value in values)
    return peak + jnp.log(total)


def gather_points(data_points):
    count_row = lax.axis_size("row")
    count_z = lax.axis_size("col") // 2
    part = data_points.shape[0] // count_row
    width = data_points.shape[1]
    quarter = lax.dynamic_slice_in_dim(data_points, lax.axis_index("row") * part, part, 0)
    far = jnp.stack([swap(quarter, "col", 2 * m) for m in range(1, count_z)])
    quarters = [far] + [swap(far, "row", k) for k in range(1, count_row)]
    far_all = jnp.stack(quarters, axis=1)
    index = lax.axis_index("row")
    own = data_points.reshape(count_row, part, width)
    own = jnp.stack([lax.dynamic_index_in_dim(own, index ^ k, 0, False) for k in range(count_row)])
    mine = jnp.concatenate([own[None], far_all], axis=0)
    return jnp.stack([mine, swap(mine, "col", 1)])


def column_log_sum(local):
    count_core, count_z, count_row, part = local.shape
    parts = [local]
    for k in range(1, count_row):
        parts.append(xor_rows(swap(local, "row", k), 2, k))
    local = log_sum(parts)
    local = log_sum([local, xor_rows(swap(local, "col", 1), 0, 1)])
    parts = [local]
    for m in range(1, count_z):
        parts.append(xor_rows(swap(local, "col", 2 * m), 1, m))
    return log_sum(parts)


def split_halves(value):
    high = value.astype(jnp.bfloat16)
    low = (value - high.astype(jnp.float32)).astype(jnp.bfloat16)
    return high, low


def colour_ids():
    count_row = lax.axis_size("row")
    count_z = lax.axis_size("col") // 2
    row, col = lax.axis_index("row"), lax.axis_index("col")
    bits = list(range(count_row.bit_length() - 1))
    orders = [bits, bits[::-1]]
    ids = []
    for order in orders:
        ident = col & 1
        for bit in order:
            ident = ident * 2 + ((row >> bit) & 1)
        ids.append(ident * count_z + (col >> 1))
    return orders, jnp.stack(ids).astype(jnp.int32)


def store_blocks(devices, ids_ref, total_ref, keep_ref, send_ref):
    unit = total_ref.shape[0] // devices
    lanes = total_ref.shape[1] // 2
    for colour in range(2):
        for pos in range(devices):
            source = pl.multiple_of((ids_ref[colour] ^ pos) * unit, unit)
            block = total_ref[pl.ds(source, unit), colour * lanes : (colour + 1) * lanes]
            out_ref = keep_ref if pos < devices // 2 else send_ref
            at = (pos % (devices // 2)) * unit
            out_ref[colour, at : at + unit, :] = block


def time_column(times_ref, k):
    times = times_ref[...]
    lane = lax.broadcasted_iota(jnp.int32, times.shape, 1)
    return jnp.sum(jnp.where(lane == k, times, 0.0), axis=1, keepdims=True)


CONTRACT_ROWS = (((0,), (0,)), ((), ()))
CONTRACT_LANES = (((1,), (1,)), ((), ()))


def forward_kernel(
    devices, pair, scale, ids_ref, anchor_ref, target_ref, times_ref, shift_ref, win_ref, wout_ref,
    pred_ref, slope_ref, delta_ref, keep_ref, send_ref,
    base, move, velocity, hidden, spread, total,
):
    tile, step = pl.program_id(0), pl.program_id(1)
    points = anchor_ref.shape[0]
    steps_each = times_ref.shape[1]

    @pl.when((tile == 0) & (step == 0))
    def _():
        total[...] = jnp.zeros_like(total)

    @pl.when(step == 0)
    def _():
        anchor = anchor_ref[...]
        diff = target_ref[...] - anchor
        velocity[...] = diff
        base[...] = jnp.dot(
            anchor.astype(jnp.bfloat16), win_ref[...], preferred_element_type=jnp.float32
        )
        move[...] = (
            jnp.dot(diff.astype(jnp.bfloat16), win_ref[...], preferred_element_type=jnp.float32)
            + shift_ref[...]
        )

    for j in range(pair):
        rows = slice(j * points, (j + 1) * points)
        t = time_column(times_ref, step * pair + j)
        pre = base[...] + t * move[...]
        sig = 0.5 * jnp.tanh(0.5 * pre) + 0.5
        act = pre * sig
        hidden[rows, :] = act.astype(jnp.bfloat16)
        slope_ref[rows, :] = (sig + act * (1.0 - sig)).astype(jnp.bfloat16)
    out = jnp.dot(hidden[...], wout_ref[...], preferred_element_type=jnp.float32)
    for j in range(pair):
        rows = slice(j * points, (j + 1) * points)
        part = out[j * points : (j + 1) * points]
        delta_ref[rows, :] = ((part - velocity[...]) * scale).astype(jnp.bfloat16)
        for c in range(spread.shape[0]):
            spread[c, pl.ds(step * pair + j, points, stride=steps_each), :] = part[
                :, c * 128 : (c + 1) * 128
            ]
    total[...] += lax.dot_general(
        hidden[...], delta_ref[...], CONTRACT_ROWS, preferred_element_type=jnp.float32
    )

    @pl.when(step == pl.num_programs(1) - 1)
    def _():
        for c in range(spread.shape[0]):
            pred_ref[:, c * 128 : (c + 1) * 128] = spread[c].astype(jnp.bfloat16)

    @pl.when((step == pl.num_programs(1) - 1) & (tile == pl.num_programs(0) - 1))
    def _():
        store_blocks(devices, ids_ref, total, keep_ref, send_ref)


def backward_kernel(
    devices, pair, ids_ref, anchor_ref, target_ref, times_ref, wout_ref, slope_ref, delta_ref,
    keep_ref, send_ref, plain, timed, total,
):
    tile, step = pl.program_id(0), pl.program_id(1)
    points, width = anchor_ref.shape
    half = plain.shape[1] // 2

    @pl.when((tile == 0) & (step == 0))
    def _():
        total[...] = jnp.zeros_like(total)

    @pl.when(step == 0)
    def _():
        plain[...] = jnp.zeros_like(plain)
        timed[...] = jnp.zeros_like(timed)

    back = lax.dot_general(
        delta_ref[...], wout_ref[...], CONTRACT_LANES, preferred_element_type=jnp.float32
    )
    plain_sum, timed_sum = plain[...], timed[...]
    for j in range(pair):
        rows = slice(j * points, (j + 1) * points)
        t = time_column(times_ref, step * pair + j)
        grad = back[rows] * slope_ref[rows, :].astype(jnp.float32)
        plain_sum = plain_sum + grad
        timed_sum = timed_sum + t * grad
    plain[...] = plain_sum
    timed[...] = timed_sum

    @pl.when(step == pl.num_programs(1) - 1)
    def _():
        anchor = anchor_ref[...]
        diff = (target_ref[...] - anchor).astype(jnp.bfloat16)
        anchor = anchor.astype(jnp.bfloat16)
        for h in range(2):
            lanes = slice(h * half, (h + 1) * half)
            total[h * width : (h + 1) * width, :] += lax.dot_general(
                anchor, plain[:, lanes].astype(jnp.bfloat16), CONTRACT_ROWS,
                preferred_element_type=jnp.float32,
            ) + lax.dot_general(
                diff, timed[:, lanes].astype(jnp.bfloat16), CONTRACT_ROWS,
                preferred_element_type=jnp.float32,
            )

    @pl.when((step == pl.num_programs(1) - 1) & (tile == pl.num_programs(0) - 1))
    def _():
        store_blocks(devices, ids_ref, total, keep_ref, send_ref)


def place_kernel(devices, wide, ids_ref, own_ref, other_ref, out_ref):
    unit = own_ref.shape[1] * 2 // devices
    lanes = own_ref.shape[2]
    for colour in range(2):
        for block in range(devices):
            pos = ids_ref[colour] ^ block
            far = pos >= devices // 2
            at = pl.multiple_of((pos & (devices // 2 - 1)) * unit, unit)
            value = jnp.where(
                far, other_ref[colour, pl.ds(at, unit), :], own_ref[colour, pl.ds(at, unit), :]
            )
            row = block * unit
            if wide:
                height = out_ref.shape[0]
                left = (row // height) * 2 * lanes + colour * lanes
                row = row % height
            else:
                left = colour * lanes
            out_ref[row : row + unit, left : left + lanes] = value


def vmem_specs(count):
    return [pl.BlockSpec(memory_space=pltpu.VMEM)] * count


def place(ids, own, other, shape):
    devices = lax.axis_size("row") * lax.axis_size("col")
    wide = shape[1] > 2 * own.shape[2]
    return pl.pallas_call(
        functools.partial(place_kernel, devices, wide),
        out_shape=jax.ShapeDtypeStruct(shape, jnp.float32),
        grid_spec=pltpu.PrefetchScalarGridSpec(
            num_scalar_prefetch=1, grid=(1,),
            in_specs=[
                pl.BlockSpec(own.shape, lambda i, ids: (0, 0, 0)),
                pl.BlockSpec(own.shape, lambda i, ids: (0, 0, 0)),
            ],
            out_specs=pl.BlockSpec(shape, lambda i, ids: (0, 0)),
        ),
        compiler_params=pltpu.CompilerParams(vmem_limit_bytes=24 << 20),
        cost_estimate=pl.CostEstimate(flops=0, transcendentals=0, bytes_accessed=4 << 20),
        name="place",
    )(ids, own, other)


def sum_over_devices(orders, keep, send):
    count_z = lax.axis_size("col") // 2
    got = swap(send, "col", 1)
    colours = [(keep[c], got[c]) for c in range(2)]
    for step in range(len(orders[0])):
        later = []
        for (mine, other), order in zip(colours, orders):
            half = mine.shape[0] // 2
            out = mine[half:] + other[half:]
            out = swap(out, "row", 1 << order[step])
            later.append((mine[:half] + other[:half], out))
        colours = later
    unit = colours[0][0].shape[0] // count_z
    part = lambda m: jnp.stack(
        [a[m * unit : (m + 1) * unit] + b[m * unit : (m + 1) * unit] for a, b in colours]
    )
    got = [swap(part(m), "col", 2 * m) for m in range(1, count_z)]
    total = part(0)
    for value in got:
        total = total + value
    parts = [total] + [swap(total, "col", 2 * m) for m in range(1, count_z)]
    colours = [jnp.concatenate([p[c] for p in parts], axis=0) for c in range(2)]
    for step in reversed(range(len(orders[0]))):
        colours = [
            jnp.concatenate([value, swap(value, "row", 1 << order[step])], axis=0)
            for value, order in zip(colours, orders)
        ]
    own = jnp.stack(colours)
    return own, swap(own, "col", 1)


def train(anchor, target, times, time_shift, weight_in, weight_out, total_noise):
    share, width = anchor.shape
    steps_each = times.shape[1]
    hid_width = weight_in.shape[1]
    devices = lax.axis_size("row") * lax.axis_size("col")
    orders, ids = colour_ids()
    scale = 1.0 / math.sqrt(float(total_noise * steps_each))
    points = min(share, 256)
    tiles = share // points
    pair = 2
    steps = steps_each // pair
    rows = pair * points
    gradient = jax.ShapeDtypeStruct((2, hid_width // 2, width // 2), jnp.float32)
    whole = lambda shape: pl.BlockSpec(shape, lambda i, j, ids: (0,) * len(shape))
    by_tile = lambda shape: pl.BlockSpec(shape, lambda i, j, ids: (i, 0))
    by_step = lambda shape: pl.BlockSpec(shape, lambda i, j, ids: (i * steps + j, 0))
    params = pltpu.CompilerParams(vmem_limit_bytes=56 << 20)
    f32, bf16 = jnp.float32, jnp.bfloat16
    macs = share * steps_each * width * hid_width
    predicted, slope, delta, keep, send = pl.pallas_call(
        functools.partial(forward_kernel, devices, pair, scale),
        out_shape=(
            jax.ShapeDtypeStruct((share * steps_each, width), bf16),
            jax.ShapeDtypeStruct((share * steps_each, hid_width), bf16),
            jax.ShapeDtypeStruct((share * steps_each, width), bf16),
            gradient, gradient,
        ),
        grid_spec=pltpu.PrefetchScalarGridSpec(
            num_scalar_prefetch=1, grid=(tiles, steps),
            in_specs=[
                by_tile((points, width)), by_tile((points, width)),
                by_tile((points, steps_each)), whole((1, hid_width)),
                whole((width, hid_width)), whole((hid_width, width)),
            ],
            out_specs=[
                by_tile((points * steps_each, width)), by_step((rows, hid_width)),
                by_step((rows, width)), whole(gradient.shape), whole(gradient.shape),
            ],
            scratch_shapes=[
                pltpu.VMEM((points, hid_width), f32), pltpu.VMEM((points, hid_width), f32),
                pltpu.VMEM((points, width), f32), pltpu.VMEM((rows, hid_width), bf16),
                pltpu.VMEM((width // 128, points * steps_each, 128), f32),
                pltpu.VMEM((hid_width, width), f32),
            ],
        ),
        compiler_params=params,
        cost_estimate=pl.CostEstimate(
            flops=5 * macs, transcendentals=share * steps_each * hid_width,
            bytes_accessed=24 << 20,
        ),
        name="forward",
    )(ids, anchor, target, times, time_shift[None, :], weight_in, weight_out)
    keep_in, send_in = pl.pallas_call(
        functools.partial(backward_kernel, devices, pair),
        out_shape=(gradient, gradient),
        grid_spec=pltpu.PrefetchScalarGridSpec(
            num_scalar_prefetch=1, grid=(tiles, steps),
            in_specs=[
                by_tile((points, width)), by_tile((points, width)),
                by_tile((points, steps_each)), whole((hid_width, width)),
                by_step((rows, hid_width)), by_step((rows, width)),
            ],
            out_specs=[whole(gradient.shape), whole(gradient.shape)],
            scratch_shapes=[
                pltpu.VMEM((points, hid_width), f32), pltpu.VMEM((points, hid_width), f32),
                pltpu.VMEM((2 * width, hid_width // 2), f32),
            ],
        ),
        compiler_params=params,
        cost_estimate=pl.CostEstimate(
            flops=3 * macs, transcendentals=0, bytes_accessed=18 << 20
        ),
        name="backward",
    )(ids, anchor, target, times, weight_out, slope, delta)
    out_own, out_other = sum_over_devices(orders, keep, send)
    in_own, in_other = sum_over_devices(orders, keep_in, send_in)
    grad_out = place(ids, out_own, out_other, (hid_width, width))
    grad_in = place(ids, in_own, in_other, (width, hid_width))
    return predicted, grad_in, grad_out


def on_device(noise_points, data_points, times, time_shift, weight_in, weight_out):
    count_row = lax.axis_size("row")
    count_col = lax.axis_size("col")
    rows_here = noise_points.shape[0]
    total_noise = rows_here * count_row
    total_data = data_points.shape[0] * count_col
    width = noise_points.shape[1]
    share = rows_here // count_col
    anchor = lax.dynamic_slice_in_dim(noise_points, lax.axis_index("col") * share, share, 0)
    relative = gather_points(data_points)
    grid = relative.shape[:-1]
    points = relative.reshape(total_data, width)
    anchor_sq = jnp.sum(anchor * anchor, axis=1)
    points_sq = jnp.sum(points * points, axis=1)
    a_high, a_low = split_halves(anchor)
    p_high, p_low = split_halves(points)
    contract_last = (((1,), (1,)), ((), ()))
    times_of = lambda a, b: lax.dot_general(
        a, b, contract_last, preferred_element_type=jnp.float32
    )
    inner = times_of(a_high, p_high) + (times_of(a_high, p_low) + times_of(a_low, p_high))
    scores = -(anchor_sq[:, None] + points_sq[None, :] - 2.0 * inner) / (width * ENTROPY)
    peak = jnp.max(scores, axis=1)
    total = jnp.sum(jnp.exp(scores - peak[:, None]), axis=1)
    f_scaled = math.log(float(total_data)) - peak - jnp.log(total)
    by_column = scores + f_scaled[:, None]
    peak = jnp.max(by_column, axis=0)
    total = jnp.sum(jnp.exp(by_column - peak[None, :]), axis=0)
    local = (peak + jnp.log(total)).reshape(grid)
    g_scaled = math.log(float(total_noise)) - column_log_sum(local).reshape(total_data)
    final = scores + g_scaled[None, :]
    weights = jnp.exp(final - jnp.max(final, axis=1)[:, None]).astype(jnp.bfloat16)
    numer = jnp.dot(weights, p_high, preferred_element_type=jnp.float32) + jnp.dot(
        weights, p_low, preferred_element_type=jnp.float32
    )
    target = numer / jnp.sum(weights.astype(jnp.float32), axis=1)[:, None]
    return train(anchor, target, times, time_shift, weight_in, weight_out, total_noise)


def solution(mesh):
    in_specs = (P("row", None), P("col", None), P(("row", "col"), None), P(), P(), P())
    out_specs = (P(("row", "col"), None), P(), P())
    return jax.shard_map(
        on_device, mesh=mesh, in_specs=in_specs, out_specs=out_specs, check_vma=False
    )
```

```python
import functools
import math

import jax
import jax.numpy as jnp
from jax import lax
from jax.experimental import pallas as pl
from jax.experimental.pallas import tpu as pltpu
from jax.sharding import PartitionSpec as P

ENTROPY = 0.05
CONTRACT_ROWS = (((0,), (0,)), ((), ()))
CONTRACT_LANES = (((1,), (1,)), ((), ()))
F32, BF16 = jnp.float32, jnp.bfloat16
STRIP = 8


def swap(value, axis, mask):
    size = lax.axis_size(axis)
    return lax.ppermute(value, axis, [(i, i ^ mask) for i in range(size)])


def xor_rows(value, axis, mask):
    if mask == 0:
        return value
    pieces = [
        lax.index_in_dim(value, i ^ mask, axis, True) for i in range(value.shape[axis])
    ]
    return jnp.concatenate(pieces, axis=axis)


def log_sum(values):
    peak = values[0]
    for value in values[1:]:
        peak = jnp.maximum(peak, value)
    total = sum(jnp.exp(value - peak) for value in values)
    return peak + jnp.log(total)


def gather_points(data_points):
    count_row = lax.axis_size("row")
    count_z = lax.axis_size("col") // 2
    part = data_points.shape[0] // count_row
    row = lax.axis_index("row")
    pieces = [
        lax.dynamic_slice_in_dim(data_points, (row ^ k) * part, part, 0) for k in range(count_row)
    ]
    own = jnp.concatenate(pieces, axis=0)
    far = [swap(pieces[0], "col", 2 * m) for m in range(1, count_z)]
    blocks = [own, swap(own, "col", 1)]
    for value in far:
        mine = jnp.concatenate(
            [value] + [swap(value, "row", k) for k in range(1, count_row)], axis=0
        )
        blocks += [mine, swap(mine, "col", 1)]
    return blocks


def column_log_sum(local):
    count_z, count_core, count_row, part = local.shape
    parts = [local]
    for k in range(1, count_row):
        parts.append(xor_rows(swap(local, "row", k), 2, k))
    local = log_sum(parts)
    local = log_sum([local, xor_rows(swap(local, "col", 1), 1, 1)])
    parts = [local]
    for m in range(1, count_z):
        parts.append(xor_rows(swap(local, "col", 2 * m), 0, m))
    return log_sum(parts)


def split_halves(value):
    high = value.astype(BF16)
    low = (value - high.astype(F32)).astype(BF16)
    return high, low


def score_kernel(count, log_data, norm, *refs):
    anchor_ref, block_refs = refs[0], refs[1 : 1 + count]
    scores_ref, high_ref, low_ref, local_ref, shift = refs[1 + count :]
    points = anchor_ref.shape[0]
    anchor = anchor_ref[...]
    anchor_sq = jnp.sum(anchor * anchor, axis=1, keepdims=True)
    a_high, a_low = split_halves(anchor)
    dots = lambda a, b: lax.dot_general(a, b, CONTRACT_LANES, preferred_element_type=F32)
    for index, ref in enumerate(block_refs):
        size = ref.shape[0]
        rows = slice(index * size, (index + 1) * size)
        block = ref[...]
        high, low = split_halves(block)
        high_ref[rows, :] = high
        low_ref[rows, :] = low
        ones = jnp.ones((8, block.shape[1]), F32)
        block_sq = lax.dot_general(
            ones, block * block, CONTRACT_LANES, precision=lax.Precision.HIGHEST,
            preferred_element_type=F32,
        )[:1]
        inner = dots(a_high, high) + dots(a_high, low) + dots(a_low, high)
        scores_ref[:, rows] = (2.0 * inner - anchor_sq - block_sq) * norm
    width = scores_ref.shape[1]

    def by_row(step, peak):
        at = pl.multiple_of(step * STRIP, STRIP)
        s = scores_ref[pl.ds(at, STRIP), :]
        top = jnp.max(s, axis=1, keepdims=True)
        total = jnp.sum(jnp.exp(s - top), axis=1, keepdims=True)
        f = log_data - top - jnp.log(total)
        shift[pl.ds(at, STRIP), :] = jnp.broadcast_to(f, (STRIP, shift.shape[1]))
        return jnp.maximum(peak, s + f)

    peak = lax.fori_loop(
        0, points // STRIP, by_row, jnp.full((STRIP, width), -jnp.inf, F32), unroll=4
    )
    peak = jnp.max(peak, axis=0, keepdims=True)
    top = jnp.broadcast_to(peak, (STRIP, width))

    def by_column(step, total):
        at = pl.multiple_of(step * STRIP, STRIP)
        f = shift[pl.ds(at, STRIP), :][:, :1]
        return total + jnp.exp((scores_ref[pl.ds(at, STRIP), :] + f) - top)

    total = lax.fori_loop(
        0, points // STRIP, by_column, jnp.zeros((STRIP, width), F32), unroll=4
    )
    local_ref[...] = peak + jnp.log(jnp.sum(total, axis=0, keepdims=True))


def score(anchor, blocks):
    points, width = anchor.shape
    count = len(blocks)
    total = count * blocks[0].shape[0]
    whole = pl.BlockSpec(memory_space=pltpu.VMEM)
    return pl.pallas_call(
        functools.partial(score_kernel, count, math.log(float(total)), 1.0 / (width * ENTROPY)),
        out_shape=(
            jax.ShapeDtypeStruct((points, total), F32),
            jax.ShapeDtypeStruct((total, width), BF16),
            jax.ShapeDtypeStruct((total, width), BF16),
            jax.ShapeDtypeStruct((1, total), F32),
        ),
        in_specs=[whole] * (1 + count),
        out_specs=[whole] * 4,
        scratch_shapes=[pltpu.VMEM((points, 128), F32)],
        compiler_params=pltpu.CompilerParams(vmem_limit_bytes=40 << 20),
        cost_estimate=pl.CostEstimate(
            flops=6 * points * total * width, transcendentals=2 * points * total,
            bytes_accessed=14 << 20,
        ),
        name="score",
    )(anchor, *blocks)


def target_kernel(scores_ref, g_ref, high_ref, low_ref, target_ref, weights, inverse):
    points = scores_ref.shape[0]
    strip = 2 * STRIP
    g = g_ref[...]

    def by_row(step, unused):
        at = pl.multiple_of(step * strip, strip)
        s = scores_ref[pl.ds(at, strip), :] + g
        w = jnp.exp(s - jnp.max(s, axis=1, keepdims=True)).astype(BF16)
        weights[pl.ds(at, strip), :] = w
        total = jnp.sum(w.astype(F32), axis=1, keepdims=True)
        inverse[pl.ds(at, strip), :] = jnp.broadcast_to(total, (strip, inverse.shape[1]))
        return unused

    lax.fori_loop(0, points // strip, by_row, 0, unroll=2)
    w = weights[...]
    numer = jnp.dot(w, high_ref[...], preferred_element_type=F32)
    numer = numer + jnp.dot(w, low_ref[...], preferred_element_type=F32)
    target_ref[...] = numer / inverse[:, :1]


def target_points(scores, g, high, low):
    points, total = scores.shape
    width = high.shape[1]
    rows = min(points, 256)
    return pl.pallas_call(
        target_kernel,
        out_shape=jax.ShapeDtypeStruct((points, width), F32),
        grid=(points // rows,),
        in_specs=[
            pl.BlockSpec((rows, total), lambda i: (i, 0)),
            pl.BlockSpec((1, total), lambda i: (0, 0)),
            pl.BlockSpec((total, width), lambda i: (0, 0)),
            pl.BlockSpec((total, width), lambda i: (0, 0)),
        ],
        out_specs=pl.BlockSpec((rows, width), lambda i: (i, 0)),
        scratch_shapes=[pltpu.VMEM((rows, total), BF16), pltpu.VMEM((rows, 128), F32)],
        compiler_params=pltpu.CompilerParams(vmem_limit_bytes=40 << 20),
        cost_estimate=pl.CostEstimate(
            flops=4 * points * total * width, transcendentals=points * total,
            bytes_accessed=9 << 20,
        ),
        name="target",
    )(scores, g, high, low)


def colour_ids():
    count_row = lax.axis_size("row")
    count_z = lax.axis_size("col") // 2
    row, col = lax.axis_index("row"), lax.axis_index("col")
    bits = list(range(count_row.bit_length() - 1))
    orders = [bits, bits[::-1]]
    ids = []
    for order in orders:
        ident = col & 1
        for bit in order:
            ident = ident * 2 + ((row >> bit) & 1)
        ids.append(ident * count_z + (col >> 1))
    return orders, jnp.stack(ids).astype(jnp.int32)


def store_blocks(devices, ids_ref, total_ref, keep_ref, send_ref):
    unit = total_ref.shape[0] // devices
    lanes = total_ref.shape[1] // 2
    for colour in range(2):
        for pos in range(devices):
            source = pl.multiple_of((ids_ref[colour] ^ pos) * unit, unit)
            block = total_ref[pl.ds(source, unit), colour * lanes : (colour + 1) * lanes]
            out_ref = keep_ref if pos < devices // 2 else send_ref
            at = (pos % (devices // 2)) * unit
            out_ref[colour, at : at + unit, :] = block


def time_column(times_ref, k):
    times = times_ref[...]
    lane = lax.broadcasted_iota(jnp.int32, times.shape, 1)
    return jnp.sum(jnp.where(lane == k, times, 0.0), axis=1, keepdims=True)


def train_kernel(
    devices, pair, scale, ids_ref, anchor_ref, target_ref, times_ref, shift_ref, win_ref, wout_ref,
    pred_ref, keep_out, send_out, keep_in, send_in,
    base, move, velocity, hidden, slope, delta, back, plain, timed, spread, total_out, total_in,
):
    tile, step = pl.program_id(0), pl.program_id(1)
    points, width = anchor_ref.shape
    steps_each = times_ref.shape[1]
    hid_width = base.shape[1]
    half = hid_width // 2
    strip, lanes = 16, 512

    @pl.when((tile == 0) & (step == 0))
    def _():
        total_out[...] = jnp.zeros_like(total_out)
        total_in[...] = jnp.zeros_like(total_in)

    @pl.when(step == 0)
    def _():
        anchor = anchor_ref[...]
        diff = target_ref[...] - anchor
        velocity[...] = diff * scale
        win = win_ref[...]
        dots = lambda a: jnp.dot(a, win, preferred_element_type=F32)
        a_high, a_low = split_halves(anchor)
        d_high, d_low = split_halves(diff)
        base[...] = dots(a_high) + dots(a_low)
        move[...] = dots(d_high) + dots(d_low) + shift_ref[...]
        plain[...] = jnp.zeros_like(plain)
        timed[...] = jnp.zeros_like(timed)

    columns = [time_column(times_ref, step * pair + j) for j in range(pair)]
    for j in range(pair):
        for r in range(0, points, strip):
            t = columns[j][r : r + strip]
            for c in range(0, hid_width, lanes):
                at = (slice(r, r + strip), slice(c, c + lanes))
                to = (slice(j * points + r, j * points + r + strip), slice(c, c + lanes))
                pre = base[at] + t * move[at]
                sig = 0.5 * jnp.tanh(0.5 * pre) + 0.5
                act = pre * sig
                hidden[to] = act.astype(BF16)
                slope[to] = (sig + act * (1.0 - sig)).astype(BF16)
        rows = slice(j * points, (j + 1) * points)
        out = jnp.dot(hidden[rows, :], wout_ref[...], preferred_element_type=F32)
        delta[rows, :] = (out * scale - velocity[...]).astype(BF16)
        for c in range(spread.shape[0]):
            spread[c, pl.ds(step * pair + j, points, stride=steps_each), :] = out[
                :, c * 128 : (c + 1) * 128
            ]
    total_out[...] += lax.dot_general(
        hidden[...], delta[...], CONTRACT_ROWS, preferred_element_type=F32
    )
    back[...] = lax.dot_general(
        delta[...], wout_ref[...], CONTRACT_LANES, preferred_element_type=F32
    )
    for r in range(0, points, strip):
        for c in range(0, hid_width, lanes):
            at = (slice(r, r + strip), slice(c, c + lanes))
            plain_sum, timed_sum = plain[at], timed[at]
            for j in range(pair):
                of = (slice(j * points + r, j * points + r + strip), slice(c, c + lanes))
                grad = back[of] * slope[of].astype(F32)
                plain_sum = plain_sum + grad
                timed_sum = timed_sum + columns[j][r : r + strip] * grad
            plain[at] = plain_sum
            timed[at] = timed_sum

    @pl.when(step == pl.num_programs(1) - 1)
    def _():
        for c in range(spread.shape[0]):
            pred_ref[:, c * 128 : (c + 1) * 128] = spread[c].astype(BF16)
        anchor = anchor_ref[...]
        diff = (target_ref[...] - anchor).astype(BF16)
        anchor = anchor.astype(BF16)
        for h in range(2):
            part = slice(h * half, (h + 1) * half)
            total_in[h * width : (h + 1) * width, :] += lax.dot_general(
                anchor, plain[:, part].astype(BF16), CONTRACT_ROWS, preferred_element_type=F32
            ) + lax.dot_general(
                diff, timed[:, part].astype(BF16), CONTRACT_ROWS, preferred_element_type=F32
            )

    @pl.when((step == pl.num_programs(1) - 1) & (tile == pl.num_programs(0) - 1))
    def _():
        store_blocks(devices, ids_ref, total_out, keep_out, send_out)
        store_blocks(devices, ids_ref, total_in, keep_in, send_in)


def place_kernel(devices, wide, ids_ref, own_ref, other_ref, out_ref):
    unit = own_ref.shape[1] * 2 // devices
    lanes = own_ref.shape[2]
    for colour in range(2):
        for block in range(devices):
            pos = ids_ref[colour] ^ block
            far = pos >= devices // 2
            at = pl.multiple_of((pos & (devices // 2 - 1)) * unit, unit)
            value = jnp.where(
                far, other_ref[colour, pl.ds(at, unit), :], own_ref[colour, pl.ds(at, unit), :]
            )
            row = block * unit
            if wide:
                height = out_ref.shape[0]
                left = (row // height) * 2 * lanes + colour * lanes
                row = row % height
            else:
                left = colour * lanes
            out_ref[row : row + unit, left : left + lanes] = value


def place(ids, own, other, shape):
    devices = lax.axis_size("row") * lax.axis_size("col")
    wide = shape[1] > 2 * own.shape[2]
    return pl.pallas_call(
        functools.partial(place_kernel, devices, wide),
        out_shape=jax.ShapeDtypeStruct(shape, jnp.float32),
        grid_spec=pltpu.PrefetchScalarGridSpec(
            num_scalar_prefetch=1, grid=(1,),
            in_specs=[
                pl.BlockSpec(own.shape, lambda i, ids: (0, 0, 0)),
                pl.BlockSpec(own.shape, lambda i, ids: (0, 0, 0)),
            ],
            out_specs=pl.BlockSpec(shape, lambda i, ids: (0, 0)),
        ),
        compiler_params=pltpu.CompilerParams(vmem_limit_bytes=24 << 20),
        cost_estimate=pl.CostEstimate(flops=0, transcendentals=0, bytes_accessed=4 << 20),
        name="place",
    )(ids, own, other)


def sum_over_devices(orders, keep, send):
    count_z = lax.axis_size("col") // 2
    got = swap(send, "col", 1)
    colours = [(keep[c], got[c]) for c in range(2)]
    for step in range(len(orders[0])):
        later = []
        for (mine, other), order in zip(colours, orders):
            half = mine.shape[0] // 2
            out = mine[half:] + other[half:]
            out = swap(out, "row", 1 << order[step])
            later.append((mine[:half] + other[:half], out))
        colours = later
    unit = colours[0][0].shape[0] // count_z
    part = lambda m: jnp.stack(
        [a[m * unit : (m + 1) * unit] + b[m * unit : (m + 1) * unit] for a, b in colours]
    )
    got = [swap(part(m), "col", 2 * m) for m in range(1, count_z)]
    total = part(0)
    for value in got:
        total = total + value
    parts = [total] + [swap(total, "col", 2 * m) for m in range(1, count_z)]
    colours = [jnp.concatenate([p[c] for p in parts], axis=0) for c in range(2)]
    for step in reversed(range(len(orders[0]))):
        colours = [
            jnp.concatenate([value, swap(value, "row", 1 << order[step])], axis=0)
            for value, order in zip(colours, orders)
        ]
    own = jnp.stack(colours)
    return own, swap(own, "col", 1)


def train(anchor, target, times, time_shift, weight_in, weight_out, total_noise):
    share, width = anchor.shape
    steps_each = times.shape[1]
    hid_width = weight_in.shape[1]
    devices = lax.axis_size("row") * lax.axis_size("col")
    orders, ids = colour_ids()
    scale = 1.0 / math.sqrt(float(total_noise * steps_each))
    points = min(share, 256)
    pair = math.gcd(steps_each, 4)
    rows = pair * points
    of_out = jax.ShapeDtypeStruct((2, hid_width // 2, width // 2), F32)
    of_in = jax.ShapeDtypeStruct((2, width, hid_width // 4), F32)
    whole = lambda shape: pl.BlockSpec(shape, lambda i, j, ids: (0,) * len(shape))
    by_tile = lambda shape: pl.BlockSpec(shape, lambda i, j, ids: (i, 0))
    macs = share * steps_each * width * hid_width
    vmem = pltpu.VMEM
    predicted, keep, send, keep_in, send_in = pl.pallas_call(
        functools.partial(train_kernel, devices, pair, scale),
        out_shape=(
            jax.ShapeDtypeStruct((share * steps_each, width), BF16),
            of_out, of_out, of_in, of_in,
        ),
        grid_spec=pltpu.PrefetchScalarGridSpec(
            num_scalar_prefetch=1, grid=(share // points, steps_each // pair),
            in_specs=[
                by_tile((points, width)), by_tile((points, width)),
                by_tile((points, steps_each)), whole((1, hid_width)),
                whole((width, hid_width)), whole((hid_width, width)),
            ],
            out_specs=[by_tile((points * steps_each, width))]
            + [whole(s.shape) for s in (of_out, of_out, of_in, of_in)],
            scratch_shapes=[
                vmem((points, hid_width), F32), vmem((points, hid_width), F32),
                vmem((points, width), F32), vmem((rows, hid_width), BF16),
                vmem((rows, hid_width), BF16), vmem((rows, width), BF16),
                vmem((rows, hid_width), F32), vmem((points, hid_width), F32),
                vmem((points, hid_width), F32),
                vmem((width // 128, points * steps_each, 128), F32),
                vmem((hid_width, width), F32), vmem((2 * width, hid_width // 2), F32),
            ],
        ),
        compiler_params=pltpu.CompilerParams(vmem_limit_bytes=62 << 20),
        cost_estimate=pl.CostEstimate(
            flops=7 * macs, transcendentals=share * steps_each * hid_width,
            bytes_accessed=12 << 20,
        ),
        name="train",
    )(ids, anchor, target, times, time_shift[None, :], weight_in, weight_out)
    out_own, out_other = sum_over_devices(orders, keep, send)
    in_own, in_other = sum_over_devices(orders, keep_in, send_in)
    grad_out = place(ids, out_own, out_other, (hid_width, width))
    grad_in = place(ids, in_own, in_other, (width, hid_width))
    return predicted, grad_in, grad_out


def on_device(noise_points, data_points, times, time_shift, weight_in, weight_out):
    count_row = lax.axis_size("row")
    count_col = lax.axis_size("col")
    rows_here = noise_points.shape[0]
    total_noise = rows_here * count_row
    share = rows_here // count_col
    anchor = lax.dynamic_slice_in_dim(noise_points, lax.axis_index("col") * share, share, 0)
    blocks = gather_points(data_points)
    scores, high, low, local = score(anchor, blocks)
    grid = (count_col // 2, 2, count_row, data_points.shape[0] // count_row)
    summed = column_log_sum(local.reshape(grid)).reshape(local.shape)
    g_scaled = math.log(float(total_noise)) - summed
    target = target_points(scores, g_scaled, high, low)
    return train(anchor, target, times, time_shift, weight_in, weight_out, total_noise)


def solution(mesh):
    in_specs = (P("row", None), P("col", None), P(("row", "col"), None), P(), P(), P())
    out_specs = (P(("row", "col"), None), P(), P())
    return jax.shard_map(
        on_device, mesh=mesh, in_specs=in_specs, out_specs=out_specs, check_vma=False
    )
```

```python
import functools
import math

import jax
import jax.numpy as jnp
from jax import lax
from jax.experimental import pallas as pl
from jax.experimental.pallas import tpu as pltpu
from jax.sharding import PartitionSpec as P

ENTROPY = 0.05
CONTRACT_ROWS = (((0,), (0,)), ((), ()))
CONTRACT_LANES = (((1,), (1,)), ((), ()))
F32, BF16 = jnp.float32, jnp.bfloat16
STRIP = 8
VMEM_BYTES = 60 << 20
ANY = pl.BlockSpec(memory_space=pl.ANY)
VMEM = pl.BlockSpec(memory_space=pltpu.VMEM)


def swap(value, axis, mask):
    size = lax.axis_size(axis)
    return lax.ppermute(value, axis, [(i, i ^ mask) for i in range(size)])


def xor_rows(value, axis, mask):
    if mask == 0:
        return value
    pieces = [
        lax.index_in_dim(value, i ^ mask, axis, True) for i in range(value.shape[axis])
    ]
    return jnp.concatenate(pieces, axis=axis)


def log_sum(values):
    peak = values[0]
    for value in values[1:]:
        peak = jnp.maximum(peak, value)
    total = sum(jnp.exp2(value - peak) for value in values)
    return peak + jnp.log2(total)


def gather_points(data_points):
    count_row = lax.axis_size("row")
    count_z = lax.axis_size("col") // 2
    part = data_points.shape[0] // count_row
    row = lax.axis_index("row")
    pieces = [
        lax.dynamic_slice_in_dim(data_points, (row ^ k) * part, part, 0) for k in range(count_row)
    ]
    own = jnp.concatenate(pieces, axis=0)
    far = [swap(pieces[0], "col", 2 * m) for m in range(1, count_z)]
    blocks = [own, swap(own, "col", 1)]
    for value in far:
        mine = jnp.concatenate(
            [value] + [swap(value, "row", k) for k in range(1, count_row)], axis=0
        )
        blocks += [mine, swap(mine, "col", 1)]
    return blocks


def column_log_sum(local):
    count_z, count_core, count_row, part = local.shape
    parts = [local]
    for k in range(1, count_row):
        parts.append(xor_rows(swap(local, "row", k), 2, k))
    local = log_sum(parts)
    local = log_sum([local, xor_rows(swap(local, "col", 1), 1, 1)])
    parts = [local]
    for m in range(1, count_z):
        parts.append(xor_rows(swap(local, "col", 2 * m), 0, m))
    return log_sum(parts)


def split_halves(value):
    high = value.astype(BF16)
    low = (value - high.astype(F32)).astype(BF16)
    return high, low


def score_kernel(count, log_data, norm, *refs):
    anchor_hbm, block_hbm = refs[0], refs[1 : 1 + count]
    scores_hbm, high_hbm, low_hbm, local_ref = refs[1 + count : 5 + count]
    anchor_ref, blocks, scores, high, low, shift, sems, out_sems = refs[5 + count :]
    points = anchor_ref.shape[0]
    size = block_hbm[0].shape[0]
    copies = [pltpu.make_async_copy(anchor_hbm, anchor_ref, sems.at[count])]
    for i in range(count):
        copies.append(pltpu.make_async_copy(block_hbm[i], blocks.at[i], sems.at[i]))
    for copy in copies:
        copy.start()
    copies[0].wait()
    anchor = anchor_ref[...]
    anchor_sq = jnp.sum(anchor * anchor, axis=1, keepdims=True)
    a_high, a_low = split_halves(anchor)
    dots = lambda a, b: lax.dot_general(a, b, CONTRACT_LANES, preferred_element_type=F32)
    for i in range(count):
        rows = slice(i * size, (i + 1) * size)
        copies[1 + i].wait()
        block = blocks[i]
        b_high, b_low = split_halves(block)
        high[rows, :] = b_high
        low[rows, :] = b_low
        block_sq = jnp.sum(block * block, axis=1, keepdims=True)
        block_sq = jnp.transpose(jnp.broadcast_to(block_sq, (size, 128)))[:1]
        inner = dots(a_high, b_high) + dots(a_high, b_low) + dots(a_low, b_high)
        scores[:, rows] = (2.0 * inner - anchor_sq - block_sq) * norm
    outs = [
        pltpu.make_async_copy(scores, scores_hbm, out_sems.at[0]),
        pltpu.make_async_copy(high, high_hbm, out_sems.at[1]),
        pltpu.make_async_copy(low, low_hbm, out_sems.at[2]),
    ]
    for copy in outs:
        copy.start()
    width = scores.shape[1]

    def by_row(step, peak):
        at = pl.multiple_of(step * STRIP, STRIP)
        s = scores[pl.ds(at, STRIP), :]
        top = jnp.max(s, axis=1, keepdims=True)
        total = jnp.sum(jnp.exp2(s - top), axis=1, keepdims=True)
        f = log_data - top - jnp.log2(total)
        shift[pl.ds(at, STRIP), :] = jnp.broadcast_to(f, (STRIP, shift.shape[1]))
        return jnp.maximum(peak, s + f)

    peak = lax.fori_loop(
        0, points // STRIP, by_row, jnp.full((STRIP, width), -jnp.inf, F32), unroll=8
    )
    peak = jnp.max(peak, axis=0, keepdims=True)
    top = jnp.broadcast_to(peak, (STRIP, width))

    def by_column(step, total):
        at = pl.multiple_of(step * STRIP, STRIP)
        f = shift[pl.ds(at, STRIP), :][:, :1]
        return total + jnp.exp2((scores[pl.ds(at, STRIP), :] + f) - top)

    total = lax.fori_loop(
        0, points // STRIP, by_column, jnp.zeros((STRIP, width), F32), unroll=8
    )
    local_ref[...] = peak + jnp.log2(jnp.sum(total, axis=0, keepdims=True))
    for copy in outs:
        copy.wait()


def score(anchor, blocks):
    points, width = anchor.shape
    count = len(blocks)
    size = blocks[0].shape[0]
    total = count * size
    norm = math.log2(math.e) / (width * ENTROPY)
    return pl.pallas_call(
        functools.partial(score_kernel, count, math.log2(float(total)), norm),
        out_shape=(
            jax.ShapeDtypeStruct((points, total), F32),
            jax.ShapeDtypeStruct((total, width), BF16),
            jax.ShapeDtypeStruct((total, width), BF16),
            jax.ShapeDtypeStruct((1, total), F32),
        ),
        in_specs=[ANY] * (1 + count),
        out_specs=[ANY, ANY, ANY, VMEM],
        scratch_shapes=[
            pltpu.VMEM((points, width), F32), pltpu.VMEM((count, size, width), F32),
            pltpu.VMEM((points, total), F32), pltpu.VMEM((total, width), BF16),
            pltpu.VMEM((total, width), BF16), pltpu.VMEM((points, 128), F32),
            pltpu.SemaphoreType.DMA((1 + count,)), pltpu.SemaphoreType.DMA((3,)),
        ],
        compiler_params=pltpu.CompilerParams(vmem_limit_bytes=VMEM_BYTES),
        cost_estimate=pl.CostEstimate(
            flops=6 * points * total * width, transcendentals=2 * points * total,
            bytes_accessed=13 << 20,
        ),
        name="score",
    )(anchor, *blocks)


def base_kernel(anchor_ref, win_ref, base_ref):
    high, low = split_halves(anchor_ref[...])
    dots = lambda a: jnp.dot(a, win_ref[...], preferred_element_type=F32)
    base_ref[...] = 0.5 * (dots(high) + dots(low))


def anchor_product(anchor, weight_in):
    points, width = anchor.shape
    hid_width = weight_in.shape[1]
    lanes = hid_width // 2
    return pl.pallas_call(
        base_kernel,
        out_shape=jax.ShapeDtypeStruct((points, hid_width), F32),
        grid=(2,),
        in_specs=[
            pl.BlockSpec((points, width), lambda i: (0, 0)),
            pl.BlockSpec((width, lanes), lambda i: (0, i)),
        ],
        out_specs=pl.BlockSpec((points, lanes), lambda i: (0, i)),
        compiler_params=pltpu.CompilerParams(vmem_limit_bytes=VMEM_BYTES),
        cost_estimate=pl.CostEstimate(
            flops=4 * points * width * hid_width, transcendentals=0, bytes_accessed=4 << 20
        ),
        name="base",
    )(anchor, weight_in)


def colour_ids():
    count_row = lax.axis_size("row")
    count_z = lax.axis_size("col") // 2
    row, col = lax.axis_index("row"), lax.axis_index("col")
    bits = list(range(count_row.bit_length() - 1))
    orders = [bits, bits[::-1]]
    ids = []
    for order in orders:
        ident = col & 1
        for bit in order:
            ident = ident * 2 + ((row >> bit) & 1)
        ids.append(ident * count_z + (col >> 1))
    return orders, jnp.stack(ids).astype(jnp.int32)


def store_blocks(devices, ids_ref, total_ref, keep_ref, send_ref):
    unit = total_ref.shape[0] // devices
    lanes = total_ref.shape[1] // 2
    for colour in range(2):
        for pos in range(devices):
            source = pl.multiple_of((ids_ref[colour] ^ pos) * unit, unit)
            block = total_ref[pl.ds(source, unit), colour * lanes : (colour + 1) * lanes]
            out_ref = keep_ref if pos < devices // 2 else send_ref
            at = (pos % (devices // 2)) * unit
            out_ref[colour, at : at + unit, :] = block


def time_column(times_ref, k):
    times = times_ref[...]
    lane = lax.broadcasted_iota(jnp.int32, times.shape, 1)
    return jnp.sum(jnp.where(lane == k, times, 0.0), axis=1, keepdims=True)


def train_kernel(
    devices, scale, ids_ref, scores_hbm, g_ref, high_hbm, low_hbm, anchor_hbm, base_hbm, times_ref,
    shift_ref, win_hbm, wout_hbm, pred_hbm, keep_out, send_out, keep_in, send_in,
    scores, high, low, anchor, base, win, wout, weights, weight_sum, target, velocity, move,
    plain, timed, hidden, slope, delta, back, staged, total_out, total_in, sems, out_sems,
):
    points, width = anchor.shape
    steps_each = times_ref.shape[1]
    hid_width = base.shape[1]
    half = hid_width // 2
    strip, lanes = 16, 512
    moves = [
        (scores_hbm, scores), (high_hbm, high), (low_hbm, low), (anchor_hbm, anchor),
        (win_hbm, win), (base_hbm, base), (wout_hbm, wout),
    ]
    copies = [pltpu.make_async_copy(a, b, sems.at[i]) for i, (a, b) in enumerate(moves)]
    for copy in copies:
        copy.start()

    g = g_ref[...]
    copies[0].wait()

    def weigh(step, unused):
        at = pl.multiple_of(step * strip, strip)
        s = scores[pl.ds(at, strip), :] + g
        w = jnp.exp2(s - jnp.max(s, axis=1, keepdims=True)).astype(BF16)
        weights[pl.ds(at, strip), :] = w
        total = jnp.sum(w.astype(F32), axis=1, keepdims=True)
        weight_sum[pl.ds(at, strip), :] = jnp.broadcast_to(total, (strip, weight_sum.shape[1]))
        return unused

    lax.fori_loop(0, points // strip, weigh, 0, unroll=4)
    for copy in copies[1:5]:
        copy.wait()
    numer = jnp.dot(weights[...], high[...], preferred_element_type=F32)
    numer = numer + jnp.dot(weights[...], low[...], preferred_element_type=F32)
    target[...] = numer / weight_sum[:, :1]
    diff = target[...] - anchor[...]
    velocity[...] = diff * scale
    d_high, d_low = split_halves(diff)
    for c in range(0, hid_width, lanes):
        part = slice(c, c + lanes)
        dots = lambda a: jnp.dot(a, win[:, part], preferred_element_type=F32)
        move[:, part] = 0.5 * (dots(d_high) + dots(d_low) + shift_ref[:, part])
    for copy in copies[5:]:
        copy.wait()
    total_out[...] = jnp.zeros_like(total_out)
    plain[...] = jnp.zeros_like(plain)
    timed[...] = jnp.zeros_like(timed)

    def activate(k, slot):
        t = time_column(times_ref, k)
        for r in range(0, points, strip):
            rows = slice(r, r + strip)
            for c in range(0, hid_width, lanes):
                part = slice(c, c + lanes)
                h = base[rows, part] + t[rows] * move[rows, part]
                u = 1.0 + jnp.tanh(h)
                act = h * u
                hidden[slot][rows, part] = act.astype(BF16)
                slope[slot][rows, part] = u + act * (2.0 - u)

    def leave(k, slot):
        at = pl.ds(pl.multiple_of(k * points, points), points)
        return pltpu.make_async_copy(staged[slot], pred_hbm.at[at], out_sems.at[slot])

    def learn(k, slot, then):
        out = jnp.dot(hidden[slot][...], wout[...], preferred_element_type=F32)
        delta[slot][...] = (out * scale - velocity[...]).astype(BF16)
        staged[slot][...] = out.astype(BF16)
        leave(k, slot).start()
        then()
        total_out[...] += lax.dot_general(
            hidden[slot][...], delta[slot][...], CONTRACT_ROWS, preferred_element_type=F32
        )
        back[slot][...] = lax.dot_general(
            delta[slot][...], wout[...], CONTRACT_LANES, preferred_element_type=F32
        )
        t = time_column(times_ref, k)
        for r in range(0, points, strip):
            rows = slice(r, r + strip)
            for c in range(0, hid_width, lanes):
                part = slice(c, c + lanes)
                grad = back[slot][rows, part] * slope[slot][rows, part]
                plain[rows, part] += grad
                timed[rows, part] += t[rows] * grad

    activate(0, 0)

    def two_steps(i, unused):
        k = 2 * i

        @pl.when(i > 0)
        def _():
            leave(k - 2, 0).wait()
            leave(k - 1, 1).wait()

        learn(k, 0, lambda: activate(k + 1, 1))
        learn(k + 1, 1, lambda: activate(jnp.minimum(k + 2, steps_each - 1), 0))
        return unused

    lax.fori_loop(0, steps_each // 2, two_steps, 0)
    diff = (target[...] - anchor[...]).astype(BF16)
    rounded = anchor[...].astype(BF16)
    for h in range(2):
        part = slice(h * half, (h + 1) * half)
        total_in[h * width : (h + 1) * width, :] = 0.5 * (
            lax.dot_general(
                rounded, plain[:, part].astype(BF16), CONTRACT_ROWS, preferred_element_type=F32
            )
            + lax.dot_general(
                diff, timed[:, part].astype(BF16), CONTRACT_ROWS, preferred_element_type=F32
            )
        )
    store_blocks(devices, ids_ref, total_out, keep_out, send_out)
    store_blocks(devices, ids_ref, total_in, keep_in, send_in)
    leave(steps_each - 2, 0).wait()
    leave(steps_each - 1, 1).wait()


def interleave_kernel(times_ref, pred_ref, spread):
    steps_each, points, width = times_ref.shape
    for k in range(steps_each):
        for c in range(width // 128):
            spread[c, pl.ds(k, points, stride=steps_each), :] = times_ref[
                k, :, c * 128 : (c + 1) * 128
            ].astype(F32)
    for c in range(width // 128):
        pred_ref[:, c * 128 : (c + 1) * 128] = spread[c].astype(BF16)


def interleave(by_time, steps_each):
    rows, width = by_time.shape
    share = rows // steps_each
    points = min(share, 128)
    return pl.pallas_call(
        interleave_kernel,
        out_shape=jax.ShapeDtypeStruct((rows, width), BF16),
        grid=(share // points,),
        in_specs=[pl.BlockSpec((steps_each, points, width), lambda i: (0, i, 0))],
        out_specs=pl.BlockSpec((points * steps_each, width), lambda i: (i, 0)),
        scratch_shapes=[pltpu.VMEM((width // 128, points * steps_each, 128), F32)],
        compiler_params=pltpu.CompilerParams(vmem_limit_bytes=VMEM_BYTES),
        cost_estimate=pl.CostEstimate(flops=0, transcendentals=0, bytes_accessed=8 << 20),
        name="interleave",
    )(by_time.reshape(steps_each, share, width))


def place_kernel(devices, wide, ids_ref, own_ref, other_ref, out_ref):
    unit = own_ref.shape[1] * 2 // devices
    lanes = own_ref.shape[2]
    for colour in range(2):
        for block in range(devices):
            pos = ids_ref[colour] ^ block
            far = pos >= devices // 2
            at = pl.multiple_of((pos & (devices // 2 - 1)) * unit, unit)
            value = jnp.where(
                far, other_ref[colour, pl.ds(at, unit), :], own_ref[colour, pl.ds(at, unit), :]
            )
            row = block * unit
            if wide:
                height = out_ref.shape[0]
                left = (row // height) * 2 * lanes + colour * lanes
                row = row % height
            else:
                left = colour * lanes
            out_ref[row : row + unit, left : left + lanes] = value


def place(ids, own, other, shape):
    devices = lax.axis_size("row") * lax.axis_size("col")
    wide = shape[1] > 2 * own.shape[2]
    return pl.pallas_call(
        functools.partial(place_kernel, devices, wide),
        out_shape=jax.ShapeDtypeStruct(shape, jnp.float32),
        grid_spec=pltpu.PrefetchScalarGridSpec(
            num_scalar_prefetch=1, grid=(1,),
            in_specs=[
                pl.BlockSpec(own.shape, lambda i, ids: (0, 0, 0)),
                pl.BlockSpec(own.shape, lambda i, ids: (0, 0, 0)),
            ],
            out_specs=pl.BlockSpec(shape, lambda i, ids: (0, 0)),
        ),
        compiler_params=pltpu.CompilerParams(vmem_limit_bytes=VMEM_BYTES),
        cost_estimate=pl.CostEstimate(flops=0, transcendentals=0, bytes_accessed=4 << 20),
        name="place",
    )(ids, own, other)


def sum_over_devices(orders, keep, send):
    count_z = lax.axis_size("col") // 2
    got = swap(send, "col", 1)
    colours = [(keep[c], got[c]) for c in range(2)]
    for step in range(len(orders[0])):
        later = []
        for (mine, other), order in zip(colours, orders):
            half = mine.shape[0] // 2
            out = mine[half:] + other[half:]
            out = swap(out, "row", 1 << order[step])
            later.append((mine[:half] + other[:half], out))
        colours = later
    unit = colours[0][0].shape[0] // count_z
    part = lambda m: jnp.stack(
        [a[m * unit : (m + 1) * unit] + b[m * unit : (m + 1) * unit] for a, b in colours]
    )
    got = [swap(part(m), "col", 2 * m) for m in range(1, count_z)]
    total = part(0)
    for value in got:
        total = total + value
    parts = [total] + [swap(total, "col", 2 * m) for m in range(1, count_z)]
    colours = [jnp.concatenate([p[c] for p in parts], axis=0) for c in range(2)]
    for step in reversed(range(len(orders[0]))):
        colours = [
            jnp.concatenate([value, swap(value, "row", 1 << order[step])], axis=0)
            for value, order in zip(colours, orders)
        ]
    own = jnp.stack(colours)
    return own, swap(own, "col", 1)


def train(
    scores, g, high, low, anchor, base, times, time_shift, weight_in, weight_out, total_noise
):
    share, width = anchor.shape
    steps_each = times.shape[1]
    hid_width = weight_in.shape[1]
    total = scores.shape[1]
    devices = lax.axis_size("row") * lax.axis_size("col")
    orders, ids = colour_ids()
    scale = 1.0 / math.sqrt(float(total_noise * steps_each))
    of_out = jax.ShapeDtypeStruct((2, hid_width // 2, width // 2), F32)
    of_in = jax.ShapeDtypeStruct((2, width, hid_width // 4), F32)
    macs = share * steps_each * width * hid_width
    vmem = pltpu.VMEM
    wide, narrow = (share, hid_width), (share, width)
    by_time, keep, send, keep_in, send_in = pl.pallas_call(
        functools.partial(train_kernel, devices, scale),
        out_shape=(
            jax.ShapeDtypeStruct((share * steps_each, width), BF16),
            of_out, of_out, of_in, of_in,
        ),
        in_specs=[
            pl.BlockSpec(memory_space=pltpu.SMEM), ANY, VMEM, ANY, ANY, ANY, ANY, VMEM, VMEM,
            ANY, ANY,
        ],
        out_specs=[ANY, VMEM, VMEM, VMEM, VMEM],
        scratch_shapes=[
            vmem((share, total), F32), vmem((total, width), BF16), vmem((total, width), BF16),
            vmem(narrow, F32), vmem(wide, F32), vmem((width, hid_width), BF16),
            vmem((hid_width, width), BF16), vmem((share, total), BF16), vmem((share, 128), F32),
            vmem(narrow, F32), vmem(narrow, F32), vmem(wide, F32), vmem(wide, F32),
            vmem(wide, F32), (vmem(wide, BF16),) * 2, (vmem(wide, F32),) * 2,
            (vmem(narrow, BF16),) * 2, (vmem(wide, F32),) * 2, (vmem(narrow, BF16),) * 2,
            vmem((hid_width, width), F32), vmem((2 * width, hid_width // 2), F32),
            pltpu.SemaphoreType.DMA((7,)), pltpu.SemaphoreType.DMA((2,)),
        ],
        compiler_params=pltpu.CompilerParams(vmem_limit_bytes=VMEM_BYTES),
        cost_estimate=pl.CostEstimate(
            flops=7 * macs, transcendentals=share * steps_each * hid_width,
            bytes_accessed=24 << 20,
        ),
        name="train",
    )(
        ids, scores, g, high, low, anchor, base, times, time_shift[None, :], weight_in, weight_out
    )
    out_own, out_other = sum_over_devices(orders, keep, send)
    in_own, in_other = sum_over_devices(orders, keep_in, send_in)
    by_time, out_own = lax.optimization_barrier((by_time, out_own))
    predicted = interleave(by_time, steps_each)
    grad_out = place(ids, out_own, out_other, (hid_width, width))
    grad_in = place(ids, in_own, in_other, (width, hid_width))
    return predicted, grad_in, grad_out


def on_device(noise_points, data_points, times, time_shift, weight_in, weight_out):
    count_row = lax.axis_size("row")
    count_col = lax.axis_size("col")
    rows_here = noise_points.shape[0]
    total_noise = rows_here * count_row
    share = rows_here // count_col
    anchor = lax.dynamic_slice_in_dim(noise_points, lax.axis_index("col") * share, share, 0)
    base = anchor_product(anchor, weight_in)
    blocks = gather_points(data_points)
    scores, high, low, local = score(anchor, blocks)
    grid = (count_col // 2, 2, count_row, data_points.shape[0] // count_row)
    summed = column_log_sum(local.reshape(grid)).reshape(local.shape)
    g = math.log2(float(total_noise)) - summed
    return train(
        scores, g, high, low, anchor, base, times, time_shift, weight_in, weight_out, total_noise
    )


def solution(mesh):
    in_specs = (P("row", None), P("col", None), P(("row", "col"), None), P(), P(), P())
    out_specs = (P(("row", "col"), None), P(), P())
    return jax.shard_map(
        on_device, mesh=mesh, in_specs=in_specs, out_specs=out_specs, check_vma=False
    )
```

```python
import functools
import math

import jax
import jax.numpy as jnp
from jax import lax
from jax.experimental import pallas as pl
from jax.experimental.pallas import tpu as pltpu
from jax.sharding import PartitionSpec as P

ENTROPY = 0.05
CONTRACT_ROWS = (((0,), (0,)), ((), ()))
CONTRACT_LANES = (((1,), (1,)), ((), ()))
F32, BF16 = jnp.float32, jnp.bfloat16
STRIP = 8
VMEM_BYTES = 60 << 20
ANY = pl.BlockSpec(memory_space=pl.ANY)
VMEM = pl.BlockSpec(memory_space=pltpu.VMEM)
SMEM = pl.BlockSpec(memory_space=pltpu.SMEM)


def swap(value, axis, mask):
    size = lax.axis_size(axis)
    return lax.ppermute(value, axis, [(i, i ^ mask) for i in range(size)])


def xor_rows(value, axis, mask):
    if mask == 0:
        return value
    pieces = [
        lax.index_in_dim(value, i ^ mask, axis, True) for i in range(value.shape[axis])
    ]
    return jnp.concatenate(pieces, axis=axis)


def log_sum(values):
    peak = values[0]
    for value in values[1:]:
        peak = jnp.maximum(peak, value)
    total = sum(jnp.exp2(value - peak) for value in values)
    return peak + jnp.log2(total)


def gather_points(data_points, ready):
    count_row = lax.axis_size("row")
    count_z = lax.axis_size("col") // 2
    part = data_points.shape[0] // count_row
    row = lax.axis_index("row")
    pieces = [
        lax.dynamic_slice_in_dim(data_points, (row ^ k) * part, part, 0) for k in range(count_row)
    ]
    own = jnp.concatenate(pieces, axis=0)
    far = [swap(pieces[0], "col", 2 * m) for m in range(1, count_z)]
    blocks = [own, swap(own, "col", 1)]
    for m, value in enumerate(far):
        mine = jnp.concatenate(
            [value] + [swap(value, "row", k) for k in range(1, count_row)], axis=0
        )
        if m == len(far) // 2:
            mine, ready = lax.optimization_barrier((mine, ready))
        blocks += [mine, swap(mine, "col", 1)]
    return blocks, ready


def column_log_sum(local):
    count_z, count_core, count_row, part = local.shape
    parts = [local]
    for k in range(1, count_row):
        parts.append(xor_rows(swap(local, "row", k), 2, k))
    local = log_sum(parts)
    local = log_sum([local, xor_rows(swap(local, "col", 1), 1, 1)])
    parts = [local]
    for m in range(1, count_z):
        parts.append(xor_rows(swap(local, "col", 2 * m), 0, m))
    return log_sum(parts)


def split_halves(value):
    high = value.astype(BF16)
    low = (value - high.astype(F32)).astype(BF16)
    return high, low


def positions(shape):
    return [
        (z, core, slice(quarter, quarter + 1), slice(None))
        for z in range(shape[0])
        for core in range(shape[1])
        for quarter in range(shape[2])
    ]


def own_rows(noise_hbm, points, ids_ref):
    at = pl.multiple_of(ids_ref[2] * points, points)
    return noise_hbm.at[pl.ds(at, points)]


def score_kernel(count, log_data, norm, ids_ref, noise_hbm, *refs):
    block_hbm = refs[:count]
    scores_hbm, high_hbm, low_hbm, local_ref = refs[count : 4 + count]
    anchor_ref, blocks, scores, high, low, shift, sems, out_sems = refs[4 + count :]
    points = anchor_ref.shape[0]
    size = block_hbm[0].shape[0]
    copies = [
        pltpu.make_async_copy(own_rows(noise_hbm, points, ids_ref), anchor_ref, sems.at[count])
    ]
    for i in range(count):
        to = blocks.at[pl.ds(i * size, size)]
        copies.append(pltpu.make_async_copy(block_hbm[i], to, sems.at[i]))
    for copy in copies:
        copy.start()
    copies[0].wait()
    anchor = anchor_ref[...]
    anchor_sq = jnp.sum(anchor * anchor, axis=1, keepdims=True)
    a_high, a_low = split_halves(anchor)
    dots = lambda a, b: lax.dot_general(a, b, CONTRACT_LANES, preferred_element_type=F32)
    for i in range(0, count, 2):
        rows = slice(i * size, (i + 2) * size)
        copies[1 + i].wait()
        copies[2 + i].wait()
        block = blocks[rows, :]
        b_high, b_low = split_halves(block)
        high[rows, :] = b_high
        low[rows, :] = b_low
        block_sq = jnp.sum(block * block, axis=1, keepdims=True)
        block_sq = jnp.transpose(jnp.broadcast_to(block_sq, (2 * size, 128)))[:1]
        inner = dots(a_high, b_high) + dots(a_high, b_low) + dots(a_low, b_high)
        scores[:, rows] = (2.0 * inner - anchor_sq - block_sq) * norm
    outs = [
        pltpu.make_async_copy(scores, scores_hbm, out_sems.at[0]),
        pltpu.make_async_copy(high, high_hbm, out_sems.at[1]),
        pltpu.make_async_copy(low, low_hbm, out_sems.at[2]),
    ]
    for copy in outs:
        copy.start()
    width = scores.shape[1]

    def by_row(step, peak):
        at = pl.multiple_of(step * STRIP, STRIP)
        s = scores[pl.ds(at, STRIP), :]
        top = jnp.max(s, axis=1, keepdims=True)
        total = jnp.sum(jnp.exp2(s - top), axis=1, keepdims=True)
        f = log_data - top - jnp.log2(total)
        shift[pl.ds(at, STRIP), :] = jnp.broadcast_to(f, (STRIP, shift.shape[1]))
        return jnp.maximum(peak, s + f)

    peak = lax.fori_loop(
        0, points // STRIP, by_row, jnp.full((STRIP, width), -jnp.inf, F32), unroll=8
    )
    peak = jnp.max(peak, axis=0, keepdims=True)
    top = jnp.broadcast_to(peak, (STRIP, width))

    def by_column(step, total):
        at = pl.multiple_of(step * STRIP, STRIP)
        f = shift[pl.ds(at, STRIP), :][:, :1]
        return total + jnp.exp2((scores[pl.ds(at, STRIP), :] + f) - top)

    total = lax.fori_loop(
        0, points // STRIP, by_column, jnp.zeros((STRIP, width), F32), unroll=8
    )
    local = peak + jnp.log2(jnp.sum(total, axis=0, keepdims=True))
    part = local_ref.shape[-1]
    for i, at in enumerate(positions(local_ref.shape[:-1])):
        local_ref[at] = local[:, i * part : (i + 1) * part]
    for copy in outs:
        copy.wait()


def score(ids, noise_points, blocks, grid):
    points, width = noise_points.shape[0] // lax.axis_size("col"), noise_points.shape[1]
    count = len(blocks)
    size = blocks[0].shape[0]
    total = count * size
    norm = math.log2(math.e) / (width * ENTROPY)
    return pl.pallas_call(
        functools.partial(score_kernel, count, math.log2(float(total)), norm),
        out_shape=(
            jax.ShapeDtypeStruct((points, total), F32),
            jax.ShapeDtypeStruct((total, width), BF16),
            jax.ShapeDtypeStruct((total, width), BF16),
            jax.ShapeDtypeStruct(grid, F32),
        ),
        in_specs=[SMEM] + [ANY] * (1 + count),
        out_specs=[ANY, ANY, ANY, VMEM],
        scratch_shapes=[
            pltpu.VMEM((points, width), F32), pltpu.VMEM((total, width), F32),
            pltpu.VMEM((points, total), F32), pltpu.VMEM((total, width), BF16),
            pltpu.VMEM((total, width), BF16), pltpu.VMEM((points, 128), F32),
            pltpu.SemaphoreType.DMA((1 + count,)), pltpu.SemaphoreType.DMA((3,)),
        ],
        compiler_params=pltpu.CompilerParams(vmem_limit_bytes=VMEM_BYTES),
        cost_estimate=pl.CostEstimate(
            flops=6 * points * total * width, transcendentals=2 * points * total,
            bytes_accessed=13 << 20,
        ),
        name="score",
    )(ids, noise_points, *blocks)


def base_kernel(ids_ref, anchor_ref, win_ref, base_ref):
    high, low = split_halves(anchor_ref[...])
    dots = lambda a: jnp.dot(a, win_ref[...], preferred_element_type=F32)
    base_ref[...] = 0.5 * (dots(high) + dots(low))


def anchor_product(ids, noise_points, weight_in):
    points, width = noise_points.shape[0] // lax.axis_size("col"), noise_points.shape[1]
    hid_width = weight_in.shape[1]
    lanes = hid_width // 2
    return pl.pallas_call(
        base_kernel,
        out_shape=jax.ShapeDtypeStruct((points, hid_width), F32),
        grid_spec=pltpu.PrefetchScalarGridSpec(
            num_scalar_prefetch=1, grid=(2,),
            in_specs=[
                pl.BlockSpec((points, width), lambda i, ids: (ids[2], 0)),
                pl.BlockSpec((width, lanes), lambda i, ids: (0, i)),
            ],
            out_specs=pl.BlockSpec((points, lanes), lambda i, ids: (0, i)),
        ),
        compiler_params=pltpu.CompilerParams(vmem_limit_bytes=VMEM_BYTES),
        cost_estimate=pl.CostEstimate(
            flops=4 * points * width * hid_width, transcendentals=0, bytes_accessed=4 << 20
        ),
        name="base",
    )(ids, noise_points, weight_in)


def colour_ids():
    count_row = lax.axis_size("row")
    count_z = lax.axis_size("col") // 2
    row, col = lax.axis_index("row"), lax.axis_index("col")
    bits = list(range(count_row.bit_length() - 1))
    orders = [bits, bits[::-1]]
    ids = []
    for order in orders:
        ident = col & 1
        for bit in order:
            ident = ident * 2 + ((row >> bit) & 1)
        ids.append(ident * count_z + (col >> 1))
    return orders, jnp.stack(ids + [col]).astype(jnp.int32)


def store_blocks(devices, factor, ids_ref, total_ref, keep_ref, send_ref):
    unit = total_ref.shape[0] // devices
    lanes = total_ref.shape[1] // 2
    for colour in range(2):
        for pos in range(devices):
            source = pl.multiple_of((ids_ref[colour] ^ pos) * unit, unit)
            block = total_ref[pl.ds(source, unit), colour * lanes : (colour + 1) * lanes]
            out_ref = keep_ref if pos < devices // 2 else send_ref
            at = (pos % (devices // 2)) * unit
            out_ref[colour, at : at + unit, :] = block * factor


def time_column(times, k):
    lane = lax.broadcasted_iota(jnp.int32, times.shape, 1)
    return jnp.sum(jnp.where(lane == k, times, 0.0), axis=1, keepdims=True)


def train_kernel(
    devices, scale, ids_ref, scores_hbm, g_ref, high_hbm, low_hbm, noise_hbm, base_hbm, times_hbm,
    shift_ref, win_hbm, wout_hbm, pred_hbm, keep_out, send_out, keep_in, send_in,
    scores, high, low, anchor, base, win, wout, weights, weight_sum, target, velocity, move,
    plain, timed, hidden, slope, delta, back, spread, staged, total_out, total_in, times_row, g_row,
    times_ref, sems, out_sems,
):
    points, width = anchor.shape
    steps_each = times_row.shape[0]
    hid_width = base.shape[1]
    half = hid_width // 2
    strip, lanes = 16, 512
    moves = [
        (scores_hbm, scores), (high_hbm, high), (low_hbm, low),
        (own_rows(noise_hbm, points, ids_ref), anchor), (win_hbm, win), (base_hbm, base),
        (wout_hbm, wout), (times_hbm, times_row),
    ]
    copies = [pltpu.make_async_copy(a, b, sems.at[i]) for i, (a, b) in enumerate(moves)]
    for copy in copies:
        copy.start()

    part = g_ref.shape[-1]
    for i, at in enumerate(positions(g_ref.shape[:-1])):
        g_row[:, i * part : (i + 1) * part] = g_ref[at]
    g = g_row[...]
    copies[0].wait()

    def weigh(step, unused):
        at = pl.multiple_of(step * strip, strip)
        s = scores[pl.ds(at, strip), :] + g
        w = jnp.exp2(s - jnp.max(s, axis=1, keepdims=True)).astype(BF16)
        weights[pl.ds(at, strip), :] = w
        total = jnp.sum(w.astype(F32), axis=1, keepdims=True)
        weight_sum[pl.ds(at, strip), :] = jnp.broadcast_to(total, (strip, weight_sum.shape[1]))
        return unused

    lax.fori_loop(0, points // strip, weigh, 0, unroll=4)
    for copy in copies[1:5]:
        copy.wait()
    numer = jnp.dot(weights[...], high[...], preferred_element_type=F32)
    numer = numer + jnp.dot(weights[...], low[...], preferred_element_type=F32)
    target[...] = numer / weight_sum[:, :1]
    diff = target[...] - anchor[...]
    velocity[...] = diff
    d_high, d_low = split_halves(diff)
    for c in range(0, hid_width, lanes):
        part = slice(c, c + lanes)
        dots = lambda a: jnp.dot(a, win[:, part], preferred_element_type=F32)
        move[:, part] = 0.5 * (dots(d_high) + dots(d_low) + shift_ref[:, part])
    for copy in copies[5:]:
        copy.wait()
    times_ref[...] = jnp.transpose(times_row[...])
    total_out[...] = jnp.zeros_like(total_out)
    plain[...] = jnp.zeros_like(plain)
    timed[...] = jnp.zeros_like(timed)

    def activate(k, slot):
        t = time_column(times_ref[...], k)
        for r in range(0, points, strip):
            rows = slice(r, r + strip)
            for c in range(0, hid_width, lanes):
                part = slice(c, c + lanes)
                h = base[rows, part] + t[rows] * move[rows, part]
                u = 1.0 + jnp.tanh(h)
                act = h * u
                hidden[slot][rows, part] = act.astype(BF16)
                slope[slot][rows, part] = u + act * (2.0 - u)

    def learn(k, slot, then):
        out = jnp.dot(hidden[slot][...], wout[...], preferred_element_type=F32)
        delta[slot][...] = (out - velocity[...]).astype(BF16)
        for c in range(spread.shape[0]):
            spread[c, pl.ds(k, points, stride=steps_each), :] = out[:, c * 128 : (c + 1) * 128]
        then()
        total_out[...] += lax.dot_general(
            hidden[slot][...], delta[slot][...], CONTRACT_ROWS, preferred_element_type=F32
        )
        back[slot][...] = lax.dot_general(
            delta[slot][...], wout[...], CONTRACT_LANES, preferred_element_type=F32
        )
        t = time_column(times_ref[...], k)
        for r in range(0, points, strip):
            rows = slice(r, r + strip)
            for c in range(0, hid_width, lanes):
                part = slice(c, c + lanes)
                grad = back[slot][rows, part] * slope[slot][rows, part]
                plain[rows, part] += grad
                timed[rows, part] += t[rows] * grad

    activate(0, 0)

    def two_steps(i, unused):
        k = 2 * i
        learn(k, 0, lambda: activate(k + 1, 1))
        learn(k + 1, 1, lambda: activate(jnp.minimum(k + 2, steps_each - 1), 0))
        return unused

    lax.fori_loop(0, steps_each // 2, two_steps, 0)
    rows = points * steps_each // len(staged)
    leaves = []
    for i, ref in enumerate(staged):
        for c in range(spread.shape[0]):
            lanes_of = slice(c * 128, (c + 1) * 128)
            ref[:, lanes_of] = spread[c, i * rows : (i + 1) * rows, :].astype(BF16)
        leaves.append(
            pltpu.make_async_copy(ref, pred_hbm.at[pl.ds(i * rows, rows)], out_sems.at[i])
        )
        leaves[-1].start()
    diff = velocity[...].astype(BF16)
    rounded = anchor[...].astype(BF16)
    for h in range(2):
        part = slice(h * half, (h + 1) * half)
        total_in[h * width : (h + 1) * width, :] = (
            lax.dot_general(
                rounded, plain[:, part].astype(BF16), CONTRACT_ROWS, preferred_element_type=F32
            )
            + lax.dot_general(
                diff, timed[:, part].astype(BF16), CONTRACT_ROWS, preferred_element_type=F32
            )
        )
    store_blocks(devices, scale, ids_ref, total_out, keep_out, send_out)
    store_blocks(devices, 0.5 * scale, ids_ref, total_in, keep_in, send_in)
    for copy in leaves:
        copy.wait()


def place_kernel(devices, wide, ids_ref, own_ref, other_ref, out_ref):
    unit = own_ref.shape[1] * 2 // devices
    lanes = own_ref.shape[2]
    for colour in range(2):
        for block in range(devices):
            pos = ids_ref[colour] ^ block
            far = pos >= devices // 2
            at = pl.multiple_of((pos & (devices // 2 - 1)) * unit, unit)
            value = jnp.where(
                far, other_ref[colour, pl.ds(at, unit), :], own_ref[colour, pl.ds(at, unit), :]
            )
            row = block * unit
            if wide:
                height = out_ref.shape[0]
                left = (row // height) * 2 * lanes + colour * lanes
                row = row % height
            else:
                left = colour * lanes
            out_ref[row : row + unit, left : left + lanes] = value


def place(ids, own, other, shape):
    devices = lax.axis_size("row") * lax.axis_size("col")
    wide = shape[1] > 2 * own.shape[2]
    return pl.pallas_call(
        functools.partial(place_kernel, devices, wide),
        out_shape=jax.ShapeDtypeStruct(shape, jnp.float32),
        grid_spec=pltpu.PrefetchScalarGridSpec(
            num_scalar_prefetch=1, grid=(1,),
            in_specs=[
                pl.BlockSpec(own.shape, lambda i, ids: (0, 0, 0)),
                pl.BlockSpec(own.shape, lambda i, ids: (0, 0, 0)),
            ],
            out_specs=pl.BlockSpec(shape, lambda i, ids: (0, 0)),
        ),
        compiler_params=pltpu.CompilerParams(vmem_limit_bytes=24 << 20),
        cost_estimate=pl.CostEstimate(flops=0, transcendentals=0, bytes_accessed=4 << 20),
        name="place",
    )(ids, own, other)


def sum_over_devices(orders, keep, send):
    count_z = lax.axis_size("col") // 2
    got = swap(send, "col", 1)
    colours = [(keep[c], got[c]) for c in range(2)]
    for step in range(len(orders[0])):
        later = []
        for (mine, other), order in zip(colours, orders):
            half = mine.shape[0] // 2
            out = mine[half:] + other[half:]
            out = swap(out, "row", 1 << order[step])
            later.append((mine[:half] + other[:half], out))
        colours = later
    unit = colours[0][0].shape[0] // count_z
    part = lambda m: jnp.stack(
        [a[m * unit : (m + 1) * unit] + b[m * unit : (m + 1) * unit] for a, b in colours]
    )
    got = [swap(part(m), "col", 2 * m) for m in range(1, count_z)]
    total = part(0)
    for value in got:
        total = total + value
    parts = [total] + [swap(total, "col", 2 * m) for m in range(1, count_z)]
    colours = [jnp.concatenate([p[c] for p in parts], axis=0) for c in range(2)]
    for step in reversed(range(len(orders[0]))):
        colours = [
            jnp.concatenate([value, swap(value, "row", 1 << order[step])], axis=0)
            for value, order in zip(colours, orders)
        ]
    own = jnp.stack(colours)
    return own, swap(own, "col", 1)


def train(
    orders, ids, scores, g, high, low, noise_points, base, times, time_shift, weight_in,
    weight_out, total_noise,
):
    share, width = scores.shape[0], high.shape[1]
    steps_each = times.shape[1]
    hid_width = weight_in.shape[1]
    total = scores.shape[1]
    devices = lax.axis_size("row") * lax.axis_size("col")
    scale = 1.0 / math.sqrt(float(total_noise * steps_each))
    of_out = jax.ShapeDtypeStruct((2, hid_width // 2, width // 2), F32)
    of_in = jax.ShapeDtypeStruct((2, width, hid_width // 4), F32)
    macs = share * steps_each * width * hid_width
    vmem = pltpu.VMEM
    wide, narrow = (share, hid_width), (share, width)
    predicted, keep, send, keep_in, send_in = pl.pallas_call(
        functools.partial(train_kernel, devices, scale),
        out_shape=(
            jax.ShapeDtypeStruct((share * steps_each, width), BF16),
            of_out, of_out, of_in, of_in,
        ),
        in_specs=[
            SMEM, ANY, VMEM, ANY, ANY, ANY, ANY, ANY, VMEM, ANY, ANY,
        ],
        out_specs=[ANY, VMEM, VMEM, VMEM, VMEM],
        scratch_shapes=[
            vmem((share, total), F32), vmem((total, width), BF16), vmem((total, width), BF16),
            vmem(narrow, F32), vmem(wide, F32), vmem((width, hid_width), BF16),
            vmem((hid_width, width), BF16), vmem((share, total), BF16), vmem((share, 128), F32),
            vmem(narrow, F32), vmem(narrow, F32), vmem(wide, F32), vmem(wide, F32),
            vmem(wide, F32), (vmem(wide, BF16),) * 2, (vmem(wide, F32),) * 2,
            (vmem(narrow, BF16),) * 2, (vmem(wide, F32),) * 2,
            vmem((width // 128, share * steps_each, 128), F32),
            (vmem((share * steps_each // 4, width), BF16),) * 4,
            vmem((hid_width, width), F32), vmem((2 * width, hid_width // 2), F32),
            vmem((steps_each, share), F32), vmem((1, total), F32), vmem((share, steps_each), F32),
            pltpu.SemaphoreType.DMA((8,)), pltpu.SemaphoreType.DMA((4,)),
        ],
        compiler_params=pltpu.CompilerParams(vmem_limit_bytes=VMEM_BYTES),
        cost_estimate=pl.CostEstimate(
            flops=7 * macs, transcendentals=share * steps_each * hid_width,
            bytes_accessed=24 << 20,
        ),
        name="train",
    )(
        ids, scores, g, high, low, noise_points, base, times.T, time_shift[None, :], weight_in,
        weight_out,
    )
    out_own, out_other = sum_over_devices(orders, keep, send)
    in_own, in_other = sum_over_devices(orders, keep_in, send_in)
    grad_out = place(ids, out_own, out_other, (hid_width, width))
    grad_in = place(ids, in_own, in_other, (width, hid_width))
    return predicted, grad_in, grad_out


def on_device(noise_points, data_points, times, time_shift, weight_in, weight_out):
    count_row = lax.axis_size("row")
    count_col = lax.axis_size("col")
    rows_here = noise_points.shape[0]
    total_noise = rows_here * count_row
    orders, ids = colour_ids()
    base = anchor_product(ids, noise_points, weight_in)
    blocks, (base, ids) = gather_points(data_points, (base, ids))
    grid = (count_col // 2, 2, count_row, data_points.shape[0] // count_row)
    scores, high, low, local = score(ids, noise_points, blocks, grid)
    g = math.log2(float(total_noise)) - column_log_sum(local)
    return train(
        orders, ids, scores, g, high, low, noise_points, base, times, time_shift, weight_in,
        weight_out, total_noise,
    )


def solution(mesh):
    in_specs = (P("row", None), P("col", None), P(("row", "col"), None), P(), P(), P())
    out_specs = (P(("row", "col"), None), P(), P())
    return jax.shard_map(
        on_device, mesh=mesh, in_specs=in_specs, out_specs=out_specs, check_vma=False
    )
```

```python
import functools
import math

import jax
import jax.numpy as jnp
from jax import lax
from jax.experimental import pallas as pl
from jax.experimental.pallas import tpu as pltpu
from jax.sharding import PartitionSpec as P

ENTROPY = 0.05
CONTRACT_ROWS = (((0,), (0,)), ((), ()))
CONTRACT_LANES = (((1,), (1,)), ((), ()))
F32, BF16 = jnp.float32, jnp.bfloat16
STRIP = 8
VMEM_BYTES = 60 << 20
ANY = pl.BlockSpec(memory_space=pl.ANY)
VMEM = pl.BlockSpec(memory_space=pltpu.VMEM)
SMEM = pl.BlockSpec(memory_space=pltpu.SMEM)


def swap(value, axis, mask):
    size = lax.axis_size(axis)
    return lax.ppermute(value, axis, [(i, i ^ mask) for i in range(size)])


def xor_rows(value, axis, mask):
    if mask == 0:
        return value
    pieces = [
        lax.index_in_dim(value, i ^ mask, axis, True) for i in range(value.shape[axis])
    ]
    return jnp.concatenate(pieces, axis=axis)


def log_sum(values):
    peak = values[0]
    for value in values[1:]:
        peak = jnp.maximum(peak, value)
    total = sum(jnp.exp2(value - peak) for value in values)
    return peak + jnp.log2(total)


def gather_points(data_points, ready):
    count_row = lax.axis_size("row")
    count_z = lax.axis_size("col") // 2
    part = data_points.shape[0] // count_row
    row = lax.axis_index("row")
    pieces = [
        lax.dynamic_slice_in_dim(data_points, (row ^ k) * part, part, 0) for k in range(count_row)
    ]
    own = jnp.concatenate(pieces, axis=0)
    far = [swap(pieces[0], "col", 2 * m) for m in range(1, count_z)]
    blocks = [own, swap(own, "col", 1)]
    for m, value in enumerate(far):
        mine = jnp.concatenate(
            [value] + [swap(value, "row", k) for k in range(1, count_row)], axis=0
        )
        if m == len(far) // 2:
            mine, ready = lax.optimization_barrier((mine, ready))
        blocks += [mine, swap(mine, "col", 1)]
    return blocks, ready


def column_log_sum(local):
    count_z, count_core, count_row, part = local.shape
    parts = [local]
    for k in range(1, count_row):
        parts.append(xor_rows(swap(local, "row", k), 2, k))
    local = log_sum(parts)
    local = log_sum([local, xor_rows(swap(local, "col", 1), 1, 1)])
    parts = [local]
    for m in range(1, count_z):
        parts.append(xor_rows(swap(local, "col", 2 * m), 0, m))
    return log_sum(parts)


def split_halves(value):
    high = value.astype(BF16)
    low = (value - high.astype(F32)).astype(BF16)
    return high, low


def positions(shape):
    return [
        (z, core, slice(quarter, quarter + 1), slice(None))
        for z in range(shape[0])
        for core in range(shape[1])
        for quarter in range(shape[2])
    ]


def own_rows(noise_hbm, points, ids_ref):
    at = pl.multiple_of(ids_ref[2] * points, points)
    return noise_hbm.at[pl.ds(at, points)]


def score_kernel(count, log_data, norm, ids_ref, noise_hbm, win_hbm, *refs):
    block_hbm = refs[:count]
    scores_hbm, high_hbm, low_hbm, base_hbm, local_ref = refs[count : 5 + count]
    anchor_ref, blocks, scores, high, low, shift, win, base, sems, out_sems = refs[5 + count :]
    points = anchor_ref.shape[0]
    size = block_hbm[0].shape[0]
    copies = [
        pltpu.make_async_copy(own_rows(noise_hbm, points, ids_ref), anchor_ref, sems.at[count]),
        pltpu.make_async_copy(win_hbm, win, sems.at[count + 1]),
    ]
    for i in range(count):
        to = blocks.at[pl.ds(i * size, size)]
        copies.append(pltpu.make_async_copy(block_hbm[i], to, sems.at[i]))
    for copy in copies:
        copy.start()
    copies[0].wait()
    anchor = anchor_ref[...]
    anchor_sq = jnp.sum(anchor * anchor, axis=1, keepdims=True)
    a_high, a_low = split_halves(anchor)
    copies[1].wait()
    lanes = min(512, base.shape[1])
    for c in range(0, base.shape[1], lanes):
        part = slice(c, c + lanes)
        product = lambda a: jnp.dot(a, win[:, part], preferred_element_type=F32)
        base[:, part] = 0.5 * (product(a_high) + product(a_low))
    dots = lambda a, b: lax.dot_general(a, b, CONTRACT_LANES, preferred_element_type=F32)
    for i in range(0, count, 2):
        rows = slice(i * size, (i + 2) * size)
        copies[2 + i].wait()
        copies[3 + i].wait()
        block = blocks[rows, :]
        b_high, b_low = split_halves(block)
        high[rows, :] = b_high
        low[rows, :] = b_low
        block_sq = jnp.sum(block * block, axis=1, keepdims=True)
        block_sq = jnp.transpose(jnp.broadcast_to(block_sq, (2 * size, 128)))[:1]
        inner = dots(a_high, b_high) + dots(a_high, b_low) + dots(a_low, b_high)
        scores[:, rows] = (2.0 * inner - anchor_sq - block_sq) * norm
    outs = [
        pltpu.make_async_copy(scores, scores_hbm, out_sems.at[0]),
        pltpu.make_async_copy(high, high_hbm, out_sems.at[1]),
        pltpu.make_async_copy(low, low_hbm, out_sems.at[2]),
        pltpu.make_async_copy(base, base_hbm, out_sems.at[3]),
    ]
    for copy in outs:
        copy.start()
    width = scores.shape[1]

    def by_row(step, peak):
        at = pl.multiple_of(step * STRIP, STRIP)
        s = scores[pl.ds(at, STRIP), :]
        top = jnp.max(s, axis=1, keepdims=True)
        total = jnp.sum(jnp.exp2(s - top), axis=1, keepdims=True)
        f = log_data - top - jnp.log2(total)
        shift[pl.ds(at, STRIP), :] = jnp.broadcast_to(f, (STRIP, shift.shape[1]))
        return jnp.maximum(peak, s + f)

    peak = lax.fori_loop(
        0, points // STRIP, by_row, jnp.full((STRIP, width), -jnp.inf, F32), unroll=8
    )
    peak = jnp.max(peak, axis=0, keepdims=True)
    top = jnp.broadcast_to(peak, (STRIP, width))

    def by_column(step, total):
        at = pl.multiple_of(step * STRIP, STRIP)
        f = shift[pl.ds(at, STRIP), :][:, :1]
        return total + jnp.exp2((scores[pl.ds(at, STRIP), :] + f) - top)

    total = lax.fori_loop(
        0, points // STRIP, by_column, jnp.zeros((STRIP, width), F32), unroll=8
    )
    local = peak + jnp.log2(jnp.sum(total, axis=0, keepdims=True))
    part = local_ref.shape[-1]
    for i, at in enumerate(positions(local_ref.shape[:-1])):
        local_ref[at] = local[:, i * part : (i + 1) * part]
    for copy in outs:
        copy.wait()


def score(ids, noise_points, weight_in, blocks, grid):
    points, width = noise_points.shape[0] // lax.axis_size("col"), noise_points.shape[1]
    count = len(blocks)
    size = blocks[0].shape[0]
    total = count * size
    hid_width = weight_in.shape[1]
    norm = math.log2(math.e) / (width * ENTROPY)
    return pl.pallas_call(
        functools.partial(score_kernel, count, math.log2(float(total)), norm),
        out_shape=(
            jax.ShapeDtypeStruct((points, total), F32),
            jax.ShapeDtypeStruct((total, width), BF16),
            jax.ShapeDtypeStruct((total, width), BF16),
            jax.ShapeDtypeStruct((points, hid_width), F32),
            jax.ShapeDtypeStruct(grid, F32),
        ),
        in_specs=[SMEM] + [ANY] * (2 + count),
        out_specs=[ANY, ANY, ANY, ANY, VMEM],
        scratch_shapes=[
            pltpu.VMEM((points, width), F32), pltpu.VMEM((total, width), F32),
            pltpu.VMEM((points, total), F32), pltpu.VMEM((total, width), BF16),
            pltpu.VMEM((total, width), BF16), pltpu.VMEM((points, 128), F32),
            pltpu.VMEM((width, hid_width), BF16), pltpu.VMEM((points, hid_width), F32),
            pltpu.SemaphoreType.DMA((2 + count,)), pltpu.SemaphoreType.DMA((4,)),
        ],
        compiler_params=pltpu.CompilerParams(vmem_limit_bytes=VMEM_BYTES),
        cost_estimate=pl.CostEstimate(
            flops=6 * points * total * width + 4 * points * width * hid_width,
            transcendentals=2 * points * total, bytes_accessed=16 << 20,
        ),
        name="score",
    )(ids, noise_points, weight_in, *blocks)


def colour_ids():
    count_row = lax.axis_size("row")
    count_z = lax.axis_size("col") // 2
    row, col = lax.axis_index("row"), lax.axis_index("col")
    bits = list(range(count_row.bit_length() - 1))
    orders = [bits, bits[::-1]]
    ids = []
    for order in orders:
        ident = col & 1
        for bit in order:
            ident = ident * 2 + ((row >> bit) & 1)
        ids.append(ident * count_z + (col >> 1))
    return orders, jnp.stack(ids + [col]).astype(jnp.int32)


def store_blocks(devices, factor, ids_ref, total_ref, keep_ref, send_ref):
    unit = total_ref.shape[0] // devices
    lanes = total_ref.shape[1] // 2
    for colour in range(2):
        for pos in range(devices):
            source = pl.multiple_of((ids_ref[colour] ^ pos) * unit, unit)
            block = total_ref[pl.ds(source, unit), colour * lanes : (colour + 1) * lanes]
            out_ref = keep_ref if pos < devices // 2 else send_ref
            at = (pos % (devices // 2)) * unit
            out_ref[colour, at : at + unit, :] = block * factor


def time_column(times, k):
    lane = lax.broadcasted_iota(jnp.int32, times.shape, 1)
    return jnp.sum(jnp.where(lane == k, times, 0.0), axis=1, keepdims=True)


def train_kernel(
    devices, scale, ids_ref, scores_hbm, g_ref, high_hbm, low_hbm, noise_hbm, base_hbm, times_hbm,
    shift_ref, win_hbm, wout_hbm, pred_hbm, keep_out, send_out, keep_in, send_in,
    scores, high, low, anchor, base, win, wout, weights, weight_sum, target, velocity, move,
    plain, timed, hidden, slope, delta, back, spread, staged, total_out, total_in, times_row, g_row,
    times_ref, sems, out_sems,
):
    points, width = anchor.shape
    steps_each = times_row.shape[0]
    hid_width = base.shape[1]
    half = hid_width // 2
    strip, lanes = 16, 512
    moves = [
        (scores_hbm, scores), (high_hbm, high), (low_hbm, low),
        (own_rows(noise_hbm, points, ids_ref), anchor), (win_hbm, win), (base_hbm, base),
        (wout_hbm, wout), (times_hbm, times_row),
    ]
    copies = [pltpu.make_async_copy(a, b, sems.at[i]) for i, (a, b) in enumerate(moves)]
    for copy in copies:
        copy.start()

    for ref in (total_out, plain, timed, back[1], slope[1]):
        ref[...] = jnp.zeros_like(ref)
    part = g_ref.shape[-1]
    for i, at in enumerate(positions(g_ref.shape[:-1])):
        g_row[:, i * part : (i + 1) * part] = g_ref[at]
    g = g_row[...]
    copies[0].wait()

    def weigh(step, unused):
        at = pl.multiple_of(step * strip, strip)
        s = scores[pl.ds(at, strip), :] + g
        w = jnp.exp2(s - jnp.max(s, axis=1, keepdims=True)).astype(BF16)
        weights[pl.ds(at, strip), :] = w
        total = jnp.sum(w.astype(F32), axis=1, keepdims=True)
        weight_sum[pl.ds(at, strip), :] = jnp.broadcast_to(total, (strip, weight_sum.shape[1]))
        return unused

    lax.fori_loop(0, points // strip, weigh, 0, unroll=4)
    for copy in copies[1:5]:
        copy.wait()
    numer = jnp.dot(weights[...], high[...], preferred_element_type=F32)
    numer = numer + jnp.dot(weights[...], low[...], preferred_element_type=F32)
    target[...] = numer / weight_sum[:, :1]
    diff = target[...] - anchor[...]
    velocity[...] = diff
    d_high, d_low = split_halves(diff)
    for c in range(0, hid_width, lanes):
        part = slice(c, c + lanes)
        dots = lambda a: jnp.dot(a, win[:, part], preferred_element_type=F32)
        move[:, part] = 0.5 * (dots(d_high) + dots(d_low) + shift_ref[:, part])
    for copy in copies[5:]:
        copy.wait()
    times_ref[...] = jnp.transpose(times_row[...])

    strips = [
        (slice(r, r + strip), slice(c, c + lanes))
        for r in range(0, points, strip)
        for c in range(0, hid_width, lanes)
    ]

    def activate(at, t, slot):
        h = base[at] + t[at[0]] * move[at]
        u = 1.0 + jnp.tanh(h)
        act = h * u
        hidden[slot][at] = act.astype(BF16)
        slope[slot][at] = u + act * (2.0 - u)

    def collect(at, t, slot):
        grad = back[slot][at] * slope[slot][at]
        plain[at] += grad
        timed[at] += t[at[0]] * grad

    def learn(k, slot):
        other = 1 - slot
        times = times_ref[...]
        before = time_column(times, k - 1)
        after = time_column(times, jnp.minimum(k + 1, steps_each - 1))
        block = 256
        to_do = list(strips)
        pieces = 2 * (points // block) + hid_width // block

        def vector_work():
            share = -(-len(strips) // pieces)
            for at in to_do[:share]:
                collect(at, before, other)
                activate(at, after, other)
            del to_do[:share]

        for r in range(0, points, block):
            rows = slice(r, r + block)
            out = jnp.dot(hidden[slot][rows, :], wout[...], preferred_element_type=F32)
            vector_work()
            delta[slot][rows, :] = (out - velocity[rows, :]).astype(BF16)
            for c in range(spread.shape[0]):
                spread[c, pl.ds(r * steps_each + k, block, stride=steps_each), :] = out[
                    :, c * 128 : (c + 1) * 128
                ]
        for r in range(0, points, block):
            rows = slice(r, r + block)
            back[slot][rows, :] = lax.dot_general(
                delta[slot][rows, :], wout[...], CONTRACT_LANES, preferred_element_type=F32
            )
            vector_work()
        for c in range(0, hid_width, block):
            part = slice(c, c + block)
            total_out[part, :] += lax.dot_general(
                hidden[slot][:, part], delta[slot][...], CONTRACT_ROWS,
                preferred_element_type=F32,
            )
            vector_work()

    first = time_column(times_ref[...], 0)
    for at in strips:
        activate(at, first, 0)

    def two_steps(i, unused):
        learn(2 * i, 0)
        learn(2 * i + 1, 1)
        return unused

    lax.fori_loop(0, steps_each // 2, two_steps, 0)
    last = time_column(times_ref[...], steps_each - 1)
    for at in strips:
        collect(at, last, 1)
    rows = points * steps_each // len(staged)
    leaves = []
    for i, ref in enumerate(staged):
        for c in range(spread.shape[0]):
            lanes_of = slice(c * 128, (c + 1) * 128)
            ref[:, lanes_of] = spread[c, i * rows : (i + 1) * rows, :].astype(BF16)
        leaves.append(
            pltpu.make_async_copy(ref, pred_hbm.at[pl.ds(i * rows, rows)], out_sems.at[i])
        )
        leaves[-1].start()
    diff = velocity[...].astype(BF16)
    rounded = anchor[...].astype(BF16)
    for h in range(2):
        part = slice(h * half, (h + 1) * half)
        total_in[h * width : (h + 1) * width, :] = (
            lax.dot_general(
                rounded, plain[:, part].astype(BF16), CONTRACT_ROWS, preferred_element_type=F32
            )
            + lax.dot_general(
                diff, timed[:, part].astype(BF16), CONTRACT_ROWS, preferred_element_type=F32
            )
        )
    store_blocks(devices, scale, ids_ref, total_out, keep_out, send_out)
    store_blocks(devices, 0.5 * scale, ids_ref, total_in, keep_in, send_in)
    for copy in leaves:
        copy.wait()


def place_kernel(devices, wide, ids_ref, own_ref, other_ref, out_ref):
    unit = own_ref.shape[1] * 2 // devices
    lanes = own_ref.shape[2]
    for colour in range(2):
        for block in range(devices):
            pos = ids_ref[colour] ^ block
            far = pos >= devices // 2
            at = pl.multiple_of((pos & (devices // 2 - 1)) * unit, unit)
            value = jnp.where(
                far, other_ref[colour, pl.ds(at, unit), :], own_ref[colour, pl.ds(at, unit), :]
            )
            row = block * unit
            if wide:
                height = out_ref.shape[0]
                left = (row // height) * 2 * lanes + colour * lanes
                row = row % height
            else:
                left = colour * lanes
            out_ref[row : row + unit, left : left + lanes] = value


def place(ids, own, other, shape):
    devices = lax.axis_size("row") * lax.axis_size("col")
    wide = shape[1] > 2 * own.shape[2]
    return pl.pallas_call(
        functools.partial(place_kernel, devices, wide),
        out_shape=jax.ShapeDtypeStruct(shape, jnp.float32),
        grid_spec=pltpu.PrefetchScalarGridSpec(
            num_scalar_prefetch=1, grid=(1,),
            in_specs=[
                pl.BlockSpec(own.shape, lambda i, ids: (0, 0, 0)),
                pl.BlockSpec(own.shape, lambda i, ids: (0, 0, 0)),
            ],
            out_specs=pl.BlockSpec(shape, lambda i, ids: (0, 0)),
        ),
        compiler_params=pltpu.CompilerParams(vmem_limit_bytes=24 << 20),
        cost_estimate=pl.CostEstimate(flops=0, transcendentals=0, bytes_accessed=4 << 20),
        name="place",
    )(ids, own, other)


def sum_over_devices(orders, keep, send, lead=None):
    count_z = lax.axis_size("col") // 2
    got = swap(send, "col", 1)
    if lead is not None:
        got, lead = lax.optimization_barrier((got, lead))
    colours = [(keep[c], got[c]) for c in range(2)]
    received = None
    for step in range(len(orders[0])):
        later = []
        for (mine, other), order in zip(colours, orders):
            half = mine.shape[0] // 2
            out = mine[half:] + other[half:]
            out = swap(out, "row", 1 << order[step])
            later.append((mine[:half] + other[:half], out))
        colours = later
        if received is None:
            received = [other for mine, other in colours]
            received, colours = lax.optimization_barrier((received, colours))
    unit = colours[0][0].shape[0] // count_z
    part = lambda m: jnp.stack(
        [a[m * unit : (m + 1) * unit] + b[m * unit : (m + 1) * unit] for a, b in colours]
    )
    got = [swap(part(m), "col", 2 * m) for m in range(1, count_z)]
    total = part(0)
    for value in got:
        total = total + value
    parts = [total] + [swap(total, "col", 2 * m) for m in range(1, count_z)]
    colours = [jnp.concatenate([p[c] for p in parts], axis=0) for c in range(2)]
    for step in reversed(range(len(orders[0]))):
        colours = [
            jnp.concatenate([value, swap(value, "row", 1 << order[step])], axis=0)
            for value, order in zip(colours, orders)
        ]
    own = jnp.stack(colours)
    return own, swap(own, "col", 1), received


def train(
    orders, ids, scores, g, high, low, noise_points, base, times, time_shift, weight_in,
    weight_out, total_noise,
):
    share, width = scores.shape[0], high.shape[1]
    steps_each = times.shape[1]
    hid_width = weight_in.shape[1]
    total = scores.shape[1]
    devices = lax.axis_size("row") * lax.axis_size("col")
    scale = 1.0 / math.sqrt(float(total_noise * steps_each))
    of_out = jax.ShapeDtypeStruct((2, hid_width // 2, width // 2), F32)
    of_in = jax.ShapeDtypeStruct((2, width, hid_width // 4), F32)
    macs = share * steps_each * width * hid_width
    vmem = pltpu.VMEM
    wide, narrow = (share, hid_width), (share, width)
    predicted, keep, send, keep_in, send_in = pl.pallas_call(
        functools.partial(train_kernel, devices, scale),
        out_shape=(
            jax.ShapeDtypeStruct((share * steps_each, width), BF16),
            of_out, of_out, of_in, of_in,
        ),
        in_specs=[
            SMEM, ANY, VMEM, ANY, ANY, ANY, ANY, ANY, VMEM, ANY, ANY,
        ],
        out_specs=[ANY, VMEM, VMEM, VMEM, VMEM],
        scratch_shapes=[
            vmem((share, total), F32), vmem((total, width), BF16), vmem((total, width), BF16),
            vmem(narrow, F32), vmem(wide, F32), vmem((width, hid_width), BF16),
            vmem((hid_width, width), BF16), vmem((share, total), BF16), vmem((share, 128), F32),
            vmem(narrow, F32), vmem(narrow, F32), vmem(wide, F32), vmem(wide, F32),
            vmem(wide, F32), (vmem(wide, BF16),) * 2, (vmem(wide, F32),) * 2,
            (vmem(narrow, BF16),) * 2, (vmem(wide, F32),) * 2,
            vmem((width // 128, share * steps_each, 128), F32),
            (vmem((share * steps_each // 4, width), BF16),) * 4,
            vmem((hid_width, width), F32), vmem((2 * width, hid_width // 2), F32),
            vmem((steps_each, share), F32), vmem((1, total), F32), vmem((share, steps_each), F32),
            pltpu.SemaphoreType.DMA((8,)), pltpu.SemaphoreType.DMA((4,)),
        ],
        compiler_params=pltpu.CompilerParams(vmem_limit_bytes=VMEM_BYTES),
        cost_estimate=pl.CostEstimate(
            flops=7 * macs, transcendentals=share * steps_each * hid_width,
            bytes_accessed=24 << 20,
        ),
        name="train",
    )(
        ids, scores, g, high, low, noise_points, base, times.T, time_shift[None, :], weight_in,
        weight_out,
    )
    out_own, out_other, lead = sum_over_devices(orders, keep, send)
    in_own, in_other, unused = sum_over_devices(orders, keep_in, send_in, lead)
    grad_out = place(ids, out_own, out_other, (hid_width, width))
    grad_in = place(ids, in_own, in_other, (width, hid_width))
    return predicted, grad_in, grad_out


def on_device(noise_points, data_points, times, time_shift, weight_in, weight_out):
    count_row = lax.axis_size("row")
    count_col = lax.axis_size("col")
    rows_here = noise_points.shape[0]
    total_noise = rows_here * count_row
    orders, ids = colour_ids()
    blocks, ids = gather_points(data_points, ids)
    grid = (count_col // 2, 2, count_row, data_points.shape[0] // count_row)
    scores, high, low, base, local = score(ids, noise_points, weight_in, blocks, grid)
    g = math.log2(float(total_noise)) - column_log_sum(local)
    return train(
        orders, ids, scores, g, high, low, noise_points, base, times, time_shift, weight_in,
        weight_out, total_noise,
    )


def solution(mesh):
    in_specs = (P("row", None), P("col", None), P(("row", "col"), None), P(), P(), P())
    out_specs = (P(("row", "col"), None), P(), P())
    return jax.shard_map(
        on_device, mesh=mesh, in_specs=in_specs, out_specs=out_specs, check_vma=False
    )
```

```python
import functools
import math

import jax
import jax.numpy as jnp
from jax import lax
from jax.experimental import pallas as pl
from jax.experimental.pallas import tpu as pltpu
from jax.sharding import PartitionSpec as P


ENTROPY = 0.05
CONTRACT_ROWS = (((0,), (0,)), ((), ()))
CONTRACT_LANES = (((1,), (1,)), ((), ()))
F32, BF16 = jnp.float32, jnp.bfloat16
STRIP = 8
VMEM_BYTES = 60 << 20
ANY = pl.BlockSpec(memory_space=pl.ANY)
VMEM = pl.BlockSpec(memory_space=pltpu.VMEM)
SMEM = pl.BlockSpec(memory_space=pltpu.SMEM)


def swap(value, axis, mask):
    size = lax.axis_size(axis)
    return lax.ppermute(value, axis, [(i, i ^ mask) for i in range(size)])


def xor_rows(value, axis, mask):
    if mask == 0:
        return value
    pieces = [
        lax.index_in_dim(value, i ^ mask, axis, True) for i in range(value.shape[axis])
    ]
    return jnp.concatenate(pieces, axis=axis)


def log_sum(values):
    peak = values[0]
    for value in values[1:]:
        peak = jnp.maximum(peak, value)
    total = sum(jnp.exp2(value - peak) for value in values)
    return peak + jnp.log2(total)


def gather_points(data_points):
    count_row = lax.axis_size("row")
    count_z = lax.axis_size("col") // 2
    part = data_points.shape[0] // count_row
    row = lax.axis_index("row")
    pieces = [
        lax.dynamic_slice_in_dim(data_points, (row ^ k) * part, part, 0) for k in range(count_row)
    ]
    own = jnp.concatenate(pieces, axis=0)
    far = [swap(pieces[0], "col", 2 * m) for m in range(1, count_z)]
    blocks = [own, swap(own, "col", 1)]
    for value in far:
        mine = jnp.concatenate(
            [value] + [swap(value, "row", k) for k in range(1, count_row)], axis=0
        )
        blocks += [mine, swap(mine, "col", 1)]
    return blocks


def column_log_sum(local):
    count_z, _, count_row, _ = local.shape
    parts = [local]
    for k in range(1, count_row):
        parts.append(xor_rows(swap(local, "row", k), 2, k))
    local = log_sum(parts)
    local = log_sum([local, xor_rows(swap(local, "col", 1), 1, 1)])
    parts = [local]
    for m in range(1, count_z):
        parts.append(xor_rows(swap(local, "col", 2 * m), 0, m))
    return log_sum(parts)


def split_halves(value):
    high = value.astype(BF16)
    low = (value - high.astype(F32)).astype(BF16)
    return high, low


def positions(shape):
    return [
        (z, core, slice(quarter, quarter + 1), slice(None))
        for z in range(shape[0])
        for core in range(shape[1])
        for quarter in range(shape[2])
    ]


def own_rows(noise_hbm, points, ids_ref):
    at = pl.multiple_of(ids_ref[2] * points, points)
    return noise_hbm.at[pl.ds(at, points)]


def score_kernel(count, log_data, norm, ids_ref, noise_hbm, win_hbm, *refs):
    block_hbm = refs[:count]
    scores_hbm, high_hbm, low_hbm, base_hbm, local_ref = refs[count : 5 + count]
    anchor_ref, blocks, scores, high, low, shift, win, base, sems, out_sems = refs[5 + count :]
    points = anchor_ref.shape[0]
    size = block_hbm[0].shape[0]
    copies = [
        pltpu.make_async_copy(own_rows(noise_hbm, points, ids_ref), anchor_ref, sems.at[count]),
        pltpu.make_async_copy(win_hbm, win, sems.at[count + 1]),
    ]
    for i in range(count):
        to = blocks.at[pl.ds(i * size, size)]
        copies.append(pltpu.make_async_copy(block_hbm[i], to, sems.at[i]))
    for copy in copies:
        copy.start()
    copies[0].wait()
    anchor = anchor_ref[...]
    anchor_sq = jnp.sum(anchor * anchor, axis=1, keepdims=True)
    a_high, a_low = split_halves(anchor)
    copies[1].wait()
    lanes = min(512, base.shape[1])
    for c in range(0, base.shape[1], lanes):
        part = slice(c, c + lanes)
        product = lambda a: jnp.dot(a, win[:, part], preferred_element_type=F32)
        base[:, part] = 0.5 * (product(a_high) + product(a_low))
    dots = lambda a, b: lax.dot_general(a, b, CONTRACT_LANES, preferred_element_type=F32)
    for i in range(0, count, 2):
        rows = slice(i * size, (i + 2) * size)
        copies[2 + i].wait()
        copies[3 + i].wait()
        block = blocks[rows, :]
        b_high, b_low = split_halves(block)
        high[rows, :] = b_high
        low[rows, :] = b_low
        block_sq = jnp.sum(block * block, axis=1, keepdims=True)
        block_sq = jnp.transpose(jnp.broadcast_to(block_sq, (2 * size, 128)))[:1]
        inner = dots(a_high, b_high) + dots(a_high, b_low) + dots(a_low, b_high)
        scores[:, rows] = (2.0 * inner - anchor_sq - block_sq) * norm
    outs = [
        pltpu.make_async_copy(scores, scores_hbm, out_sems.at[0]),
        pltpu.make_async_copy(high, high_hbm, out_sems.at[1]),
        pltpu.make_async_copy(low, low_hbm, out_sems.at[2]),
        pltpu.make_async_copy(base, base_hbm, out_sems.at[3]),
    ]
    for copy in outs:
        copy.start()
    width = scores.shape[1]

    def by_row(step, peak):
        at = pl.multiple_of(step * STRIP, STRIP)
        s = scores[pl.ds(at, STRIP), :]
        top = jnp.max(s, axis=1, keepdims=True)
        total = jnp.sum(jnp.exp2(s - top), axis=1, keepdims=True)
        f = log_data - top - jnp.log2(total)
        shift[pl.ds(at, STRIP), :] = jnp.broadcast_to(f, (STRIP, shift.shape[1]))
        return jnp.maximum(peak, s + f)

    peak = lax.fori_loop(
        0, points // STRIP, by_row, jnp.full((STRIP, width), -jnp.inf, F32), unroll=8
    )
    peak = jnp.max(peak, axis=0, keepdims=True)
    top = jnp.broadcast_to(peak, (STRIP, width))

    def by_column(step, total):
        at = pl.multiple_of(step * STRIP, STRIP)
        f = shift[pl.ds(at, STRIP), :][:, :1]
        return total + jnp.exp2((scores[pl.ds(at, STRIP), :] + f) - top)

    total = lax.fori_loop(
        0, points // STRIP, by_column, jnp.zeros((STRIP, width), F32), unroll=8
    )
    local = peak + jnp.log2(jnp.sum(total, axis=0, keepdims=True))
    part = local_ref.shape[-1]
    for i, at in enumerate(positions(local_ref.shape[:-1])):
        local_ref[at] = local[:, i * part : (i + 1) * part]
    for copy in outs:
        copy.wait()


def score(ids, noise_points, weight_in, blocks, grid):
    points, width = noise_points.shape[0] // lax.axis_size("col"), noise_points.shape[1]
    count = len(blocks)
    size = blocks[0].shape[0]
    total = count * size
    hid_width = weight_in.shape[1]
    norm = math.log2(math.e) / (width * ENTROPY)
    return pl.pallas_call(
        functools.partial(score_kernel, count, math.log2(float(total)), norm),
        out_shape=(
            jax.ShapeDtypeStruct((points, total), F32),
            jax.ShapeDtypeStruct((total, width), BF16),
            jax.ShapeDtypeStruct((total, width), BF16),
            jax.ShapeDtypeStruct((points, hid_width), F32),
            jax.ShapeDtypeStruct(grid, F32),
        ),
        in_specs=[SMEM] + [ANY] * (2 + count),
        out_specs=[ANY, ANY, ANY, ANY, VMEM],
        scratch_shapes=[
            pltpu.VMEM((points, width), F32), pltpu.VMEM((total, width), F32),
            pltpu.VMEM((points, total), F32), pltpu.VMEM((total, width), BF16),
            pltpu.VMEM((total, width), BF16), pltpu.VMEM((points, 128), F32),
            pltpu.VMEM((width, hid_width), BF16), pltpu.VMEM((points, hid_width), F32),
            pltpu.SemaphoreType.DMA((2 + count,)), pltpu.SemaphoreType.DMA((4,)),
        ],
        compiler_params=pltpu.CompilerParams(vmem_limit_bytes=VMEM_BYTES),
        cost_estimate=pl.CostEstimate(
            flops=6 * points * total * width + 4 * points * width * hid_width,
            transcendentals=2 * points * total, bytes_accessed=16 << 20,
        ),
        name="score",
    )(ids, noise_points, weight_in, *blocks)


def colour_ids():
    count_row = lax.axis_size("row")
    count_z = lax.axis_size("col") // 2
    row, col = lax.axis_index("row"), lax.axis_index("col")
    bits = list(range(count_row.bit_length() - 1))
    orders = [bits, bits[::-1]]
    ids = []
    for order in orders:
        ident = col & 1
        for bit in order:
            ident = ident * 2 + ((row >> bit) & 1)
        ids.append(ident * count_z + (col >> 1))
    return orders, jnp.stack(ids + [col]).astype(jnp.int32)


def store_blocks(devices, factor, ids_ref, total_ref, keep_ref, send_ref):
    unit = total_ref.shape[0] // devices
    lanes = total_ref.shape[1] // 2
    for colour in range(2):
        for pos in range(devices):
            source = pl.multiple_of((ids_ref[colour] ^ pos) * unit, unit)
            block = total_ref[pl.ds(source, unit), colour * lanes : (colour + 1) * lanes]
            out_ref = keep_ref if pos < devices // 2 else send_ref
            at = (pos % (devices // 2)) * unit
            out_ref[colour, at : at + unit, :] = block * factor


def time_column(times, k):
    lane = lax.broadcasted_iota(jnp.int32, times.shape, 1)
    return jnp.sum(jnp.where(lane == k, times, 0.0), axis=1, keepdims=True)


def train_kernel(
    devices, scale, ids_ref, scores_hbm, g_ref, high_hbm, low_hbm, noise_hbm, base_hbm, times_hbm,
    shift_ref, win_hbm, wout_hbm, pred_hbm, keep_out, send_out, keep_in, send_in,
    scores, high, low, anchor, base, win, wout, weights, weight_sum, target, velocity, move,
    plain, timed, hidden, slope, delta, back, spread, staged, total_out, total_in, times_row, g_row,
    times_ref, sems, out_sems,
):
    points, width = anchor.shape
    steps_each = times_row.shape[0]
    hid_width = base.shape[1]
    half = hid_width // 2
    strip, lanes = 16, 512
    moves = [
        (scores_hbm, scores), (high_hbm, high), (low_hbm, low),
        (own_rows(noise_hbm, points, ids_ref), anchor), (win_hbm, win), (base_hbm, base),
        (wout_hbm, wout), (times_hbm, times_row),
    ]
    copies = [pltpu.make_async_copy(a, b, sems.at[i]) for i, (a, b) in enumerate(moves)]
    for copy in copies:
        copy.start()

    for ref in (total_out, plain, timed, back[1], slope[1]):
        ref[...] = jnp.zeros_like(ref)
    part = g_ref.shape[-1]
    for i, at in enumerate(positions(g_ref.shape[:-1])):
        g_row[:, i * part : (i + 1) * part] = g_ref[at]
    g = g_row[...]
    copies[0].wait()

    def weigh(step, unused):
        at = pl.multiple_of(step * strip, strip)
        s = scores[pl.ds(at, strip), :] + g
        w = jnp.exp2(s - jnp.max(s, axis=1, keepdims=True)).astype(BF16)
        weights[pl.ds(at, strip), :] = w
        total = jnp.sum(w.astype(F32), axis=1, keepdims=True)
        weight_sum[pl.ds(at, strip), :] = jnp.broadcast_to(total, (strip, weight_sum.shape[1]))
        return unused

    lax.fori_loop(0, points // strip, weigh, 0, unroll=4)
    for copy in copies[1:5]:
        copy.wait()
    numer = jnp.dot(weights[...], high[...], preferred_element_type=F32)
    numer = numer + jnp.dot(weights[...], low[...], preferred_element_type=F32)
    target[...] = numer / weight_sum[:, :1]
    diff = target[...] - anchor[...]
    velocity[...] = diff
    d_high, d_low = split_halves(diff)
    for c in range(0, hid_width, lanes):
        part = slice(c, c + lanes)
        dots = lambda a: jnp.dot(a, win[:, part], preferred_element_type=F32)
        move[:, part] = 0.5 * (dots(d_high) + dots(d_low) + shift_ref[:, part])
    for copy in copies[5:]:
        copy.wait()
    times_ref[...] = jnp.transpose(times_row[...])

    strips = [
        (slice(r, r + strip), slice(c, c + lanes))
        for r in range(0, points, strip)
        for c in range(0, hid_width, lanes)
    ]

    def activate(at, t, slot):
        h = base[at] + t[at[0]] * move[at]
        u = 1.0 + jnp.tanh(h)
        act = h * u
        hidden[slot][at] = act.astype(BF16)
        slope[slot][at] = u + act * (2.0 - u)

    def collect(at, t, slot):
        grad = back[slot][at] * slope[slot][at]
        plain[at] += grad
        timed[at] += t[at[0]] * grad

    def learn(k, slot):
        other = 1 - slot
        times = times_ref[...]
        before = time_column(times, k - 1)
        after = time_column(times, jnp.minimum(k + 1, steps_each - 1))
        to_do = list(strips)

        def vector_work(count):
            for at in to_do[:count]:
                collect(at, before, other)
                activate(at, after, other)
            del to_do[:count]

        out = jnp.dot(hidden[slot][...], wout[...], preferred_element_type=F32)
        vector_work(len(strips) // 2)
        delta[slot][...] = (out - velocity[...]).astype(BF16)
        for c in range(spread.shape[0]):
            spread[c, pl.ds(k, points, stride=steps_each), :] = out[:, c * 128 : (c + 1) * 128]
        back[slot][...] = lax.dot_general(
            delta[slot][...], wout[...], CONTRACT_LANES, preferred_element_type=F32
        )
        vector_work(len(strips))
        total_out[...] += lax.dot_general(
            hidden[slot][...], delta[slot][...], CONTRACT_ROWS, preferred_element_type=F32
        )

    start = time_column(times_ref[...], 0)
    for at in strips:
        activate(at, start, 0)

    def two_steps(i, unused):
        learn(2 * i, 0)
        learn(2 * i + 1, 1)
        return unused

    lax.fori_loop(0, steps_each // 2, two_steps, 0)
    last = time_column(times_ref[...], steps_each - 1)
    for at in strips:
        collect(at, last, 1)
    rows = points * steps_each // len(staged)
    leaves = []
    for i, ref in enumerate(staged):
        for c in range(spread.shape[0]):
            lanes_of = slice(c * 128, (c + 1) * 128)
            ref[:, lanes_of] = spread[c, i * rows : (i + 1) * rows, :].astype(BF16)
        leaves.append(
            pltpu.make_async_copy(ref, pred_hbm.at[pl.ds(i * rows, rows)], out_sems.at[i])
        )
        leaves[-1].start()
    diff = velocity[...].astype(BF16)
    rounded = anchor[...].astype(BF16)
    for h in range(2):
        part = slice(h * half, (h + 1) * half)
        total_in[h * width : (h + 1) * width, :] = (
            lax.dot_general(
                rounded, plain[:, part].astype(BF16), CONTRACT_ROWS, preferred_element_type=F32
            )
            + lax.dot_general(
                diff, timed[:, part].astype(BF16), CONTRACT_ROWS, preferred_element_type=F32
            )
        )
    store_blocks(devices, scale, ids_ref, total_out, keep_out, send_out)
    store_blocks(devices, 0.5 * scale, ids_ref, total_in, keep_in, send_in)
    for copy in leaves:
        copy.wait()


def place_kernel(devices, wide, ids_ref, own_ref, other_ref, out_ref):
    unit = own_ref.shape[1] * 2 // devices
    lanes = own_ref.shape[2]
    for colour in range(2):
        for block in range(devices):
            pos = ids_ref[colour] ^ block
            far = pos >= devices // 2
            at = pl.multiple_of((pos & (devices // 2 - 1)) * unit, unit)
            value = jnp.where(
                far, other_ref[colour, pl.ds(at, unit), :], own_ref[colour, pl.ds(at, unit), :]
            )
            row = block * unit
            if wide:
                height = out_ref.shape[0]
                left = (row // height) * 2 * lanes + colour * lanes
                row = row % height
            else:
                left = colour * lanes
            out_ref[row : row + unit, left : left + lanes] = value


def place(ids, own, other, shape):
    devices = lax.axis_size("row") * lax.axis_size("col")
    wide = shape[1] > 2 * own.shape[2]
    return pl.pallas_call(
        functools.partial(place_kernel, devices, wide),
        out_shape=jax.ShapeDtypeStruct(shape, jnp.float32),
        grid_spec=pltpu.PrefetchScalarGridSpec(
            num_scalar_prefetch=1, grid=(1,),
            in_specs=[
                pl.BlockSpec(own.shape, lambda i, ids: (0, 0, 0)),
                pl.BlockSpec(own.shape, lambda i, ids: (0, 0, 0)),
            ],
            out_specs=pl.BlockSpec(shape, lambda i, ids: (0, 0)),
        ),
        compiler_params=pltpu.CompilerParams(vmem_limit_bytes=24 << 20),
        cost_estimate=pl.CostEstimate(flops=0, transcendentals=0, bytes_accessed=4 << 20),
        name="place",
    )(ids, own, other)


def sum_over_devices(orders, keep, send):
    count_z = lax.axis_size("col") // 2
    got = swap(send, "col", 1)
    colours = [(keep[c], got[c]) for c in range(2)]
    for step in range(len(orders[0])):
        later = []
        for (mine, other), order in zip(colours, orders):
            half = mine.shape[0] // 2
            out = mine[half:] + other[half:]
            out = swap(out, "row", 1 << order[step])
            later.append((mine[:half] + other[:half], out))
        colours = later
    unit = colours[0][0].shape[0] // count_z
    part = lambda m: jnp.stack(
        [a[m * unit : (m + 1) * unit] + b[m * unit : (m + 1) * unit] for a, b in colours]
    )
    got = [swap(part(m), "col", 2 * m) for m in range(1, count_z)]
    total = part(0)
    for value in got:
        total = total + value
    parts = [total]
    parts += [swap(total, "col", 2 * m) for m in range(1, count_z)]
    colours = [jnp.concatenate([p[c] for p in parts], axis=0) for c in range(2)]
    for step in reversed(range(len(orders[0]))):
        colours = [
            jnp.concatenate([value, swap(value, "row", 1 << order[step])], axis=0)
            for value, order in zip(colours, orders)
        ]
    own = jnp.stack(colours)
    return own, swap(own, "col", 1)


def train(
    orders, ids, scores, g, high, low, noise_points, base, times, time_shift, weight_in,
    weight_out, total_noise,
):
    share, width = scores.shape[0], high.shape[1]
    steps_each = times.shape[1]
    hid_width = weight_in.shape[1]
    total = scores.shape[1]
    devices = lax.axis_size("row") * lax.axis_size("col")
    scale = 1.0 / math.sqrt(float(total_noise * steps_each))
    of_out = jax.ShapeDtypeStruct((2, hid_width // 2, width // 2), F32)
    of_in = jax.ShapeDtypeStruct((2, width, hid_width // 4), F32)
    macs = share * steps_each * width * hid_width
    vmem = pltpu.VMEM
    wide, narrow = (share, hid_width), (share, width)
    predicted, keep, send, keep_in, send_in = pl.pallas_call(
        functools.partial(train_kernel, devices, scale),
        out_shape=(
            jax.ShapeDtypeStruct((share * steps_each, width), BF16),
            of_out, of_out, of_in, of_in,
        ),
        in_specs=[
            SMEM, ANY, VMEM, ANY, ANY, ANY, ANY, ANY, VMEM, ANY, ANY,
        ],
        out_specs=[ANY, VMEM, VMEM, VMEM, VMEM],
        scratch_shapes=[
            vmem((share, total), F32), vmem((total, width), BF16), vmem((total, width), BF16),
            vmem(narrow, F32), vmem(wide, F32), vmem((width, hid_width), BF16),
            vmem((hid_width, width), BF16), vmem((share, total), BF16), vmem((share, 128), F32),
            vmem(narrow, F32), vmem(narrow, F32), vmem(wide, F32), vmem(wide, F32),
            vmem(wide, F32), (vmem(wide, BF16),) * 2, (vmem(wide, F32),) * 2,
            (vmem(narrow, BF16),) * 2, (vmem(wide, F32),) * 2,
            vmem((width // 128, share * steps_each, 128), F32),
            (vmem((share * steps_each // 4, width), BF16),) * 4,
            vmem((hid_width, width), F32), vmem((2 * width, hid_width // 2), F32),
            vmem((steps_each, share), F32), vmem((1, total), F32), vmem((share, steps_each), F32),
            pltpu.SemaphoreType.DMA((8,)), pltpu.SemaphoreType.DMA((4,)),
        ],
        compiler_params=pltpu.CompilerParams(vmem_limit_bytes=VMEM_BYTES),
        cost_estimate=pl.CostEstimate(
            flops=7 * macs, transcendentals=share * steps_each * hid_width,
            bytes_accessed=24 << 20,
        ),
        name="train",
    )(
        ids, scores, g, high, low, noise_points, base, times.T, time_shift[None, :], weight_in,
        weight_out,
    )
    out_own, out_other = sum_over_devices(orders, keep, send)
    in_own, in_other = sum_over_devices(orders, keep_in, send_in)
    grad_out = place(ids, out_own, out_other, (hid_width, width))
    grad_in = place(ids, in_own, in_other, (width, hid_width))
    return predicted, grad_in, grad_out


def on_device(noise_points, data_points, times, time_shift, weight_in, weight_out):
    count_row = lax.axis_size("row")
    count_col = lax.axis_size("col")
    rows_here = noise_points.shape[0]
    total_noise = rows_here * count_row
    orders, ids = colour_ids()
    blocks = gather_points(data_points)
    grid = (count_col // 2, 2, count_row, data_points.shape[0] // count_row)
    scores, high, low, base, local = score(ids, noise_points, weight_in, blocks, grid)
    g = math.log2(float(total_noise)) - column_log_sum(local)
    return train(
        orders, ids, scores, g, high, low, noise_points, base, times, time_shift, weight_in,
        weight_out, total_noise,
    )


def solution(mesh):
    in_specs = (P("row", None), P("col", None), P(("row", "col"), None), P(), P(), P())
    out_specs = (P(("row", "col"), None), P(), P())

    return jax.shard_map(
        on_device, mesh=mesh, in_specs=in_specs, out_specs=out_specs, check_vma=False
    )
```

```python
import functools
import math

import jax
import jax.numpy as jnp
from jax import lax
from jax.experimental import pallas as pl
from jax.experimental.pallas import tpu as pltpu
from jax.sharding import PartitionSpec as P

ENTROPY = 0.05
CONTRACT_ROWS = (((0,), (0,)), ((), ()))
CONTRACT_LANES = (((1,), (1,)), ((), ()))
F32, BF16 = jnp.float32, jnp.bfloat16
STRIP = 8
VMEM_BYTES = 60 << 20
ANY = pl.BlockSpec(memory_space=pl.ANY)
VMEM = pl.BlockSpec(memory_space=pltpu.VMEM)
SMEM = pl.BlockSpec(memory_space=pltpu.SMEM)


def swap(value, axis, mask, scope="swap"):
    size = lax.axis_size(axis)
    with jax.named_scope(scope):
        return lax.ppermute(value, axis, [(i, i ^ mask) for i in range(size)])


def xor_rows(value, axis, mask):
    if mask == 0:
        return value
    pieces = [
        lax.index_in_dim(value, i ^ mask, axis, True) for i in range(value.shape[axis])
    ]
    return jnp.concatenate(pieces, axis=axis)


def log_sum(values):
    peak = values[0]
    for value in values[1:]:
        peak = jnp.maximum(peak, value)
    total = sum(jnp.exp2(value - peak) for value in values)
    return peak + jnp.log2(total)


def gather_points(data_points):
    count_row = lax.axis_size("row")
    count_z = lax.axis_size("col") // 2
    part = data_points.shape[0] // count_row
    row = lax.axis_index("row")
    pieces = [
        lax.dynamic_slice_in_dim(data_points, (row ^ k) * part, part, 0) for k in range(count_row)
    ]
    own = jnp.concatenate(pieces, axis=0)
    far = [swap(pieces[0], "col", 2 * m) for m in range(1, count_z)]
    blocks = [own, swap(own, "col", 1)]
    for value in far:
        mine = jnp.concatenate(
            [value] + [swap(value, "row", k) for k in range(1, count_row)], axis=0
        )
        blocks += [mine, swap(mine, "col", 1)]
    return blocks


def column_log_sum(local):
    count_z, count_core, count_row, part = local.shape
    parts = [local]
    for k in range(1, count_row):
        parts.append(xor_rows(swap(local, "row", k), 2, k))
    local = log_sum(parts)
    local = log_sum([local, xor_rows(swap(local, "col", 1), 1, 1)])
    parts = [local]
    for m in range(1, count_z):
        parts.append(xor_rows(swap(local, "col", 2 * m), 0, m))
    return log_sum(parts)


def split_halves(value):
    high = value.astype(BF16)
    low = (value - high.astype(F32)).astype(BF16)
    return high, low


def positions(shape):
    return [
        (z, core, slice(quarter, quarter + 1), slice(None))
        for z in range(shape[0])
        for core in range(shape[1])
        for quarter in range(shape[2])
    ]


def own_rows(noise_hbm, points, ids_ref):
    at = pl.multiple_of(ids_ref[2] * points, points)
    return noise_hbm.at[pl.ds(at, points)]


def score_kernel(count, log_data, norm, ids_ref, noise_hbm, win_hbm, *refs):
    block_hbm = refs[:count]
    scores_hbm, high_hbm, low_hbm, base_hbm, local_ref = refs[count : 5 + count]
    anchor_ref, blocks, scores, high, low, shift, win, base, sems, out_sems = refs[5 + count :]
    points = anchor_ref.shape[0]
    size = block_hbm[0].shape[0]
    copies = [
        pltpu.make_async_copy(own_rows(noise_hbm, points, ids_ref), anchor_ref, sems.at[count]),
        pltpu.make_async_copy(win_hbm, win, sems.at[count + 1]),
    ]
    for i in range(count):
        to = blocks.at[pl.ds(i * size, size)]
        copies.append(pltpu.make_async_copy(block_hbm[i], to, sems.at[i]))
    for copy in copies:
        copy.start()
    copies[0].wait()
    anchor = anchor_ref[...]
    anchor_sq = jnp.sum(anchor * anchor, axis=1, keepdims=True)
    a_high, a_low = split_halves(anchor)
    copies[1].wait()
    lanes = min(512, base.shape[1])
    for c in range(0, base.shape[1], lanes):
        part = slice(c, c + lanes)
        product = lambda a: jnp.dot(a, win[:, part], preferred_element_type=F32)
        base[:, part] = 0.5 * (product(a_high) + product(a_low))
    dots = lambda a, b: lax.dot_general(a, b, CONTRACT_LANES, preferred_element_type=F32)
    for i in range(0, count, 2):
        rows = slice(i * size, (i + 2) * size)
        copies[2 + i].wait()
        copies[3 + i].wait()
        block = blocks[rows, :]
        b_high, b_low = split_halves(block)
        high[rows, :] = b_high
        low[rows, :] = b_low
        block_sq = jnp.sum(block * block, axis=1, keepdims=True)
        block_sq = jnp.transpose(jnp.broadcast_to(block_sq, (2 * size, 128)))[:1]
        inner = dots(a_high, b_high) + dots(a_high, b_low) + dots(a_low, b_high)
        scores[:, rows] = (2.0 * inner - anchor_sq - block_sq) * norm
    outs = [
        pltpu.make_async_copy(scores, scores_hbm, out_sems.at[0]),
        pltpu.make_async_copy(high, high_hbm, out_sems.at[1]),
        pltpu.make_async_copy(low, low_hbm, out_sems.at[2]),
        pltpu.make_async_copy(base, base_hbm, out_sems.at[3]),
    ]
    for copy in outs:
        copy.start()
    width = scores.shape[1]

    def by_row(step, peak):
        at = pl.multiple_of(step * STRIP, STRIP)
        s = scores[pl.ds(at, STRIP), :]
        top = jnp.max(s, axis=1, keepdims=True)
        total = jnp.sum(jnp.exp2(s - top), axis=1, keepdims=True)
        f = log_data - top - jnp.log2(total)
        shift[pl.ds(at, STRIP), :] = jnp.broadcast_to(f, (STRIP, shift.shape[1]))
        return jnp.maximum(peak, s + f)

    peak = lax.fori_loop(
        0, points // STRIP, by_row, jnp.full((STRIP, width), -jnp.inf, F32), unroll=8
    )
    peak = jnp.max(peak, axis=0, keepdims=True)
    top = jnp.broadcast_to(peak, (STRIP, width))

    def by_column(step, total):
        at = pl.multiple_of(step * STRIP, STRIP)
        f = shift[pl.ds(at, STRIP), :][:, :1]
        return total + jnp.exp2((scores[pl.ds(at, STRIP), :] + f) - top)

    total = lax.fori_loop(
        0, points // STRIP, by_column, jnp.zeros((STRIP, width), F32), unroll=8
    )
    local = peak + jnp.log2(jnp.sum(total, axis=0, keepdims=True))
    part = local_ref.shape[-1]
    for i, at in enumerate(positions(local_ref.shape[:-1])):
        local_ref[at] = local[:, i * part : (i + 1) * part]
    for copy in outs:
        copy.wait()


def score(ids, noise_points, weight_in, blocks, grid):
    points, width = noise_points.shape[0] // lax.axis_size("col"), noise_points.shape[1]
    count = len(blocks)
    size = blocks[0].shape[0]
    total = count * size
    hid_width = weight_in.shape[1]
    norm = math.log2(math.e) / (width * ENTROPY)
    return pl.pallas_call(
        functools.partial(score_kernel, count, math.log2(float(total)), norm),
        out_shape=(
            jax.ShapeDtypeStruct((points, total), F32),
            jax.ShapeDtypeStruct((total, width), BF16),
            jax.ShapeDtypeStruct((total, width), BF16),
            jax.ShapeDtypeStruct((points, hid_width), F32),
            jax.ShapeDtypeStruct(grid, F32),
        ),
        in_specs=[SMEM] + [ANY] * (2 + count),
        out_specs=[ANY, ANY, ANY, ANY, VMEM],
        scratch_shapes=[
            pltpu.VMEM((points, width), F32), pltpu.VMEM((total, width), F32),
            pltpu.VMEM((points, total), F32), pltpu.VMEM((total, width), BF16),
            pltpu.VMEM((total, width), BF16), pltpu.VMEM((points, 128), F32),
            pltpu.VMEM((width, hid_width), BF16), pltpu.VMEM((points, hid_width), F32),
            pltpu.SemaphoreType.DMA((2 + count,)), pltpu.SemaphoreType.DMA((4,)),
        ],
        compiler_params=pltpu.CompilerParams(vmem_limit_bytes=VMEM_BYTES),
        cost_estimate=pl.CostEstimate(
            flops=6 * points * total * width + 4 * points * width * hid_width,
            transcendentals=2 * points * total, bytes_accessed=16 << 20,
        ),
        name="score",
    )(ids, noise_points, weight_in, *blocks)


def colour_ids():
    count_row = lax.axis_size("row")
    count_z = lax.axis_size("col") // 2
    row, col = lax.axis_index("row"), lax.axis_index("col")
    bits = list(range(count_row.bit_length() - 1))
    orders = [bits, bits[::-1]]
    ids = []
    for order in orders:
        ident = col & 1
        for bit in order:
            ident = ident * 2 + ((row >> bit) & 1)
        ids.append(ident * count_z + (col >> 1))
    return orders, jnp.stack(ids + [col]).astype(jnp.int32)


def store_blocks(devices, factor, ids_ref, total_ref, keep_ref, send_ref):
    unit = total_ref.shape[0] // devices
    lanes = total_ref.shape[1] // 2
    for colour in range(2):
        for pos in range(devices):
            source = pl.multiple_of((ids_ref[colour] ^ pos) * unit, unit)
            block = total_ref[pl.ds(source, unit), colour * lanes : (colour + 1) * lanes]
            out_ref = keep_ref if pos < devices // 2 else send_ref
            at = (pos % (devices // 2)) * unit
            out_ref[colour, at : at + unit, :] = block * factor


def time_column(times, k):
    lane = lax.broadcasted_iota(jnp.int32, times.shape, 1)
    return jnp.sum(jnp.where(lane == k, times, 0.0), axis=1, keepdims=True)


def train_kernel(
    devices, scale, ids_ref, scores_hbm, g_ref, high_hbm, low_hbm, noise_hbm, base_hbm, times_hbm,
    shift_ref, win_hbm, wout_hbm, pred_hbm, keep_out, send_out, keep_in, send_in,
    scores, high, low, anchor, base, win, wout, weights, weight_sum, target, velocity, move,
    plain, timed, hidden, slope, delta, back, spread, staged, total_out, total_in, times_row, g_row,
    times_ref, sems, out_sems,
):
    points, width = anchor.shape
    steps_each = times_row.shape[0]
    hid_width = base.shape[1]
    half = hid_width // 2
    strip, lanes = 16, 512
    moves = [
        (scores_hbm, scores), (high_hbm, high), (low_hbm, low),
        (own_rows(noise_hbm, points, ids_ref), anchor), (win_hbm, win), (base_hbm, base),
        (wout_hbm, wout), (times_hbm, times_row),
    ]
    copies = [pltpu.make_async_copy(a, b, sems.at[i]) for i, (a, b) in enumerate(moves)]
    for copy in copies:
        copy.start()

    for ref in (total_out, plain, timed, back[1], slope[1]):
        ref[...] = jnp.zeros_like(ref)
    part = g_ref.shape[-1]
    for i, at in enumerate(positions(g_ref.shape[:-1])):
        g_row[:, i * part : (i + 1) * part] = g_ref[at]
    g = g_row[...]
    copies[0].wait()

    def weigh(step, unused):
        at = pl.multiple_of(step * strip, strip)
        s = scores[pl.ds(at, strip), :] + g
        w = jnp.exp2(s - jnp.max(s, axis=1, keepdims=True)).astype(BF16)
        weights[pl.ds(at, strip), :] = w
        total = jnp.sum(w.astype(F32), axis=1, keepdims=True)
        weight_sum[pl.ds(at, strip), :] = jnp.broadcast_to(total, (strip, weight_sum.shape[1]))
        return unused

    lax.fori_loop(0, points // strip, weigh, 0, unroll=4)
    for copy in copies[1:5]:
        copy.wait()
    numer = jnp.dot(weights[...], high[...], preferred_element_type=F32)
    numer = numer + jnp.dot(weights[...], low[...], preferred_element_type=F32)
    target[...] = numer / weight_sum[:, :1]
    diff = target[...] - anchor[...]
    velocity[...] = diff
    d_high, d_low = split_halves(diff)
    for c in range(0, hid_width, lanes):
        part = slice(c, c + lanes)
        dots = lambda a: jnp.dot(a, win[:, part], preferred_element_type=F32)
        move[:, part] = 0.5 * (dots(d_high) + dots(d_low) + shift_ref[:, part])
    for copy in copies[5:]:
        copy.wait()
    times_ref[...] = jnp.transpose(times_row[...])

    strips = [
        (slice(r, r + strip), slice(c, c + lanes))
        for r in range(0, points, strip)
        for c in range(0, hid_width, lanes)
    ]

    def activate(at, t, slot):
        h = base[at] + t[at[0]] * move[at]
        u = 1.0 + jnp.tanh(h)
        act = h * u
        hidden[slot][at] = act.astype(BF16)
        slope[slot][at] = u + act * (2.0 - u)

    def collect(at, t, slot):
        grad = back[slot][at] * slope[slot][at]
        plain[at] += grad
        timed[at] += t[at[0]] * grad

    def learn(k, slot):
        other = 1 - slot
        times = times_ref[...]
        before = time_column(times, k - 1)
        after = time_column(times, jnp.minimum(k + 1, steps_each - 1))
        to_do = list(strips)

        def vector_work(count):
            for at in to_do[:count]:
                collect(at, before, other)
                activate(at, after, other)
            del to_do[:count]

        out = jnp.dot(hidden[slot][...], wout[...], preferred_element_type=F32)
        vector_work(len(strips) // 2)
        delta[slot][...] = (out - velocity[...]).astype(BF16)
        for c in range(spread.shape[0]):
            spread[c, pl.ds(k, points, stride=steps_each), :] = out[:, c * 128 : (c + 1) * 128]
        back[slot][...] = lax.dot_general(
            delta[slot][...], wout[...], CONTRACT_LANES, preferred_element_type=F32
        )
        vector_work(len(strips))
        total_out[...] += lax.dot_general(
            hidden[slot][...], delta[slot][...], CONTRACT_ROWS, preferred_element_type=F32
        )

    start = time_column(times_ref[...], 0)
    for at in strips:
        activate(at, start, 0)

    def two_steps(i, unused):
        learn(2 * i, 0)
        learn(2 * i + 1, 1)
        return unused

    lax.fori_loop(0, steps_each // 2, two_steps, 0)
    last = time_column(times_ref[...], steps_each - 1)
    for at in strips:
        collect(at, last, 1)
    rows = points * steps_each // len(staged)
    leaves = []
    for i, ref in enumerate(staged):
        for c in range(spread.shape[0]):
            lanes_of = slice(c * 128, (c + 1) * 128)
            ref[:, lanes_of] = spread[c, i * rows : (i + 1) * rows, :].astype(BF16)
        leaves.append(
            pltpu.make_async_copy(ref, pred_hbm.at[pl.ds(i * rows, rows)], out_sems.at[i])
        )
        leaves[-1].start()
    diff = velocity[...].astype(BF16)
    rounded = anchor[...].astype(BF16)
    for h in range(2):
        part = slice(h * half, (h + 1) * half)
        total_in[h * width : (h + 1) * width, :] = (
            lax.dot_general(
                rounded, plain[:, part].astype(BF16), CONTRACT_ROWS, preferred_element_type=F32
            )
            + lax.dot_general(
                diff, timed[:, part].astype(BF16), CONTRACT_ROWS, preferred_element_type=F32
            )
        )
    store_blocks(devices, scale, ids_ref, total_out, keep_out, send_out)
    store_blocks(devices, 0.5 * scale, ids_ref, total_in, keep_in, send_in)
    for copy in leaves:
        copy.wait()


def place_kernel(devices, wide, ids_ref, own_ref, other_ref, out_ref):
    unit = own_ref.shape[1] * 2 // devices
    lanes = own_ref.shape[2]
    for colour in range(2):
        for block in range(devices):
            pos = ids_ref[colour] ^ block
            far = pos >= devices // 2
            at = pl.multiple_of((pos & (devices // 2 - 1)) * unit, unit)
            value = jnp.where(
                far, other_ref[colour, pl.ds(at, unit), :], own_ref[colour, pl.ds(at, unit), :]
            )
            row = block * unit
            if wide:
                height = out_ref.shape[0]
                left = (row // height) * 2 * lanes + colour * lanes
                row = row % height
            else:
                left = colour * lanes
            out_ref[row : row + unit, left : left + lanes] = value


def place(ids, own, other, shape):
    devices = lax.axis_size("row") * lax.axis_size("col")
    wide = shape[1] > 2 * own.shape[2]
    return pl.pallas_call(
        functools.partial(place_kernel, devices, wide),
        out_shape=jax.ShapeDtypeStruct(shape, jnp.float32),
        grid_spec=pltpu.PrefetchScalarGridSpec(
            num_scalar_prefetch=1, grid=(1,),
            in_specs=[
                pl.BlockSpec(own.shape, lambda i, ids: (0, 0, 0)),
                pl.BlockSpec(own.shape, lambda i, ids: (0, 0, 0)),
            ],
            out_specs=pl.BlockSpec(shape, lambda i, ids: (0, 0)),
        ),
        compiler_params=pltpu.CompilerParams(vmem_limit_bytes=24 << 20),
        cost_estimate=pl.CostEstimate(flops=0, transcendentals=0, bytes_accessed=4 << 20),
        name="place",
    )(ids, own, other)


def sum_over_devices(name, orders, keep, send):
    count_z = lax.axis_size("col") // 2
    got = swap(send, "col", 1, f"{name}_core")
    colours = [(keep[c], got[c]) for c in range(2)]
    for step in range(len(orders[0])):
        later = []
        for c, ((mine, other), order) in enumerate(zip(colours, orders)):
            half = mine.shape[0] // 2
            out = mine[half:] + other[half:]
            out = swap(out, "row", 1 << order[step], f"{name}_halve_{step}_{c}")
            later.append((mine[:half] + other[:half], out))
        colours = later
    unit = colours[0][0].shape[0] // count_z
    parts = {
        m: [a[m * unit : (m + 1) * unit] + b[m * unit : (m + 1) * unit] for a, b in colours]
        for m in range(count_z)
    }
    bits = range(count_z.bit_length() - 1)
    for bit in bits:
        far = [m for m in parts if m >> bit & 1]
        sent = jnp.concatenate([piece for m in far for piece in parts[m]], axis=0)
        got = swap(sent, "col", 2 << bit, f"{name}_layer_{bit}")
        parts = {
            m ^ (1 << bit): [
                near + got[(2 * i + c) * unit : (2 * i + c + 1) * unit]
                for c, near in enumerate(parts[m ^ (1 << bit)])
            ]
            for i, m in enumerate(far)
        }
    for bit in reversed(bits):
        known = list(parts)
        sent = jnp.concatenate([piece for m in known for piece in parts[m]], axis=0)
        got = swap(sent, "col", 2 << bit, f"{name}_spread_{bit}")
        for i, m in enumerate(known):
            parts[m ^ (1 << bit)] = [
                got[(2 * i + c) * unit : (2 * i + c + 1) * unit] for c in range(2)
            ]
    colours = [
        jnp.concatenate([parts[m][c] for m in range(count_z)], axis=0) for c in range(2)
    ]
    for step in reversed(range(len(orders[0]))):
        colours = [
            jnp.concatenate(
                [value, swap(value, "row", 1 << order[step], f"{name}_double_{step}_{c}")], axis=0
            )
            for c, (value, order) in enumerate(zip(colours, orders))
        ]
    own = jnp.stack(colours)
    return own, swap(own, "col", 1, f"{name}_back")


def train(
    orders, ids, scores, g, high, low, noise_points, base, times, time_shift, weight_in,
    weight_out, total_noise,
):
    share, width = scores.shape[0], high.shape[1]
    steps_each = times.shape[1]
    hid_width = weight_in.shape[1]
    total = scores.shape[1]
    devices = lax.axis_size("row") * lax.axis_size("col")
    scale = 1.0 / math.sqrt(float(total_noise * steps_each))
    of_out = jax.ShapeDtypeStruct((2, hid_width // 2, width // 2), F32)
    of_in = jax.ShapeDtypeStruct((2, width, hid_width // 4), F32)
    macs = share * steps_each * width * hid_width
    vmem = pltpu.VMEM
    wide, narrow = (share, hid_width), (share, width)
    predicted, keep, send, keep_in, send_in = pl.pallas_call(
        functools.partial(train_kernel, devices, scale),
        out_shape=(
            jax.ShapeDtypeStruct((share * steps_each, width), BF16),
            of_out, of_out, of_in, of_in,
        ),
        in_specs=[
            SMEM, ANY, VMEM, ANY, ANY, ANY, ANY, ANY, VMEM, ANY, ANY,
        ],
        out_specs=[ANY, VMEM, VMEM, VMEM, VMEM],
        scratch_shapes=[
            vmem((share, total), F32), vmem((total, width), BF16), vmem((total, width), BF16),
            vmem(narrow, F32), vmem(wide, F32), vmem((width, hid_width), BF16),
            vmem((hid_width, width), BF16), vmem((share, total), BF16), vmem((share, 128), F32),
            vmem(narrow, F32), vmem(narrow, F32), vmem(wide, F32), vmem(wide, F32),
            vmem(wide, F32), (vmem(wide, BF16),) * 2, (vmem(wide, F32),) * 2,
            (vmem(narrow, BF16),) * 2, (vmem(wide, F32),) * 2,
            vmem((width // 128, share * steps_each, 128), F32),
            (vmem((share * steps_each // 4, width), BF16),) * 4,
            vmem((hid_width, width), F32), vmem((2 * width, hid_width // 2), F32),
            vmem((steps_each, share), F32), vmem((1, total), F32), vmem((share, steps_each), F32),
            pltpu.SemaphoreType.DMA((8,)), pltpu.SemaphoreType.DMA((4,)),
        ],
        compiler_params=pltpu.CompilerParams(vmem_limit_bytes=VMEM_BYTES),
        cost_estimate=pl.CostEstimate(
            flops=7 * macs, transcendentals=share * steps_each * hid_width,
            bytes_accessed=24 << 20,
        ),
        name="train",
    )(
        ids, scores, g, high, low, noise_points, base, times.T, time_shift[None, :], weight_in,
        weight_out,
    )
    out_own, out_other = sum_over_devices("out", orders, keep, send)
    in_own, in_other = sum_over_devices("in", orders, keep_in, send_in)
    grad_out = place(ids, out_own, out_other, (hid_width, width))
    grad_in = place(ids, in_own, in_other, (width, hid_width))
    return predicted, grad_in, grad_out


def on_device(noise_points, data_points, times, time_shift, weight_in, weight_out):
    count_row = lax.axis_size("row")
    count_col = lax.axis_size("col")
    rows_here = noise_points.shape[0]
    total_noise = rows_here * count_row
    orders, ids = colour_ids()
    blocks = gather_points(data_points)
    grid = (count_col // 2, 2, count_row, data_points.shape[0] // count_row)
    scores, high, low, base, local = score(ids, noise_points, weight_in, blocks, grid)
    g = math.log2(float(total_noise)) - column_log_sum(local)
    return train(
        orders, ids, scores, g, high, low, noise_points, base, times, time_shift, weight_in,
        weight_out, total_noise,
    )


def solution(mesh):
    in_specs = (P("row", None), P("col", None), P(("row", "col"), None), P(), P(), P())
    out_specs = (P(("row", "col"), None), P(), P())
    return jax.shard_map(
        on_device, mesh=mesh, in_specs=in_specs, out_specs=out_specs, check_vma=False
    )
```

```python
import functools
import math

import jax
import jax.numpy as jnp
from jax import lax
from jax.experimental import pallas as pl
from jax.experimental.pallas import tpu as pltpu
from jax.sharding import PartitionSpec as P

ENTROPY = 0.05
CONTRACT_ROWS = (((0,), (0,)), ((), ()))
CONTRACT_LANES = (((1,), (1,)), ((), ()))
F32, BF16 = jnp.float32, jnp.bfloat16
STRIP = 8
VMEM_BYTES = 60 << 20
ANY = pl.BlockSpec(memory_space=pl.ANY)
VMEM = pl.BlockSpec(memory_space=pltpu.VMEM)
SMEM = pl.BlockSpec(memory_space=pltpu.SMEM)


def swap(value, axis, mask, scope="swap"):
    size = lax.axis_size(axis)
    with jax.named_scope(scope):
        return lax.ppermute(value, axis, [(i, i ^ mask) for i in range(size)])


def xor_rows(value, axis, mask):
    if mask == 0:
        return value
    pieces = [
        lax.index_in_dim(value, i ^ mask, axis, True) for i in range(value.shape[axis])
    ]
    return jnp.concatenate(pieces, axis=axis)


def log_sum(values):
    peak = values[0]
    for value in values[1:]:
        peak = jnp.maximum(peak, value)
    total = sum(jnp.exp2(value - peak) for value in values)
    return peak + jnp.log2(total)


def gather_points(data_points):
    count_row = lax.axis_size("row")
    count_z = lax.axis_size("col") // 2
    part = data_points.shape[0] // count_row
    row = lax.axis_index("row")
    pieces = [
        lax.dynamic_slice_in_dim(data_points, (row ^ k) * part, part, 0) for k in range(count_row)
    ]
    own = jnp.concatenate(pieces, axis=0)
    far = [swap(pieces[0], "col", 2 * m) for m in range(1, count_z)]
    blocks = [own, swap(own, "col", 1)]
    for value in far:
        mine = jnp.concatenate(
            [value] + [swap(value, "row", k) for k in range(1, count_row)], axis=0
        )
        blocks += [mine, swap(mine, "col", 1)]
    return blocks


def column_log_sum(local):
    count_z, count_core, count_row, part = local.shape
    parts = [local]
    for k in range(1, count_row):
        parts.append(xor_rows(swap(local, "row", k), 2, k))
    local = log_sum(parts)
    local = log_sum([local, xor_rows(swap(local, "col", 1), 1, 1)])
    parts = [local]
    for m in range(1, count_z):
        parts.append(xor_rows(swap(local, "col", 2 * m), 0, m))
    return log_sum(parts)


def split_halves(value):
    high = value.astype(BF16)
    low = (value - high.astype(F32)).astype(BF16)
    return high, low


def positions(shape):
    return [
        (z, core, slice(quarter, quarter + 1), slice(None))
        for z in range(shape[0])
        for core in range(shape[1])
        for quarter in range(shape[2])
    ]


def own_rows(noise_hbm, points, ids_ref):
    at = pl.multiple_of(ids_ref[2] * points, points)
    return noise_hbm.at[pl.ds(at, points)]


def score_kernel(count, log_data, norm, ids_ref, noise_hbm, win_hbm, *refs):
    block_hbm = refs[:count]
    scores_hbm, high_hbm, low_hbm, base_hbm, local_ref = refs[count : 5 + count]
    anchor_ref, blocks, scores, high, low, shift, win, base, sems, out_sems = refs[5 + count :]
    points = anchor_ref.shape[0]
    size = block_hbm[0].shape[0]
    copies = [
        pltpu.make_async_copy(own_rows(noise_hbm, points, ids_ref), anchor_ref, sems.at[count]),
        pltpu.make_async_copy(win_hbm, win, sems.at[count + 1]),
    ]
    for i in range(count):
        to = blocks.at[pl.ds(i * size, size)]
        copies.append(pltpu.make_async_copy(block_hbm[i], to, sems.at[i]))
    for copy in copies:
        copy.start()
    copies[0].wait()
    anchor = anchor_ref[...]
    anchor_sq = jnp.sum(anchor * anchor, axis=1, keepdims=True)
    a_high, a_low = split_halves(anchor)
    copies[1].wait()
    lanes = min(512, base.shape[1])
    for c in range(0, base.shape[1], lanes):
        part = slice(c, c + lanes)
        product = lambda a: jnp.dot(a, win[:, part], preferred_element_type=F32)
        base[:, part] = 0.5 * (product(a_high) + product(a_low))
    dots = lambda a, b: lax.dot_general(a, b, CONTRACT_LANES, preferred_element_type=F32)
    for i in range(0, count, 2):
        rows = slice(i * size, (i + 2) * size)
        copies[2 + i].wait()
        copies[3 + i].wait()
        block = blocks[rows, :]
        b_high, b_low = split_halves(block)
        high[rows, :] = b_high
        low[rows, :] = b_low
        block_sq = jnp.sum(block * block, axis=1, keepdims=True)
        block_sq = jnp.transpose(jnp.broadcast_to(block_sq, (2 * size, 128)))[:1]
        inner = dots(a_high, b_high) + dots(a_high, b_low) + dots(a_low, b_high)
        scores[:, rows] = (2.0 * inner - anchor_sq - block_sq) * norm
    outs = [
        pltpu.make_async_copy(scores, scores_hbm, out_sems.at[0]),
        pltpu.make_async_copy(high, high_hbm, out_sems.at[1]),
        pltpu.make_async_copy(low, low_hbm, out_sems.at[2]),
        pltpu.make_async_copy(base, base_hbm, out_sems.at[3]),
    ]
    for copy in outs:
        copy.start()
    width = scores.shape[1]

    def by_row(step, peak):
        at = pl.multiple_of(step * STRIP, STRIP)
        s = scores[pl.ds(at, STRIP), :]
        top = jnp.max(s, axis=1, keepdims=True)
        total = jnp.sum(jnp.exp2(s - top), axis=1, keepdims=True)
        f = log_data - top - jnp.log2(total)
        shift[pl.ds(at, STRIP), :] = jnp.broadcast_to(f, (STRIP, shift.shape[1]))
        return jnp.maximum(peak, s + f)

    peak = lax.fori_loop(
        0, points // STRIP, by_row, jnp.full((STRIP, width), -jnp.inf, F32), unroll=8
    )
    peak = jnp.max(peak, axis=0, keepdims=True)
    top = jnp.broadcast_to(peak, (STRIP, width))

    def by_column(step, total):
        at = pl.multiple_of(step * STRIP, STRIP)
        f = shift[pl.ds(at, STRIP), :][:, :1]
        return total + jnp.exp2((scores[pl.ds(at, STRIP), :] + f) - top)

    total = lax.fori_loop(
        0, points // STRIP, by_column, jnp.zeros((STRIP, width), F32), unroll=8
    )
    local = peak + jnp.log2(jnp.sum(total, axis=0, keepdims=True))
    part = local_ref.shape[-1]
    for i, at in enumerate(positions(local_ref.shape[:-1])):
        local_ref[at] = local[:, i * part : (i + 1) * part]
    for copy in outs:
        copy.wait()


def score(ids, noise_points, weight_in, blocks, grid):
    points, width = noise_points.shape[0] // lax.axis_size("col"), noise_points.shape[1]
    count = len(blocks)
    size = blocks[0].shape[0]
    total = count * size
    hid_width = weight_in.shape[1]
    norm = math.log2(math.e) / (width * ENTROPY)
    return pl.pallas_call(
        functools.partial(score_kernel, count, math.log2(float(total)), norm),
        out_shape=(
            jax.ShapeDtypeStruct((points, total), F32),
            jax.ShapeDtypeStruct((total, width), BF16),
            jax.ShapeDtypeStruct((total, width), BF16),
            jax.ShapeDtypeStruct((points, hid_width), F32),
            jax.ShapeDtypeStruct(grid, F32),
        ),
        in_specs=[SMEM] + [ANY] * (2 + count),
        out_specs=[ANY, ANY, ANY, ANY, VMEM],
        scratch_shapes=[
            pltpu.VMEM((points, width), F32), pltpu.VMEM((total, width), F32),
            pltpu.VMEM((points, total), F32), pltpu.VMEM((total, width), BF16),
            pltpu.VMEM((total, width), BF16), pltpu.VMEM((points, 128), F32),
            pltpu.VMEM((width, hid_width), BF16), pltpu.VMEM((points, hid_width), F32),
            pltpu.SemaphoreType.DMA((2 + count,)), pltpu.SemaphoreType.DMA((4,)),
        ],
        compiler_params=pltpu.CompilerParams(vmem_limit_bytes=VMEM_BYTES),
        cost_estimate=pl.CostEstimate(
            flops=6 * points * total * width + 4 * points * width * hid_width,
            transcendentals=2 * points * total, bytes_accessed=16 << 20,
        ),
        name="score",
    )(ids, noise_points, weight_in, *blocks)


def colour_ids():
    count_row = lax.axis_size("row")
    count_z = lax.axis_size("col") // 2
    row, col = lax.axis_index("row"), lax.axis_index("col")
    bits = list(range(count_row.bit_length() - 1))
    orders = [bits, bits[::-1]]
    ids = []
    for order in orders:
        ident = col & 1
        for bit in order:
            ident = ident * 2 + ((row >> bit) & 1)
        ids.append(ident * count_z + (col >> 1))
    return orders, jnp.stack(ids + [col]).astype(jnp.int32)


def store_blocks(devices, factor, ids_ref, total_ref, keep_ref, send_ref):
    unit = total_ref.shape[0] // devices
    lanes = total_ref.shape[1] // 2
    for colour in range(2):
        for pos in range(devices):
            source = pl.multiple_of((ids_ref[colour] ^ pos) * unit, unit)
            block = total_ref[pl.ds(source, unit), colour * lanes : (colour + 1) * lanes]
            out_ref = keep_ref if pos < devices // 2 else send_ref
            at = (pos % (devices // 2)) * unit
            out_ref[colour, at : at + unit, :] = block * factor


def time_column(times, k):
    lane = lax.broadcasted_iota(jnp.int32, times.shape, 1)
    return jnp.sum(jnp.where(lane == k, times, 0.0), axis=1, keepdims=True)


def train_kernel(
    devices, scale, ids_ref, scores_hbm, g_ref, high_hbm, low_hbm, noise_hbm, base_hbm, times_hbm,
    shift_ref, win_hbm, wout_hbm, pred_hbm, keep_out_hbm, send_out_hbm, keep_in_hbm, send_in_hbm,
    scores, high, low, anchor, base, win, wout, weights, weight_sum, target, velocity, move,
    plain, timed, hidden, slope, delta, back, spread, staged, total_out, total_in, times_row, g_row,
    times_ref, keep_out, send_out, keep_in, send_in, sems, out_sems,
):
    points, width = anchor.shape
    steps_each = times_row.shape[0]
    hid_width = base.shape[1]
    half = hid_width // 2
    strip, lanes = 16, 512
    moves = [
        (scores_hbm, scores), (high_hbm, high), (low_hbm, low),
        (own_rows(noise_hbm, points, ids_ref), anchor), (win_hbm, win), (base_hbm, base),
        (wout_hbm, wout), (times_hbm, times_row),
    ]
    copies = [pltpu.make_async_copy(a, b, sems.at[i]) for i, (a, b) in enumerate(moves)]
    for copy in copies:
        copy.start()

    for ref in (total_out, plain, timed, back[1], slope[1]):
        ref[...] = jnp.zeros_like(ref)
    part = g_ref.shape[-1]
    for i, at in enumerate(positions(g_ref.shape[:-1])):
        g_row[:, i * part : (i + 1) * part] = g_ref[at]
    g = g_row[...]
    copies[0].wait()

    def weigh(step, unused):
        at = pl.multiple_of(step * strip, strip)
        s = scores[pl.ds(at, strip), :] + g
        w = jnp.exp2(s - jnp.max(s, axis=1, keepdims=True)).astype(BF16)
        weights[pl.ds(at, strip), :] = w
        total = jnp.sum(w.astype(F32), axis=1, keepdims=True)
        weight_sum[pl.ds(at, strip), :] = jnp.broadcast_to(total, (strip, weight_sum.shape[1]))
        return unused

    lax.fori_loop(0, points // strip, weigh, 0, unroll=4)
    for copy in copies[1:5]:
        copy.wait()
    numer = jnp.dot(weights[...], high[...], preferred_element_type=F32)
    numer = numer + jnp.dot(weights[...], low[...], preferred_element_type=F32)
    target[...] = numer / weight_sum[:, :1]
    diff = target[...] - anchor[...]
    velocity[...] = diff
    d_high, d_low = split_halves(diff)
    for c in range(0, hid_width, lanes):
        part = slice(c, c + lanes)
        dots = lambda a: jnp.dot(a, win[:, part], preferred_element_type=F32)
        move[:, part] = 0.5 * (dots(d_high) + dots(d_low) + shift_ref[:, part])
    for copy in copies[5:]:
        copy.wait()
    times_ref[...] = jnp.transpose(times_row[...])

    strips = [
        (slice(r, r + strip), slice(c, c + lanes))
        for r in range(0, points, strip)
        for c in range(0, hid_width, lanes)
    ]

    def activate(at, t, slot):
        h = base[at] + t[at[0]] * move[at]
        u = 1.0 + jnp.tanh(h)
        act = h * u
        hidden[slot][at] = act.astype(BF16)
        slope[slot][at] = u + act * (2.0 - u)

    def collect(at, t, slot):
        grad = back[slot][at] * slope[slot][at]
        plain[at] += grad
        timed[at] += t[at[0]] * grad

    def learn(k, slot):
        other = 1 - slot
        times = times_ref[...]
        before = time_column(times, k - 1)
        after = time_column(times, jnp.minimum(k + 1, steps_each - 1))
        to_do = list(strips)

        def vector_work(count):
            for at in to_do[:count]:
                collect(at, before, other)
                activate(at, after, other)
            del to_do[:count]

        out = jnp.dot(hidden[slot][...], wout[...], preferred_element_type=F32)
        vector_work(len(strips) // 2)
        delta[slot][...] = (out - velocity[...]).astype(BF16)
        for c in range(spread.shape[0]):
            spread[c, pl.ds(k, points, stride=steps_each), :] = out[:, c * 128 : (c + 1) * 128]
        back[slot][...] = lax.dot_general(
            delta[slot][...], wout[...], CONTRACT_LANES, preferred_element_type=F32
        )
        vector_work(len(strips))
        total_out[...] += lax.dot_general(
            hidden[slot][...], delta[slot][...], CONTRACT_ROWS, preferred_element_type=F32
        )

    start = time_column(times_ref[...], 0)
    for at in strips:
        activate(at, start, 0)

    def two_steps(i, unused):
        learn(2 * i, 0)
        learn(2 * i + 1, 1)
        return unused

    lax.fori_loop(0, steps_each // 2, two_steps, 0)
    last = time_column(times_ref[...], steps_each - 1)
    for at in strips:
        collect(at, last, 1)
    rows = points * steps_each // len(staged)
    leaves = []
    for i, ref in enumerate(staged):
        for c in range(spread.shape[0]):
            lanes_of = slice(c * 128, (c + 1) * 128)
            ref[:, lanes_of] = spread[c, i * rows : (i + 1) * rows, :].astype(BF16)
        leaves.append(
            pltpu.make_async_copy(ref, pred_hbm.at[pl.ds(i * rows, rows)], out_sems.at[i])
        )
        leaves[-1].start()
    def hand_over(pairs):
        for ref, to in pairs:
            leaves.append(pltpu.make_async_copy(ref, to, out_sems.at[len(leaves)]))
            leaves[-1].start()

    store_blocks(devices, scale, ids_ref, total_out, keep_out, send_out)
    hand_over([(send_out, send_out_hbm), (keep_out, keep_out_hbm)])
    diff = velocity[...].astype(BF16)
    rounded = anchor[...].astype(BF16)
    for h in range(2):
        part = slice(h * half, (h + 1) * half)
        total_in[h * width : (h + 1) * width, :] = (
            lax.dot_general(
                rounded, plain[:, part].astype(BF16), CONTRACT_ROWS, preferred_element_type=F32
            )
            + lax.dot_general(
                diff, timed[:, part].astype(BF16), CONTRACT_ROWS, preferred_element_type=F32
            )
        )
    store_blocks(devices, 0.5 * scale, ids_ref, total_in, keep_in, send_in)
    hand_over([(send_in, send_in_hbm), (keep_in, keep_in_hbm)])
    for copy in leaves:
        copy.wait()


def place_kernel(devices, ids_ref, half_ref, *refs):
    out_ref = refs[-1]
    unit = half_ref.shape[1] * 2 // devices
    lanes = half_ref.shape[2]
    for colour in range(2):
        for block in range(devices // 2):
            at = (ids_ref[colour] ^ block) & (devices // 2 - 1)
            at = pl.multiple_of(at * unit, unit)
            out_ref[
                block * unit : (block + 1) * unit, colour * lanes : (colour + 1) * lanes
            ] = half_ref[colour, pl.ds(at, unit), :]


def place_half(ids, half, far, shape, rest=None):
    devices = lax.axis_size("row") * lax.axis_size("col")
    top = devices.bit_length() - 2
    wide = shape[1] > 2 * half.shape[2]
    side = lambda ids: (ids[0] >> top) ^ far
    if wide:
        out = pl.BlockSpec((shape[0], shape[1] // 2), lambda i, ids: (0, side(ids)))
    else:
        out = pl.BlockSpec((shape[0] // 2, shape[1]), lambda i, ids: (side(ids), 0))
    operands = (half,) if rest is None else (half, rest)
    return pl.pallas_call(
        functools.partial(place_kernel, devices),
        out_shape=jax.ShapeDtypeStruct(shape, F32),
        grid_spec=pltpu.PrefetchScalarGridSpec(
            num_scalar_prefetch=1, grid=(1,),
            in_specs=[pl.BlockSpec(half.shape, lambda i, ids: (0, 0, 0))]
            + [ANY] * (len(operands) - 1),
            out_specs=out,
        ),
        input_output_aliases={} if rest is None else {2: 0},
        compiler_params=pltpu.CompilerParams(vmem_limit_bytes=24 << 20),
        cost_estimate=pl.CostEstimate(flops=0, transcendentals=0, bytes_accessed=2 << 20),
        name="place",
    )(ids, *operands)


def place(ids, own, other, shape):
    return place_half(ids, other, 1, shape, place_half(ids, own, 0, shape))


def sum_over_devices(name, orders, keep, send):
    count_z = lax.axis_size("col") // 2
    got = swap(send, "col", 1, f"{name}_core")
    colours = [(keep[c], got[c]) for c in range(2)]
    for step in range(len(orders[0])):
        later = []
        for c, ((mine, other), order) in enumerate(zip(colours, orders)):
            half = mine.shape[0] // 2
            out = mine[half:] + other[half:]
            out = swap(out, "row", 1 << order[step], f"{name}_halve_{step}_{c}")
            later.append((mine[:half] + other[:half], out))
        colours = later
    unit = colours[0][0].shape[0] // count_z
    part = lambda m: jnp.stack(
        [a[m * unit : (m + 1) * unit] + b[m * unit : (m + 1) * unit] for a, b in colours]
    )
    got = [swap(part(m), "col", 2 * m, f"{name}_layer_{m}") for m in range(1, count_z)]
    total = part(0)
    for value in got:
        total = total + value
    parts = [total]
    parts += [swap(total, "col", 2 * m, f"{name}_spread_{m}") for m in range(1, count_z)]
    colours = [jnp.concatenate([p[c] for p in parts], axis=0) for c in range(2)]
    for step in reversed(range(len(orders[0]))):
        colours = [
            jnp.concatenate(
                [value, swap(value, "row", 1 << order[step], f"{name}_double_{step}_{c}")], axis=0
            )
            for c, (value, order) in enumerate(zip(colours, orders))
        ]
    own = jnp.stack(colours)
    return own, swap(own, "col", 1, f"{name}_back")


def train(
    orders, ids, scores, g, high, low, noise_points, base, times, time_shift, weight_in,
    weight_out, total_noise,
):
    share, width = scores.shape[0], high.shape[1]
    steps_each = times.shape[1]
    hid_width = weight_in.shape[1]
    total = scores.shape[1]
    devices = lax.axis_size("row") * lax.axis_size("col")
    scale = 1.0 / math.sqrt(float(total_noise * steps_each))
    of_out = jax.ShapeDtypeStruct((2, hid_width // 2, width // 2), F32)
    of_in = jax.ShapeDtypeStruct((2, width, hid_width // 4), F32)
    macs = share * steps_each * width * hid_width
    vmem = pltpu.VMEM
    wide, narrow = (share, hid_width), (share, width)
    predicted, keep, send, keep_in, send_in = pl.pallas_call(
        functools.partial(train_kernel, devices, scale),
        out_shape=(
            jax.ShapeDtypeStruct((share * steps_each, width), BF16),
            of_out, of_out, of_in, of_in,
        ),
        in_specs=[
            SMEM, ANY, VMEM, ANY, ANY, ANY, ANY, ANY, VMEM, ANY, ANY,
        ],
        out_specs=[ANY] * 5,
        scratch_shapes=[
            vmem((share, total), F32), vmem((total, width), BF16), vmem((total, width), BF16),
            vmem(narrow, F32), vmem(wide, F32), vmem((width, hid_width), BF16),
            vmem((hid_width, width), BF16), vmem((share, total), BF16), vmem((share, 128), F32),
            vmem(narrow, F32), vmem(narrow, F32), vmem(wide, F32), vmem(wide, F32),
            vmem(wide, F32), (vmem(wide, BF16),) * 2, (vmem(wide, F32),) * 2,
            (vmem(narrow, BF16),) * 2, (vmem(wide, F32),) * 2,
            vmem((width // 128, share * steps_each, 128), F32),
            (vmem((share * steps_each // 4, width), BF16),) * 4,
            vmem((hid_width, width), F32), vmem((2 * width, hid_width // 2), F32),
            vmem((steps_each, share), F32), vmem((1, total), F32), vmem((share, steps_each), F32),
            vmem(of_out.shape, F32), vmem(of_out.shape, F32), vmem(of_in.shape, F32),
            vmem(of_in.shape, F32),
            pltpu.SemaphoreType.DMA((8,)), pltpu.SemaphoreType.DMA((8,)),
        ],
        compiler_params=pltpu.CompilerParams(vmem_limit_bytes=VMEM_BYTES),
        cost_estimate=pl.CostEstimate(
            flops=7 * macs, transcendentals=share * steps_each * hid_width,
            bytes_accessed=24 << 20,
        ),
        name="train",
    )(
        ids, scores, g, high, low, noise_points, base, times.T, time_shift[None, :], weight_in,
        weight_out,
    )
    out_own, out_other = sum_over_devices("out", orders, keep, send)
    in_own, in_other = sum_over_devices("in", orders, keep_in, send_in)
    grad_out = place(ids, out_own, out_other, (hid_width, width))
    grad_in = place(ids, in_own, in_other, (width, hid_width))
    return predicted, grad_in, grad_out


def on_device(noise_points, data_points, times, time_shift, weight_in, weight_out):
    count_row = lax.axis_size("row")
    count_col = lax.axis_size("col")
    rows_here = noise_points.shape[0]
    total_noise = rows_here * count_row
    orders, ids = colour_ids()
    blocks = gather_points(data_points)
    grid = (count_col // 2, 2, count_row, data_points.shape[0] // count_row)
    scores, high, low, base, local = score(ids, noise_points, weight_in, blocks, grid)
    g = math.log2(float(total_noise)) - column_log_sum(local)
    return train(
        orders, ids, scores, g, high, low, noise_points, base, times, time_shift, weight_in,
        weight_out, total_noise,
    )


def solution(mesh):
    in_specs = (P("row", None), P("col", None), P(("row", "col"), None), P(), P(), P())
    out_specs = (P(("row", "col"), None), P(), P())
    return jax.shard_map(
        on_device, mesh=mesh, in_specs=in_specs, out_specs=out_specs, check_vma=False
    )
```

```python
import functools
import math

import jax
import jax.numpy as jnp
from jax import lax
from jax.experimental import pallas as pl
from jax.experimental.pallas import tpu as pltpu
from jax.sharding import PartitionSpec as P

ENTROPY = 0.05
CONTRACT_ROWS = (((0,), (0,)), ((), ()))
CONTRACT_LANES = (((1,), (1,)), ((), ()))
F32, BF16 = jnp.float32, jnp.bfloat16
STRIP = 8
VMEM_BYTES = 60 << 20
ANY = pl.BlockSpec(memory_space=pl.ANY)
VMEM = pl.BlockSpec(memory_space=pltpu.VMEM)
SMEM = pl.BlockSpec(memory_space=pltpu.SMEM)


def swap(value, axis, mask, scope="swap"):
    size = lax.axis_size(axis)
    with jax.named_scope(scope):
        return lax.ppermute(value, axis, [(i, i ^ mask) for i in range(size)])


def xor_rows(value, axis, mask):
    if mask == 0:
        return value
    pieces = [
        lax.index_in_dim(value, i ^ mask, axis, True) for i in range(value.shape[axis])
    ]
    return jnp.concatenate(pieces, axis=axis)


def log_sum(values):
    peak = values[0]
    for value in values[1:]:
        peak = jnp.maximum(peak, value)
    total = sum(jnp.exp2(value - peak) for value in values)
    return peak + jnp.log2(total)


def gather_points(data_points, ready):
    count_row = lax.axis_size("row")
    count_z = lax.axis_size("col") // 2
    part = data_points.shape[0] // count_row
    row = lax.axis_index("row")
    pieces = [
        lax.dynamic_slice_in_dim(data_points, (row ^ k) * part, part, 0) for k in range(count_row)
    ]
    own = jnp.concatenate(pieces, axis=0)
    far = [swap(pieces[0], "col", 2 * m) for m in range(1, count_z)]
    blocks = [own, swap(own, "col", 1)]
    for m, value in enumerate(far):
        mine = jnp.concatenate(
            [value] + [swap(value, "row", k) for k in range(1, count_row)], axis=0
        )
        if m == len(far) // 2:
            mine, ready = lax.optimization_barrier((mine, ready))
        blocks += [mine, swap(mine, "col", 1)]
    return blocks, ready


def column_log_sum(local):
    count_z, count_core, count_row, part = local.shape
    parts = [local]
    for k in range(1, count_row):
        parts.append(xor_rows(swap(local, "row", k), 2, k))
    local = log_sum(parts)
    local = log_sum([local, xor_rows(swap(local, "col", 1), 1, 1)])
    parts = [local]
    for m in range(1, count_z):
        parts.append(xor_rows(swap(local, "col", 2 * m), 0, m))
    return log_sum(parts)


def split_halves(value):
    high = value.astype(BF16)
    low = (value - high.astype(F32)).astype(BF16)
    return high, low


def positions(shape):
    return [
        (z, core, slice(quarter, quarter + 1), slice(None))
        for z in range(shape[0])
        for core in range(shape[1])
        for quarter in range(shape[2])
    ]


def own_rows(noise_hbm, points, ids_ref):
    at = pl.multiple_of(ids_ref[2] * points, points)
    return noise_hbm.at[pl.ds(at, points)]


def score_kernel(count, log_data, norm, ids_ref, noise_hbm, *refs):
    block_hbm = refs[:count]
    scores_hbm, high_hbm, low_hbm, local_ref = refs[count : 4 + count]
    anchor_ref, blocks, scores, high, low, shift, sems, out_sems = refs[4 + count :]
    points = anchor_ref.shape[0]
    size = block_hbm[0].shape[0]
    copies = [
        pltpu.make_async_copy(own_rows(noise_hbm, points, ids_ref), anchor_ref, sems.at[count])
    ]
    for i in range(count):
        to = blocks.at[pl.ds(i * size, size)]
        copies.append(pltpu.make_async_copy(block_hbm[i], to, sems.at[i]))
    for copy in copies:
        copy.start()
    copies[0].wait()
    anchor = anchor_ref[...]
    anchor_sq = jnp.sum(anchor * anchor, axis=1, keepdims=True)
    a_high, a_low = split_halves(anchor)
    dots = lambda a, b: lax.dot_general(a, b, CONTRACT_LANES, preferred_element_type=F32)
    for i in range(0, count, 2):
        rows = slice(i * size, (i + 2) * size)
        copies[1 + i].wait()
        copies[2 + i].wait()
        block = blocks[rows, :]
        b_high, b_low = split_halves(block)
        high[rows, :] = b_high
        low[rows, :] = b_low
        block_sq = jnp.sum(block * block, axis=1, keepdims=True)
        block_sq = jnp.transpose(jnp.broadcast_to(block_sq, (2 * size, 128)))[:1]
        inner = dots(a_high, b_high) + dots(a_high, b_low) + dots(a_low, b_high)
        scores[:, rows] = (2.0 * inner - anchor_sq - block_sq) * norm
    outs = [
        pltpu.make_async_copy(scores, scores_hbm, out_sems.at[0]),
        pltpu.make_async_copy(high, high_hbm, out_sems.at[1]),
        pltpu.make_async_copy(low, low_hbm, out_sems.at[2]),
    ]
    for copy in outs:
        copy.start()
    width = scores.shape[1]

    def by_row(step, peak):
        at = pl.multiple_of(step * STRIP, STRIP)
        s = scores[pl.ds(at, STRIP), :]
        top = jnp.max(s, axis=1, keepdims=True)
        total = jnp.sum(jnp.exp2(s - top), axis=1, keepdims=True)
        f = log_data - top - jnp.log2(total)
        shift[pl.ds(at, STRIP), :] = jnp.broadcast_to(f, (STRIP, shift.shape[1]))
        return jnp.maximum(peak, s + f)

    peak = lax.fori_loop(
        0, points // STRIP, by_row, jnp.full((STRIP, width), -jnp.inf, F32), unroll=8
    )
    peak = jnp.max(peak, axis=0, keepdims=True)
    top = jnp.broadcast_to(peak, (STRIP, width))

    def by_column(step, total):
        at = pl.multiple_of(step * STRIP, STRIP)
        f = shift[pl.ds(at, STRIP), :][:, :1]
        return total + jnp.exp2((scores[pl.ds(at, STRIP), :] + f) - top)

    total = lax.fori_loop(
        0, points // STRIP, by_column, jnp.zeros((STRIP, width), F32), unroll=8
    )
    local = peak + jnp.log2(jnp.sum(total, axis=0, keepdims=True))
    part = local_ref.shape[-1]
    for i, at in enumerate(positions(local_ref.shape[:-1])):
        local_ref[at] = local[:, i * part : (i + 1) * part]
    for copy in outs:
        copy.wait()


def score(ids, noise_points, blocks, grid):
    points, width = noise_points.shape[0] // lax.axis_size("col"), noise_points.shape[1]
    count = len(blocks)
    size = blocks[0].shape[0]
    total = count * size
    norm = math.log2(math.e) / (width * ENTROPY)
    return pl.pallas_call(
        functools.partial(score_kernel, count, math.log2(float(total)), norm),
        out_shape=(
            jax.ShapeDtypeStruct((points, total), F32),
            jax.ShapeDtypeStruct((total, width), BF16),
            jax.ShapeDtypeStruct((total, width), BF16),
            jax.ShapeDtypeStruct(grid, F32),
        ),
        in_specs=[SMEM] + [ANY] * (1 + count),
        out_specs=[ANY, ANY, ANY, VMEM],
        scratch_shapes=[
            pltpu.VMEM((points, width), F32), pltpu.VMEM((total, width), F32),
            pltpu.VMEM((points, total), F32), pltpu.VMEM((total, width), BF16),
            pltpu.VMEM((total, width), BF16), pltpu.VMEM((points, 128), F32),
            pltpu.SemaphoreType.DMA((1 + count,)), pltpu.SemaphoreType.DMA((3,)),
        ],
        compiler_params=pltpu.CompilerParams(vmem_limit_bytes=VMEM_BYTES),
        cost_estimate=pl.CostEstimate(
            flops=6 * points * total * width, transcendentals=2 * points * total,
            bytes_accessed=13 << 20,
        ),
        name="score",
    )(ids, noise_points, *blocks)


def base_kernel(ids_ref, anchor_ref, win_ref, base_ref):
    high, low = split_halves(anchor_ref[...])
    dots = lambda a: jnp.dot(a, win_ref[...], preferred_element_type=F32)
    base_ref[...] = 0.5 * (dots(high) + dots(low))


def anchor_product(ids, noise_points, weight_in):
    points, width = noise_points.shape[0] // lax.axis_size("col"), noise_points.shape[1]
    hid_width = weight_in.shape[1]
    lanes = hid_width // 2
    return pl.pallas_call(
        base_kernel,
        out_shape=jax.ShapeDtypeStruct((points, hid_width), F32),
        grid_spec=pltpu.PrefetchScalarGridSpec(
            num_scalar_prefetch=1, grid=(2,),
            in_specs=[
                pl.BlockSpec((points, width), lambda i, ids: (ids[2], 0)),
                pl.BlockSpec((width, lanes), lambda i, ids: (0, i)),
            ],
            out_specs=pl.BlockSpec((points, lanes), lambda i, ids: (0, i)),
        ),
        compiler_params=pltpu.CompilerParams(vmem_limit_bytes=VMEM_BYTES),
        cost_estimate=pl.CostEstimate(
            flops=4 * points * width * hid_width, transcendentals=0, bytes_accessed=4 << 20
        ),
        name="base",
    )(ids, noise_points, weight_in)


def colour_ids():
    count_row = lax.axis_size("row")
    count_z = lax.axis_size("col") // 2
    row, col = lax.axis_index("row"), lax.axis_index("col")
    bits = list(range(count_row.bit_length() - 1))
    orders = [bits, bits[::-1]]
    ids = []
    for order in orders:
        ident = col & 1
        for bit in order:
            ident = ident * 2 + ((row >> bit) & 1)
        ids.append(ident * count_z + (col >> 1))
    return orders, jnp.stack(ids + [col]).astype(jnp.int32)


def store_blocks(devices, factor, ids_ref, total_ref, keep_ref, send_ref):
    unit = total_ref.shape[0] // devices
    lanes = total_ref.shape[1] // 2
    for colour in range(2):
        for pos in range(devices):
            source = pl.multiple_of((ids_ref[colour] ^ pos) * unit, unit)
            block = total_ref[pl.ds(source, unit), colour * lanes : (colour + 1) * lanes]
            out_ref = keep_ref if pos < devices // 2 else send_ref
            at = (pos % (devices // 2)) * unit
            out_ref[colour, at : at + unit, :] = block * factor


def time_column(times, k):
    lane = lax.broadcasted_iota(jnp.int32, times.shape, 1)
    return jnp.sum(jnp.where(lane == k, times, 0.0), axis=1, keepdims=True)


def train_kernel(
    devices, scale, ids_ref, scores_hbm, g_ref, high_hbm, low_hbm, noise_hbm, base_hbm, times_hbm,
    shift_ref, win_hbm, wout_hbm, pred_hbm, keep_out_hbm, send_out_hbm, keep_in_hbm, send_in_hbm,
    scores, high, low, anchor, base, win, wout, weights, weight_sum, target, velocity, move,
    plain, timed, hidden, slope, delta, back, spread, staged, total_out, total_in, times_row, g_row,
    times_ref, keep_out, send_out, keep_in, send_in, sems, out_sems,
):
    points, width = anchor.shape
    steps_each = times_row.shape[0]
    hid_width = base.shape[1]
    half = hid_width // 2
    strip, lanes = 16, 512
    moves = [
        (scores_hbm, scores), (high_hbm, high), (low_hbm, low),
        (own_rows(noise_hbm, points, ids_ref), anchor), (win_hbm, win), (base_hbm, base),
        (wout_hbm, wout), (times_hbm, times_row),
    ]
    copies = [pltpu.make_async_copy(a, b, sems.at[i]) for i, (a, b) in enumerate(moves)]
    for copy in copies:
        copy.start()

    for ref in (total_out, plain, timed, back[1], slope[1]):
        ref[...] = jnp.zeros_like(ref)
    part = g_ref.shape[-1]
    for i, at in enumerate(positions(g_ref.shape[:-1])):
        g_row[:, i * part : (i + 1) * part] = g_ref[at]
    g = g_row[...]
    copies[0].wait()

    def weigh(step, unused):
        at = pl.multiple_of(step * strip, strip)
        s = scores[pl.ds(at, strip), :] + g
        w = jnp.exp2(s - jnp.max(s, axis=1, keepdims=True)).astype(BF16)
        weights[pl.ds(at, strip), :] = w
        total = jnp.sum(w.astype(F32), axis=1, keepdims=True)
        weight_sum[pl.ds(at, strip), :] = jnp.broadcast_to(total, (strip, weight_sum.shape[1]))
        return unused

    lax.fori_loop(0, points // strip, weigh, 0, unroll=4)
    for copy in copies[1:5]:
        copy.wait()
    numer = jnp.dot(weights[...], high[...], preferred_element_type=F32)
    numer = numer + jnp.dot(weights[...], low[...], preferred_element_type=F32)
    target[...] = numer / weight_sum[:, :1]
    diff = target[...] - anchor[...]
    velocity[...] = diff
    d_high, d_low = split_halves(diff)
    for c in range(0, hid_width, lanes):
        part = slice(c, c + lanes)
        dots = lambda a: jnp.dot(a, win[:, part], preferred_element_type=F32)
        move[:, part] = 0.5 * (dots(d_high) + dots(d_low) + shift_ref[:, part])
    for copy in copies[5:]:
        copy.wait()
    times_ref[...] = jnp.transpose(times_row[...])

    strips = [
        (slice(r, r + strip), slice(c, c + lanes))
        for r in range(0, points, strip)
        for c in range(0, hid_width, lanes)
    ]

    def activate(at, t, slot):
        h = base[at] + t[at[0]] * move[at]
        u = 1.0 + jnp.tanh(h)
        act = h * u
        hidden[slot][at] = act.astype(BF16)
        slope[slot][at] = u + act * (2.0 - u)

    def collect(at, t, slot):
        grad = back[slot][at] * slope[slot][at]
        plain[at] += grad
        timed[at] += t[at[0]] * grad

    def learn(k, slot):
        other = 1 - slot
        times = times_ref[...]
        before = time_column(times, k - 1)
        after = time_column(times, jnp.minimum(k + 1, steps_each - 1))
        to_do = list(strips)

        def vector_work(count):
            for at in to_do[:count]:
                collect(at, before, other)
                activate(at, after, other)
            del to_do[:count]

        out = jnp.dot(hidden[slot][...], wout[...], preferred_element_type=F32)
        vector_work(len(strips) // 2)
        delta[slot][...] = (out - velocity[...]).astype(BF16)
        for c in range(spread.shape[0]):
            spread[c, pl.ds(k, points, stride=steps_each), :] = out[:, c * 128 : (c + 1) * 128]
        back[slot][...] = lax.dot_general(
            delta[slot][...], wout[...], CONTRACT_LANES, preferred_element_type=F32
        )
        vector_work(len(strips))
        total_out[...] += lax.dot_general(
            hidden[slot][...], delta[slot][...], CONTRACT_ROWS, preferred_element_type=F32
        )

    start = time_column(times_ref[...], 0)
    for at in strips:
        activate(at, start, 0)

    def two_steps(i, unused):
        learn(2 * i, 0)
        learn(2 * i + 1, 1)
        return unused

    lax.fori_loop(0, steps_each // 2, two_steps, 0)
    last = time_column(times_ref[...], steps_each - 1)
    for at in strips:
        collect(at, last, 1)
    rows = points * steps_each // len(staged)
    leaves = []
    for i, ref in enumerate(staged):
        for c in range(spread.shape[0]):
            lanes_of = slice(c * 128, (c + 1) * 128)
            ref[:, lanes_of] = spread[c, i * rows : (i + 1) * rows, :].astype(BF16)
        leaves.append(
            pltpu.make_async_copy(ref, pred_hbm.at[pl.ds(i * rows, rows)], out_sems.at[i])
        )
        leaves[-1].start()
    def hand_over(pairs):
        for ref, to in pairs:
            leaves.append(pltpu.make_async_copy(ref, to, out_sems.at[len(leaves)]))
            leaves[-1].start()

    store_blocks(devices, scale, ids_ref, total_out, keep_out, send_out)
    hand_over([(send_out, send_out_hbm), (keep_out, keep_out_hbm)])
    diff = velocity[...].astype(BF16)
    rounded = anchor[...].astype(BF16)
    for h in range(2):
        part = slice(h * half, (h + 1) * half)
        total_in[h * width : (h + 1) * width, :] = (
            lax.dot_general(
                rounded, plain[:, part].astype(BF16), CONTRACT_ROWS, preferred_element_type=F32
            )
            + lax.dot_general(
                diff, timed[:, part].astype(BF16), CONTRACT_ROWS, preferred_element_type=F32
            )
        )
    store_blocks(devices, 0.5 * scale, ids_ref, total_in, keep_in, send_in)
    hand_over([(send_in, send_in_hbm), (keep_in, keep_in_hbm)])
    for copy in leaves:
        copy.wait()


def place_kernel(devices, wide, ids_ref, own_ref, other_ref, out_ref):
    unit = own_ref.shape[1] * 2 // devices
    lanes = own_ref.shape[2]
    for colour in range(2):
        for block in range(devices):
            pos = ids_ref[colour] ^ block
            far = pos >= devices // 2
            at = pl.multiple_of((pos & (devices // 2 - 1)) * unit, unit)
            value = jnp.where(
                far, other_ref[colour, pl.ds(at, unit), :], own_ref[colour, pl.ds(at, unit), :]
            )
            row = block * unit
            if wide:
                height = out_ref.shape[0]
                left = (row // height) * 2 * lanes + colour * lanes
                row = row % height
            else:
                left = colour * lanes
            out_ref[row : row + unit, left : left + lanes] = value


def place(ids, own, other, shape):
    devices = lax.axis_size("row") * lax.axis_size("col")
    wide = shape[1] > 2 * own.shape[2]
    return pl.pallas_call(
        functools.partial(place_kernel, devices, wide),
        out_shape=jax.ShapeDtypeStruct(shape, jnp.float32),
        grid_spec=pltpu.PrefetchScalarGridSpec(
            num_scalar_prefetch=1, grid=(1,),
            in_specs=[
                pl.BlockSpec(own.shape, lambda i, ids: (0, 0, 0)),
                pl.BlockSpec(own.shape, lambda i, ids: (0, 0, 0)),
            ],
            out_specs=pl.BlockSpec(shape, lambda i, ids: (0, 0)),
        ),
        compiler_params=pltpu.CompilerParams(vmem_limit_bytes=24 << 20),
        cost_estimate=pl.CostEstimate(flops=0, transcendentals=0, bytes_accessed=4 << 20),
        name="place",
    )(ids, own, other)


def sum_over_devices(name, orders, keep, send):
    count_z = lax.axis_size("col") // 2
    got = swap(send, "col", 1, f"{name}_core")
    colours = [(keep[c], got[c]) for c in range(2)]
    for step in range(len(orders[0])):
        later = []
        for c, ((mine, other), order) in enumerate(zip(colours, orders)):
            half = mine.shape[0] // 2
            out = mine[half:] + other[half:]
            out = swap(out, "row", 1 << order[step], f"{name}_halve_{step}_{c}")
            later.append((mine[:half] + other[:half], out))
        colours = later
    unit = colours[0][0].shape[0] // count_z
    part = lambda m: jnp.stack(
        [a[m * unit : (m + 1) * unit] + b[m * unit : (m + 1) * unit] for a, b in colours]
    )
    got = [swap(part(m), "col", 2 * m, f"{name}_layer_{m}") for m in range(1, count_z)]
    total = part(0)
    for value in got:
        total = total + value
    parts = [total]
    parts += [swap(total, "col", 2 * m, f"{name}_spread_{m}") for m in range(1, count_z)]
    colours = [jnp.concatenate([p[c] for p in parts], axis=0) for c in range(2)]
    for step in reversed(range(len(orders[0]))):
        colours = [
            jnp.concatenate(
                [value, swap(value, "row", 1 << order[step], f"{name}_double_{step}_{c}")], axis=0
            )
            for c, (value, order) in enumerate(zip(colours, orders))
        ]
    own = jnp.stack(colours)
    return own, swap(own, "col", 1, f"{name}_back")


def train(
    orders, ids, scores, g, high, low, noise_points, base, times, time_shift, weight_in,
    weight_out, total_noise,
):
    share, width = scores.shape[0], high.shape[1]
    steps_each = times.shape[1]
    hid_width = weight_in.shape[1]
    total = scores.shape[1]
    devices = lax.axis_size("row") * lax.axis_size("col")
    scale = 1.0 / math.sqrt(float(total_noise * steps_each))
    of_out = jax.ShapeDtypeStruct((2, hid_width // 2, width // 2), F32)
    of_in = jax.ShapeDtypeStruct((2, width, hid_width // 4), F32)
    macs = share * steps_each * width * hid_width
    vmem = pltpu.VMEM
    wide, narrow = (share, hid_width), (share, width)
    predicted, keep, send, keep_in, send_in = pl.pallas_call(
        functools.partial(train_kernel, devices, scale),
        out_shape=(
            jax.ShapeDtypeStruct((share * steps_each, width), BF16),
            of_out, of_out, of_in, of_in,
        ),
        in_specs=[
            SMEM, ANY, VMEM, ANY, ANY, ANY, ANY, ANY, VMEM, ANY, ANY,
        ],
        out_specs=[ANY] * 5,
        scratch_shapes=[
            vmem((share, total), F32), vmem((total, width), BF16), vmem((total, width), BF16),
            vmem(narrow, F32), vmem(wide, F32), vmem((width, hid_width), BF16),
            vmem((hid_width, width), BF16), vmem((share, total), BF16), vmem((share, 128), F32),
            vmem(narrow, F32), vmem(narrow, F32), vmem(wide, F32), vmem(wide, F32),
            vmem(wide, F32), (vmem(wide, BF16),) * 2, (vmem(wide, F32),) * 2,
            (vmem(narrow, BF16),) * 2, (vmem(wide, F32),) * 2,
            vmem((width // 128, share * steps_each, 128), F32),
            (vmem((share * steps_each // 4, width), BF16),) * 4,
            vmem((hid_width, width), F32), vmem((2 * width, hid_width // 2), F32),
            vmem((steps_each, share), F32), vmem((1, total), F32), vmem((share, steps_each), F32),
            vmem(of_out.shape, F32), vmem(of_out.shape, F32), vmem(of_in.shape, F32),
            vmem(of_in.shape, F32),
            pltpu.SemaphoreType.DMA((8,)), pltpu.SemaphoreType.DMA((8,)),
        ],
        compiler_params=pltpu.CompilerParams(vmem_limit_bytes=VMEM_BYTES),
        cost_estimate=pl.CostEstimate(
            flops=7 * macs, transcendentals=share * steps_each * hid_width,
            bytes_accessed=24 << 20,
        ),
        name="train",
    )(
        ids, scores, g, high, low, noise_points, base, times.T, time_shift[None, :], weight_in,
        weight_out,
    )
    out_own, out_other = sum_over_devices("out", orders, keep, send)
    in_own, in_other = sum_over_devices("in", orders, keep_in, send_in)
    grad_out = place(ids, out_own, out_other, (hid_width, width))
    grad_in = place(ids, in_own, in_other, (width, hid_width))
    return predicted, grad_in, grad_out


def on_device(noise_points, data_points, times, time_shift, weight_in, weight_out):
    count_row = lax.axis_size("row")
    count_col = lax.axis_size("col")
    rows_here = noise_points.shape[0]
    total_noise = rows_here * count_row
    orders, ids = colour_ids()
    base = anchor_product(ids, noise_points, weight_in)
    blocks, (base, ids) = gather_points(data_points, (base, ids))
    grid = (count_col // 2, 2, count_row, data_points.shape[0] // count_row)
    scores, high, low, local = score(ids, noise_points, blocks, grid)
    g = math.log2(float(total_noise)) - column_log_sum(local)
    return train(
        orders, ids, scores, g, high, low, noise_points, base, times, time_shift, weight_in,
        weight_out, total_noise,
    )


def solution(mesh):
    in_specs = (P("row", None), P("col", None), P(("row", "col"), None), P(), P(), P())
    out_specs = (P(("row", "col"), None), P(), P())
    return jax.shard_map(
        on_device, mesh=mesh, in_specs=in_specs, out_specs=out_specs, check_vma=False
    )
```
